512 devices in a mesh: event: 8 (over y, core), tile: 64 (over x, z).
Axes of the slice: x: 4, y: 4, z: 16, core: 2. Of those that a mesh axis runs over, the one named last changes fastest.
Arguments:
- surface_start: float32 [8, 512, 8192], P('event', 'tile'), may hold values from -6 to 6
- east_start: float32 [8, 512, 8192], P('event', 'tile'), may hold values from -5 to 5
- north_start: float32 [8, 512, 8192], P('event', 'tile'), may hold values from -5 to 5
- still_depth: float32 [512, 8192], P('tile'), may hold values from 1 to 4
- roughness: float32 [512, 8192], P('tile'), may hold values from 0.5 to 2
- wet_masks: int32 [8, 2, 512, 8192], P('event', None, 'tile'), may hold values 0 or 1
- gauge_tiles: int32 [8, 16384, 1], P('event', 'tile'), may hold values from 0 to 63; in each aligned block of 256 rows (0 to 255, 256 to 511, ..., all dimensions but the last counted through in order) at most 8 rows name the same one
- gauge_cells: int32 [8, 16384], P('event', 'tile'), may hold values from 0 to 65535
- gauge_values: float32 [8, 16384], P('event', 'tile'), may hold values from -6 to 6
- survey_surface: float32 [8, 512, 8192], P('event', 'tile'), may hold values from -6 to 6
Outputs:
- roughness_grad: float32 [512, 8192], P('tile', 'event')
The draws below stay inside these ranges and needn't reach their ends.
Inputs may be any that keep to these rules, and one draw needn't show every extreme that they name: `gauge_tiles`: of the gauges of one event listed on one strip, at most 8 lie in any one strip, and some strip receives exactly 8.
All inputs are finite; a program needn't handle non-finite values. No bound on the sum of `wet_masks` on one device may be relied on, other than what follows from the above.
Results may differ from the reference program's by a relative error of at most 0.0003.
Values sent between devices are 32-bit elements; how exact they have to be, the bound alone decides.
No kernel may reach another device: no remote copies, remote signals or barrier semaphores. Data moves between devices by JAX's collectives and lax.ppermute only.
A program may use at most 64 MiB of HBM per device.

```python
import math
import jax
import jax.numpy as jnp
import numpy as np

ROWS_DEV = 8
COLS = 8192
G_DEV = 256
STEPS = 2
EVENTS = 8
NX = 512
GAUGES = 16384
CAP = 8
N_TILE = 64


def touch_ends(array, stream_key, least, high):
    longest = array.shape.index(max(array.shape))
    spots = []
    for shift in (0, 1):
        where = [jax.random.randint(jax.random.fold_in(stream_key, axis), (), 0, length) for axis, length in enumerate(array.shape)]
        where[longest] = (where[longest] + shift) % array.shape[longest]
        spots.append(tuple(where))
    return array.at[spots[0]].set(least).at[spots[1]].set(high)


def steps_of(own_key, dims, split, least, largest):
    level = 1.0
    for axis_at, blocks in split:
        heights = jax.random.uniform(jax.random.fold_in(jax.random.fold_in(own_key, 6), axis_at), (blocks,), jnp.float32, least / len(split), largest / len(split))
        level = level * jnp.repeat(jnp.exp(heights), dims[axis_at] // blocks).reshape((-1,) + (1,) * (len(dims) - 1 - axis_at))
    return level


def shared_out(rng, own, number, rows, count, top, most, slope):
    order = jax.random.permutation(rng, count)
    heavy_load, common = shares(count, rows * top, most, slope, True), shares(count, rows * top, most, slope, False)
    places = jnp.arange(count)

    def named(sizes, offset_by):
        used = int((sizes > 0).sum())
        fixed = max(1, used // 4)
        moved = fixed + (places - fixed + offset_by * (used - fixed)) % max(1, count - fixed)
        return jnp.zeros((count,), jnp.int32).at[order[jnp.where(places < fixed, places, moved)]].set(jnp.asarray(sizes, jnp.int32))

    sizes = jnp.where(number % 4 == 0, named(heavy_load, number // 4), named(common, number - number // 4 - 1))
    mixed = jax.random.permutation(jax.random.fold_in(own, 3), count)
    source_of, sink = mixed[0:count // 2 * 2:2], mixed[1:count // 2 * 2:2]
    room = jnp.minimum(sizes[source_of] - 1, most - sizes[sink]) // 2
    room = jnp.where((source_of == order[0]) | (sink == order[0]) | (sizes[sink] == 0), 0, jnp.maximum(room, 0))
    moved = jax.random.randint(jax.random.fold_in(own, 4), (count // 2,), 0, 1 << 20) % (room + 1)
    sizes = sizes.at[source_of].add(-moved).at[sink].add(moved)
    items = jnp.searchsorted(jnp.cumsum(sizes), jnp.arange(rows * top), side="right").astype(jnp.int32)
    table = items.reshape(top, rows).T
    table = table[jax.random.permutation(jax.random.fold_in(own, 1), rows)]
    offset_by = jax.random.randint(jax.random.fold_in(own, 2), (rows, 1), 0, top)
    return jnp.take_along_axis(table, (jnp.arange(top)[None, :] + offset_by) % top, axis=1)


def shares(amount, total, bound, skew, full):
    portions = [(1 << 20) // math.isqrt(grade ** skew) + 1 for grade in range(1, amount + 1)]
    largest = bound if full else min(bound, max(-(-total // amount), total * portions[0] // sum(portions)))
    least = 1 if total - largest >= amount - 1 else 0
    counts, spare = [largest] + [least] * (amount - 1), total - largest - least * (amount - 1)
    while spare > 0:
        movable = [i for i in range(1, amount) if counts[i] < largest] or [i for i in range(1, amount) if counts[i] < bound]
        mass, remaining = sum([portions[i] for i in movable]), spare
        for i in movable:
            more = min(bound - counts[i], max(1, remaining * portions[i] // mass), spare)
            counts[i] = counts[i] + more
            spare = spare - more
    return np.array(counts)


def normal_values(rng, shape, scale, bound, split=(), kind=jnp.bfloat16):
    values = scale * jax.random.normal(rng, shape, jnp.float32)
    if split:
        values = values * steps_of(rng, shape, split, -0.22, 0.18)
    return jnp.clip(values, -bound, bound).astype(kind)


def setup_inputs(seed: int = 0) -> dict:
    arg_keys = jax.random.split(jax.random.key(seed), 11)
    surface_start = normal_values(arg_keys[0], (EVENTS, NX, COLS), 1.0, 6.0, ((0, 8), (1, 64)), jnp.float32)
    east_start = normal_values(arg_keys[1], (EVENTS, NX, COLS), 0.7, 5.0, ((0, 8), (1, 64)), jnp.float32)
    north_start = normal_values(arg_keys[2], (EVENTS, NX, COLS), 0.7, 5.0, ((0, 8), (1, 64)), jnp.float32)
    still_depth = jnp.clip(jnp.exp(math.log(4.0) - 1.3862944 * jax.random.uniform(arg_keys[3], (NX, COLS), jnp.float32) ** steps_of(arg_keys[3], (NX, COLS), ((0, 64),), -0.2, 0.2)), 1.0, 4.0)
    roughness = jnp.clip(jnp.exp(math.log(2.0) - 1.3862944 * jax.random.uniform(arg_keys[4], (NX, COLS), jnp.float32) ** steps_of(arg_keys[4], (NX, COLS), ((0, 64),), -0.2, 0.2)), 0.5, 2.0)
    wet_masks = touch_ends((jax.random.randint(arg_keys[5], (EVENTS, STEPS, NX, COLS), 0, 8) < 7).astype(jnp.int32), jax.random.fold_in(arg_keys[5], 1), 0, 1)
    gauge_tiles_keys = jax.random.split(jax.random.fold_in(arg_keys[6], 1), EVENTS * GAUGES // G_DEV)
    gauge_tiles_turns = jax.random.permutation(jax.random.fold_in(arg_keys[6], 3), EVENTS * GAUGES // G_DEV)
    gauge_tiles = jax.vmap(lambda own, number: shared_out(jax.random.fold_in(arg_keys[6], 2), own, number, G_DEV, N_TILE, 1, CAP, 2))(gauge_tiles_keys, gauge_tiles_turns).reshape((EVENTS, GAUGES, 1))
    gauge_cells = touch_ends(jax.random.randint(arg_keys[7], (EVENTS, GAUGES), 0, ROWS_DEV * COLS), jax.random.fold_in(arg_keys[7], 1), 0, (ROWS_DEV * COLS) - 1).astype(jnp.int32)
    gauge_values = normal_values(arg_keys[8], (EVENTS, GAUGES), 1.0, 6.0, ((0, 8), (1, 64)), jnp.float32)
    survey_surface = normal_values(arg_keys[9], (EVENTS, NX, COLS), 1.0, 6.0, ((0, 8), (1, 64)), jnp.float32)
    return dict(surface_start=surface_start, east_start=east_start, north_start=north_start, still_depth=still_depth, roughness=roughness, wet_masks=wet_masks, gauge_tiles=gauge_tiles, gauge_cells=gauge_cells, gauge_values=gauge_values, survey_surface=survey_surface)


def interior(field):
    return field[1:-1]

def across(field):
    padded = jnp.pad(field, ((0, 0), (1, 1)))
    return padded[:, 2:] - padded[:, :-2]

def along(field):
    return field[2:] - field[:-2]

def advance(surface, east, north, depth_rows, rough_rows, wetness):
    depth_inner = interior(depth_rows)
    depth_safe = jnp.where(depth_inner > 0, depth_inner, 1.0)
    east_inner = interior(east)
    north_inner = interior(north)
    speed = jnp.sqrt(east_inner * east_inner + north_inner * north_inner + 1.0)
    rough_inner = interior(rough_rows)
    friction = 1.0 + 2.0 * rough_inner * rough_inner * speed / depth_safe ** (4.0 / 3.0)
    wet_inner = interior(wetness)
    new_east = wet_inner * (east_inner - 0.2 * depth_inner * across(interior(surface))) / friction
    new_north = wet_inner * (north_inner - 0.2 * depth_inner * along(surface)) / friction
    new_surface = interior(interior(surface)) - 0.25 * interior(wet_inner) * (interior(across(new_east)) + along(new_north))
    return (new_surface, interior(new_east), interior(new_north))

def pad_rows(field):
    return jnp.pad(field, ((2, 2), (0, 0)))

def reference(surface_start, east_start, north_start, still_depth, roughness, wet_masks, gauge_tiles, gauge_cells, gauge_values, survey_surface):
    total = jnp.zeros(roughness.shape, jnp.float32)
    for event_index in range(EVENTS):

        def misfit(rough_field):
            surface = surface_start[event_index]
            east = east_start[event_index]
            north = north_start[event_index]
            for step_index in range(STEPS):
                wetness = wet_masks[event_index, step_index].astype(jnp.float32)
                surface, east, north = advance(pad_rows(surface), pad_rows(east), pad_rows(north), pad_rows(still_depth), pad_rows(rough_field), pad_rows(wetness))
            flat_index = (gauge_tiles[event_index, :, 0] * (ROWS_DEV * COLS) + gauge_cells[event_index]).astype(jnp.int32)
            missing = surface.reshape(-1)[flat_index] - gauge_values[event_index]
            spread = surface - survey_surface[event_index]
            return 0.5 * jnp.sum(missing * missing) + 0.5 * jnp.sum(spread * spread)
        total = total + jax.grad(misfit)(roughness)
    return total
```

```python
import functools
import jax
import jax.numpy as jnp
from jax import lax
from jax.experimental import pallas as pl
from jax.experimental.pallas import tpu as pltpu
from jax.sharding import PartitionSpec as P

LANES = 128
ROWS = 8
STEP = 4
RIM1 = ("s0", "v1", "b", "s1", "r", "u1", "k", "sv")
RIM2 = ("s1", "w0", "v2", "h", "u2", "sv")
RIM3 = ("v2", "h", "s2", "sv")
SENT = tuple((1, x) for x in RIM1) + tuple((2, x) for x in RIM2) + tuple((3, x) for x in RIM3)
SLOT = {key: i for i, key in enumerate(SENT)}
PASS = ("s2_1", "s2_2", "s2_3", "y1", "w0")


def masks(rows):
    lane = lax.broadcasted_iota(jnp.int32, (rows, LANES), 1)
    sub = lax.broadcasted_iota(jnp.int32, (rows, LANES), 0) & (ROWS - 1)
    return lane, sub


def across(ref, c, n, lane, lead=ROWS):
    x = ref[lead + ROWS * c : lead + ROWS * (c + n), :]
    left = ref[ROWS * c : ROWS * (c + n), :]
    right = ref[2 * lead + ROWS * c : 2 * lead + ROWS * (c + n), :]
    ahead = pltpu.roll(jnp.where(lane == 0, right, x), LANES - 1, 1)
    behind = pltpu.roll(jnp.where(lane == LANES - 1, left, x), 1, 1)
    return ahead - behind


def along(ref, rim, c, n, sub):
    down = ref[ROWS + 1 + ROWS * c : ROWS + 1 + ROWS * (c + n), :]
    up = ref[ROWS - 1 + ROWS * c : ROWS - 1 + ROWS * (c + n), :]
    edge = 0.0 if rim is None else rim[ROWS * c : ROWS * (c + n), :]
    return jnp.where(sub == ROWS - 1, edge, down) - jnp.where(sub == 0, edge, up)


def across_dense(x, scr, lane):
    tiles = x.shape[0]
    scr[ROWS : ROWS + tiles, :] = x
    right = scr[ROWS + 1 : ROWS + 1 + tiles, :]
    left = scr[ROWS - 1 : ROWS - 1 + tiles, :]
    ahead = pltpu.roll(jnp.where(lane == 0, right, x), LANES - 1, 1)
    behind = pltpu.roll(jnp.where(lane == LANES - 1, left, x), 1, 1)
    return ahead - behind


def clear_ends(*refs):
    zero = jnp.zeros((ROWS, LANES), jnp.float32)
    for ref in refs:
        ref[0:ROWS, :] = zero
        ref[ref.shape[0] - ROWS :, :] = zero


def row_of(ref, row, tiles, lead=0):
    return ref[pl.ds(lead + row, tiles, stride=ROWS), :]


def prepare_kernel(
    s0_ref, u0_ref, v0_ref, h_ref, rough_ref, wet_ref, sv_ref,
    down_ref, up_ref, u1_ref, v1_ref, b_ref, q1_ref, k_ref, t0_ref, kr_ref,
    s0p, u1p, v1p, s1p, u2p, v2p, hh, rr, w0q, s2p,
):
    total = s0_ref.shape[0]
    tiles = total // ROWS
    lane, sub = masks(ROWS * STEP)
    clear_ends(s0p, u1p, v1p, s1p, u2p, v2p)
    s0p[ROWS : ROWS + total, :] = s0_ref[...]
    blocks = range(0, tiles, STEP)

    def cut(c, lead=0):
        return slice(lead + ROWS * c, lead + ROWS * (c + STEP))

    for c in blocks:
        at = cut(c)
        depth, rough, east, north = h_ref[at, :], rough_ref[at, :], u0_ref[at, :], v0_ref[at, :]
        wet = wet_ref[at, :].astype(jnp.float32)
        kr = 4.0 * rough * jnp.exp((-4.0 / 3.0) * jnp.log(depth))
        k = 0.5 * kr * rough
        speed = jnp.sqrt(east * east + north * north + 1.0)
        inverse = 1.0 / (1.0 + k * speed)
        y = wet * inverse
        b = 0.2 * depth * y
        u1 = y * east - b * across(s0p, c, STEP, lane)
        v1 = y * north - b * along(s0p, None, c, STEP, sub)
        u1p[cut(c, ROWS), :] = u1
        v1p[cut(c, ROWS), :] = v1
        u1_ref[at, :] = u1
        v1_ref[at, :] = v1
        b_ref[at, :] = b
        k_ref[at, :] = k
        kr_ref[at, :] = kr
        t0_ref[at, :] = kr * speed * inverse
        w0q[at, :] = 0.25 * wet
    for c in blocks:
        at = cut(c)
        quarter = w0q[at, :]
        q1 = s0_ref[at, :] - quarter * across(u1p, c, STEP, lane)
        q1_ref[at, :] = q1
        s1p[cut(c, ROWS), :] = q1 - quarter * along(v1p, None, c, STEP, sub)
    for c in blocks:
        at = cut(c)
        wet = wet_ref[cut(c, total), :].astype(jnp.float32)
        east, north = u1_ref[at, :], v1_ref[at, :]
        depth = 0.2 * h_ref[at, :]
        y = wet / (1.0 + k_ref[at, :] * jnp.sqrt(east * east + north * north + 1.0))
        h = depth * y
        hh[at, :] = h
        rr[at, :] = depth * wet
        u2p[cut(c, ROWS), :] = y * east - h * across(s1p, c, STEP, lane)
        v2p[cut(c, ROWS), :] = y * north - h * along(s1p, None, c, STEP, sub)
    for c in blocks:
        at = cut(c)
        wet = wet_ref[cut(c, total), :].astype(jnp.float32)
        change = across(u2p, c, STEP, lane) + along(v2p, None, c, STEP, sub)
        s2p[at, :] = s1p[cut(c, ROWS), :] - 0.25 * wet * change
    held = {
        (1, "s0"): (s0_ref, 0), (1, "v1"): (v1_ref, 0), (1, "b"): (b_ref, 0), (1, "s1"): (s1p, ROWS),
        (1, "r"): (rr, 0), (1, "u1"): (u1_ref, 0), (1, "k"): (k_ref, 0), (1, "sv"): (sv_ref, 0),
        (2, "s1"): (s1p, ROWS), (2, "w0"): (w0q, 0), (2, "v2"): (v2p, ROWS), (2, "h"): (hh, 0),
        (2, "u2"): (u2p, ROWS), (2, "sv"): (sv_ref, 0),
        (3, "v2"): (v2p, ROWS), (3, "h"): (hh, 0), (3, "s2"): (s2p, 0), (3, "sv"): (sv_ref, 0),
    }
    for key, place in SLOT.items():
        ref, lead = held[key]
        down_ref[place * tiles : (place + 1) * tiles, :] = row_of(ref, ROWS - key[0], tiles, lead)
        up_ref[place * tiles : (place + 1) * tiles, :] = row_of(ref, key[0] - 1, tiles, lead)


def forward_kernel(
    top_ref, bot_ref, s0_ref, h_ref, wet_ref, u1_ref, v1i_ref, b_ref, q1_ref, k_ref, kr_ref,
    v1_ref, s2_ref, u2_ref, v2_ref, y_ref, yh_ref, t2_ref, kk_ref, pass_ref,
    v1p, s1p, u2p, v2p, v1r, s1r, v2r, da, db, dc, dd, de, df,
):
    total = s0_ref.shape[0]
    tiles = total // ROWS
    lane, sub = masks(ROWS * STEP)
    dlane = lax.broadcasted_iota(jnp.int32, (tiles, LANES), 1)
    clear_ends(v1p, s1p, u2p, v2p, da, db, dc, dd, de, df)
    blocks = range(0, tiles, STEP)

    def cut(c, lead=0):
        return slice(lead + ROWS * c, lead + ROWS * (c + STEP))

    sides = ((top_ref, -1.0, 0, (da, db, dc)), (bot_ref, 1.0, ROWS - 1, (dd, de, df)))

    def got(ref, n, name):
        place = SLOT[(n, name)]
        return ref[place * tiles : (place + 1) * tiles, :]

    v1p[ROWS : ROWS + total, :] = v1i_ref[...]
    kept = []
    for ref, sigma, edge, scr in sides:
        b = got(ref, 1, "b")
        delta = b * row_of(s0_ref, edge, tiles)
        v1_1 = got(ref, 1, "v1") + sigma * delta
        v1_e = row_of(v1i_ref, edge, tiles) - sigma * row_of(b_ref, edge, tiles) * got(ref, 1, "s0")
        v1p[pl.ds(ROWS + edge, tiles, stride=ROWS), :] = v1_e
        v1r[pl.ds(edge, tiles, stride=ROWS), :] = v1_1
        bump = got(ref, 2, "w0") * delta
        s1_2 = got(ref, 2, "s1") + bump
        w0_1 = jnp.where(b > 0.0, 1.0, 0.0)
        s1_1 = got(ref, 1, "s1") + (0.25 * sigma) * w0_1 * v1_e
        s1r[pl.ds(edge, tiles, stride=ROWS), :] = s1_1
        r, u1_1, h2, h3 = got(ref, 1, "r"), got(ref, 1, "u1"), got(ref, 2, "h"), got(ref, 3, "h")
        w1_1 = jnp.where(r > 0.0, 1.0, 0.0)
        inverse = 1.0 / (1.0 + got(ref, 1, "k") * jnp.sqrt(u1_1 * u1_1 + v1_1 * v1_1 + 1.0))
        v2i_2 = got(ref, 2, "v2")
        v2_2 = v2i_2 + 0.25 * w0_1 * h2 * v1_e
        v2_3 = got(ref, 3, "v2") + sigma * h3 * bump
        u2_2 = got(ref, 2, "u2") - h2 * across_dense(bump, scr[0], dlane)
        s2_3 = got(ref, 3, "s2") + (0.25 * sigma) * jnp.where(h3 > 0.0, 1.0, 0.0) * (v2_2 - v2i_2)
        u2_1 = (w1_1 * u1_1 - r * across_dense(s1_1, scr[1], dlane)) * inverse
        kept.append((v1_1, s1_1, s1_2, w0_1, w1_1, r, inverse, h2, v2_2, v2_3, u2_1, u2_2, s2_3))
    for c in blocks:
        at = cut(c)
        quarter = 0.25 * wet_ref[at, :].astype(jnp.float32)
        v1_ref[at, :] = v1p[cut(c, ROWS), :]
        s1p[cut(c, ROWS), :] = q1_ref[at, :] - quarter * along(v1p, v1r, c, STEP, sub)
    late = []
    for (ref, sigma, edge, scr), values in zip(sides, kept):
        v1_1, s1_1, s1_2, w0_1, w1_1, r, inverse, h2, v2_2, v2_3, u2_1, u2_2, s2_3 = values
        s1_e = row_of(s1p, edge, tiles, ROWS)
        v2_1 = (w1_1 * v1_1 - sigma * r * (s1_2 - s1_e)) * inverse
        v2r[pl.ds(edge, tiles, stride=ROWS), :] = v2_1
        w1_2 = jnp.where(h2 > 0.0, 0.25, 0.0)
        s2_2 = s1_2 - w1_2 * (across_dense(u2_2, scr[2], dlane) + sigma * (v2_3 - v2_1))
        late.append((s2_2, across_dense(u2_1, scr[0], dlane)))
    for c in blocks:
        at = cut(c)
        wet = wet_ref[cut(c, total), :].astype(jnp.float32)
        east, north = u1_ref[at, :], v1_ref[at, :]
        speed2 = east * east + north * north + 1.0
        slow = lax.rsqrt(speed2)
        speed = speed2 * slow
        k = k_ref[at, :]
        inverse = 1.0 / (1.0 + k * speed)
        y = wet * inverse
        yh = 0.2 * h_ref[at, :] * y
        u2 = y * east - yh * across(s1p, c, STEP, lane)
        v2 = y * north - yh * along(s1p, s1r, c, STEP, sub)
        u2p[cut(c, ROWS), :] = u2
        v2p[cut(c, ROWS), :] = v2
        u2_ref[at, :] = u2
        v2_ref[at, :] = v2
        y_ref[at, :] = y
        yh_ref[at, :] = yh
        t2_ref[at, :] = kr_ref[at, :] * speed * inverse
        kk_ref[at, :] = k * inverse * slow
    for c in blocks:
        at = cut(c)
        wet = wet_ref[cut(c, total), :].astype(jnp.float32)
        change = across(u2p, c, STEP, lane) + along(v2p, v2r, c, STEP, sub)
        s2_ref[at, :] = s1p[cut(c, ROWS), :] - 0.25 * wet * change
    for d, ((ref, sigma, edge, scr), values, more) in enumerate(zip(sides, kept, late)):
        v1_1, s1_1, s1_2, w0_1, w1_1, r, inverse, h2, v2_2, v2_3, u2_1, u2_2, s2_3 = values
        s2_2, du2_1 = more
        v2_e = row_of(v2p, edge, tiles, ROWS)
        s2_1 = s1_1 - 0.25 * w1_1 * (du2_1 + sigma * (v2_2 - v2_e))
        for i, value in enumerate((s2_1, s2_2, s2_3, r * inverse, w0_1)):
            first = (d * len(PASS) + i) * tiles
            pass_ref[first : first + tiles, :] = value


def gauge_fields(places, lanes, values, rows):
    grid = lax.broadcasted_iota(jnp.int32, (rows, LANES), 0)
    lane = lax.broadcasted_iota(jnp.int32, (LANES, LANES), 0)
    left, right = [], []
    for place, at, value in zip(places, lanes, values):
        left.append(jnp.where(grid == place, 1.0, 0.0).astype(jnp.bfloat16))
        hit = lane == at
        high = value.astype(jnp.bfloat16).astype(jnp.float32)
        rest = value - high
        middle = rest.astype(jnp.bfloat16).astype(jnp.float32)
        low = rest - middle
        parts = [jnp.where(hit, part, 0.0).astype(jnp.bfloat16) for part in (high, middle, low)]
        parts.append(jnp.where(hit, 1.0, 0.0).astype(jnp.bfloat16))
        right.append(jnp.concatenate(parts, axis=0))
    out = lax.dot_general(
        jnp.concatenate(left, axis=1), jnp.concatenate(right, axis=1), (((1,), (1,)), ((), ())),
        preferred_element_type=jnp.float32,
    )
    summed = out[:, :LANES] + out[:, LANES : 2 * LANES] + out[:, 2 * LANES : 3 * LANES]
    return summed, out[:, 3 * LANES :]


def backward_kernel(
    gauge_ref, top_ref, bot_ref, pass_ref, wet_ref, sv_ref, u1_ref, v1_ref, s2_ref, u2_ref, v2_ref,
    y_ref, yh_ref, t2_ref, kk_ref, t0_ref,
    grad_ref,
    x2p, x2r, pup, pvp, pvr, x1p, x1r, b2s, au1, av1, vs, ms, vt, mt, da, db, dc, dd,
):
    total = s2_ref.shape[0]
    tiles = total // ROWS
    lane, sub = masks(ROWS * STEP)
    dlane = lax.broadcasted_iota(jnp.int32, (tiles, LANES), 1)
    clear_ends(x2p, pup, pvp, x1p, da, db, dc, dd)
    blocks = range(0, tiles, STEP)

    def cut(c, lead=0):
        return slice(lead + ROWS * c, lead + ROWS * (c + STEP))

    x = gauge_ref[...]
    turned = jnp.concatenate([x, pltpu.roll(x, LANES - 4, 1)], axis=0)
    if turned.shape[0] < LANES:
        fill = jnp.full((LANES - turned.shape[0], LANES), -1.0, jnp.float32)
        turned = jnp.concatenate([turned, fill], axis=0)
    turned = jnp.transpose(turned)
    for group in range(3):
        places, lanes, values = [], [], []
        for k in range(4):
            cell = turned[8 * group + k : 8 * group + k + 1, :].astype(jnp.int32)
            value = turned[64 + 8 * group + k : 65 + 8 * group + k, :]
            row, col = cell >> 13, cell & 8191
            tile = col >> 7
            if group == 0:
                place = jnp.where(cell < 0, -1, tile * ROWS + row)
            elif group == 1:
                place = jnp.where((cell < 0) | (row < 5), -1, (7 - row) * tiles + tile)
            else:
                place = jnp.where((cell < 0) | (row > 2), -1, row * tiles + tile)
            places.append(place)
            lanes.append(col & 127)
            values.append(value)
        if group == 0:
            vs[...], ms[...] = gauge_fields(places, lanes, values, total)
        else:
            first = (group - 1) * 3 * tiles
            sums, counts = gauge_fields(places, lanes, values, 3 * tiles)
            vt[first : first + 3 * tiles, :] = sums
            mt[first : first + 3 * tiles, :] = counts
    sides = ((top_ref, -1.0, 0, (da, db)), (bot_ref, 1.0, ROWS - 1, (dc, dd)))

    def got(ref, n, name):
        place = SLOT[(n, name)]
        return ref[place * tiles : (place + 1) * tiles, :]

    kept = []
    for d, (ref, sigma, edge, scr) in enumerate(sides):
        values = [pass_ref[(d * len(PASS) + i) * tiles : (d * len(PASS) + i + 1) * tiles, :] for i in range(len(PASS))]
        senses = []
        for n in (1, 2, 3):
            first = (d * 3 + n - 1) * tiles
            count, summed = mt[first : first + tiles, :], vt[first : first + tiles, :]
            senses.append((1.0 + count) * values[n - 1] - got(ref, n, "sv") - summed)
        x2_1 = jnp.where(got(ref, 1, "r") > 0.0, senses[0], 0.0)
        x2_2 = jnp.where(got(ref, 2, "h") > 0.0, senses[1], 0.0)
        x2_3 = jnp.where(got(ref, 3, "h") > 0.0, senses[2], 0.0)
        x2r[pl.ds(edge, tiles, stride=ROWS), :] = x2_1
        y1, w0_1 = values[3], values[4]
        pu_1 = 0.25 * y1 * across_dense(x2_1, scr[0], dlane)
        pv_2 = (0.25 * sigma) * got(ref, 2, "h") * (x2_3 - x2_1)
        kept.append((senses[0] + across_dense(pu_1, scr[1], dlane) + sigma * pv_2, x2_2, y1, w0_1))
    for c in blocks:
        at = cut(c)
        wet = wet_ref[cut(c, total), :].astype(jnp.float32)
        b2 = (1.0 + ms[at, :]) * s2_ref[at, :] - sv_ref[at, :] - vs[at, :]
        b2s[at, :] = b2
        x2p[cut(c, ROWS), :] = wet * b2
    for (ref, sigma, edge, scr), (part, x2_2, y1, w0_1) in zip(sides, kept):
        pvr[pl.ds(edge, tiles, stride=ROWS), :] = (0.25 * sigma) * y1 * (x2_2 - row_of(x2p, edge, tiles, ROWS))
    for c in blocks:
        at = cut(c)
        a_u2 = 0.25 * across(x2p, c, STEP, lane)
        a_v2 = 0.25 * along(x2p, x2r, c, STEP, sub)
        energy = a_u2 * u2_ref[at, :] + a_v2 * v2_ref[at, :]
        y, yh, pull = y_ref[at, :], yh_ref[at, :], energy * kk_ref[at, :]
        pup[cut(c, ROWS), :] = yh * a_u2
        pvp[cut(c, ROWS), :] = yh * a_v2
        au1[at, :] = y * a_u2 - pull * u1_ref[at, :]
        av1[at, :] = y * a_v2 - pull * v1_ref[at, :]
        vs[at, :] = energy * t2_ref[at, :]
    for (ref, sigma, edge, scr), (part, x2_2, y1, w0_1) in zip(sides, kept):
        x1r[pl.ds(edge, tiles, stride=ROWS), :] = w0_1 * (part - sigma * row_of(pvp, edge, tiles, ROWS))
    for c in blocks:
        at = cut(c)
        wet = wet_ref[at, :].astype(jnp.float32)
        a_s1 = b2s[at, :] + across(pup, c, STEP, lane) + along(pvp, pvr, c, STEP, sub)
        x1p[cut(c, ROWS), :] = wet * a_s1
    for c in blocks:
        at = cut(c)
        a_u1 = au1[at, :] + 0.25 * across(x1p, c, STEP, lane)
        a_v1 = av1[at, :] + 0.25 * along(x1p, x1r, c, STEP, sub)
        energy = a_u1 * u1_ref[at, :] + a_v1 * v1_ref[at, :]
        grad_ref[at, :] = -(energy * t0_ref[at, :] + vs[at, :])


def gauge_kernel(tile_ref, cell_ref, value_ref, out_ref):
    strips = out_ref.shape[0]
    listed = tile_ref.shape[1]
    hit = lax.broadcasted_iota(jnp.int32, (strips, listed), 0) == tile_ref[...]
    earlier = lax.broadcasted_iota(jnp.int32, (listed, listed), 0) < lax.broadcasted_iota(jnp.int32, (listed, listed), 1)
    rank = jnp.dot(
        jnp.where(hit, 1.0, 0.0).astype(jnp.bfloat16), jnp.where(earlier, 1.0, 0.0).astype(jnp.bfloat16),
        preferred_element_type=jnp.float32,
    )
    rank = jnp.where(hit, rank, -1.0)
    cell = cell_ref[...].astype(jnp.float32) + 1.0
    value = value_ref[...]
    lane = lax.broadcasted_iota(jnp.int32, (strips, LANES), 1)
    line = lax.broadcasted_iota(jnp.int32, (strips, LANES), 0)
    own = jnp.full((strips, LANES), -1.0, jnp.float32)
    for k in range(8):
        taken = rank == float(k)
        cells = jnp.sum(jnp.where(taken, cell, 0.0), axis=1, keepdims=True) - 1.0
        values = jnp.sum(jnp.where(taken, value, 0.0), axis=1, keepdims=True)
        own = jnp.where(lane == k, cells, jnp.where(lane == 64 + k, values, own))
    above = jnp.where(line == 0, -1.0, pltpu.roll(own, 1, 0))
    below = jnp.where(line == strips - 1, -1.0, pltpu.roll(own, strips - 1, 0))
    part = lane & 63
    out_ref[...] = jnp.where(part < 8, own, jnp.where(part < 16, pltpu.roll(above, 8, 1), pltpu.roll(below, 16, 1)))


def sum_kernel(x_ref, out_ref):
    count, lines = x_ref.shape[0], x_ref.shape[1]
    for k in range(lines // ROWS):
        acc = x_ref[0, ROWS * k : ROWS * (k + 1), :]
        for e in range(1, count):
            acc = acc + x_ref[e, ROWS * k : ROWS * (k + 1), :]
        out_ref[:, LANES * k : LANES * (k + 1)] = acc


def call(kernel, outs, scratch, name):
    shapes = [jax.ShapeDtypeStruct(o, jnp.float32) for o in outs]
    return pl.pallas_call(
        kernel,
        out_shape=shapes if len(shapes) > 1 else shapes[0],
        scratch_shapes=[pltpu.VMEM(s, jnp.float32) for s in scratch],
        name=name,
        compiler_params=pltpu.CompilerParams(vmem_limit_bytes=48 * 1024 * 1024),
    )


def tiled(field):
    rows, cols = field.shape[-2:]
    lead = field.shape[:-2]
    parts = field.reshape(-1, rows, cols // LANES, LANES)
    return jnp.transpose(parts, (0, 2, 1, 3)).reshape(-1, LANES)


def shifted(value, axis, steps):
    count = lax.axis_size(axis)
    initial, last = max(0, -steps), min(count, count - steps)
    return lax.ppermute(value, axis, [(i, i + steps) for i in range(initial, last)])


def per_device(s0, u0, v0, depth, rough, wet, gauge_tiles, gauge_cells, gauge_values, survey):
    row_count, col_count = depth.shape
    assert row_count == ROWS and col_count == 8192
    total = row_count * col_count // LANES
    tiles = col_count // LANES
    strips = lax.axis_size("tile")
    events = lax.axis_size("event")
    s0, u0, v0, depth, rough, wet, survey = (tiled(f) for f in (s0[0], u0[0], v0[0], depth, rough, wet[0], survey[0]))
    field, padded, dense = (total, LANES), (total + 2 * ROWS, LANES), (tiles + 2 * ROWS, LANES)
    packet = (len(SENT) * tiles, LANES)
    down, up, u1, v1i, b, q1, k, t0, kr = call(
        prepare_kernel, [packet, packet] + [field] * 7, [padded] * 6 + [field] * 4, "prepare"
    )(s0, u0, v0, depth, rough, wet, survey)
    from_above = shifted(down, "tile", 1)
    from_below = shifted(up, "tile", -1)
    listed = gauge_cells.shape[1]
    send = call(gauge_kernel, [(strips, LANES)], [], "gauges")(
        gauge_tiles.reshape(1, listed), gauge_cells.reshape(1, listed), gauge_values.reshape(1, listed)
    )
    gauges = lax.all_to_all(send, "tile", 0, 0, tiled=True)
    rim_pass = (2 * len(PASS) * tiles, LANES)
    v1, s2, u2, v2, y, yh, t2, kk, passed = call(
        forward_kernel, [field] * 8 + [rim_pass], [padded] * 4 + [field] * 3 + [dense] * 6, "forward"
    )(from_above, from_below, s0, depth, wet, u1, v1i, b, q1, k, kr)
    grad = call(
        backward_kernel, [field],
        [padded, field, padded, padded, field, padded, field, field, field, field, field, field]
        + [(6 * tiles, LANES)] * 2 + [dense] * 4,
        "backward",
    )(gauges, from_above, from_below, passed, wet, survey, u1, v1, s2, u2, v2, y, yh, t2, kk, t0)
    parts = lax.all_to_all(grad.reshape(events, total // events, LANES), "event", 0, 0, tiled=True)
    return call(sum_kernel, [(ROWS, col_count // events)], [], "total")(parts)


def solution(mesh):
    placed = (
        P("event", "tile", None),
        P("event", "tile", None),
        P("event", "tile", None),
        P("tile", None),
        P("tile", None),
        P("event", None, "tile", None),
        P("event", "tile", None),
        P("event", "tile"),
        P("event", "tile"),
        P("event", "tile", None),
    )
    return jax.shard_map(
        per_device, mesh=mesh, in_specs=placed, out_specs=P("tile", "event"), check_vma=False
    )
```

```python
import functools
import jax
import jax.numpy as jnp
from jax import lax
from jax.experimental import pallas as pl
from jax.experimental.pallas import tpu as pltpu
from jax.sharding import PartitionSpec as P

LANES = 128
ROWS = 8
STEP = 4
GRANT = 16 * 1024 * 1024
HERE = None
RIM1 = ("s0", "v1", "b", "s1", "r", "u1", "k", "sv")
RIM2 = ("s1", "w0", "v2", "h", "u2", "sv")
RIM3 = ("v2", "h", "s2", "sv")
SENT = tuple((1, x) for x in RIM1) + tuple((2, x) for x in RIM2) + tuple((3, x) for x in RIM3)
SLOT = {key: i for i, key in enumerate(SENT)}
PASS = ("s2_1", "s2_2", "s2_3", "y1", "w0", "h2", "h3", "sv1", "sv2", "sv3")
EDGES = ((1, "s0"), (1, "v1"), (1, "b"))


def masks(rows):
    lane = lax.broadcasted_iota(jnp.int32, (rows, LANES), 1)
    sub = lax.broadcasted_iota(jnp.int32, (rows, LANES), 0) & (ROWS - 1)
    return lane, sub


def across(ref, c, n, lane, lead=ROWS):
    x = ref[lead + ROWS * c : lead + ROWS * (c + n), :]
    left = ref[ROWS * c : ROWS * (c + n), :]
    right = ref[2 * lead + ROWS * c : 2 * lead + ROWS * (c + n), :]
    ahead = pltpu.roll(jnp.where(lane == 0, right, x), LANES - 1, 1)
    behind = pltpu.roll(jnp.where(lane == LANES - 1, left, x), 1, 1)
    return ahead - behind


def along(ref, rim, c, n, sub):
    down = ref[ROWS + 1 + ROWS * c : ROWS + 1 + ROWS * (c + n), :]
    up = ref[ROWS - 1 + ROWS * c : ROWS - 1 + ROWS * (c + n), :]
    edge = 0.0 if rim is None else rim[ROWS * c : ROWS * (c + n), :]
    return jnp.where(sub == ROWS - 1, edge, down) - jnp.where(sub == 0, edge, up)


def across_dense(x, scr, lane):
    tiles = x.shape[0]
    scr[ROWS : ROWS + tiles, :] = x
    right = scr[ROWS + 1 : ROWS + 1 + tiles, :]
    left = scr[ROWS - 1 : ROWS - 1 + tiles, :]
    ahead = pltpu.roll(jnp.where(lane == 0, right, x), LANES - 1, 1)
    behind = pltpu.roll(jnp.where(lane == LANES - 1, left, x), 1, 1)
    return ahead - behind


def clear_ends(*refs):
    zero = jnp.zeros((ROWS, LANES), jnp.float32)
    for ref in refs:
        ref[0:ROWS, :] = zero
        ref[ref.shape[0] - ROWS :, :] = zero


def row_of(ref, row, tiles, lead=0):
    return ref[pl.ds(lead + row, tiles, stride=ROWS), :]


def prepare_kernel(
    tile_ref, cell_ref, value_ref, s0p, h_ref, rough_ref, u0_ref, v0_ref, wet_ref, sv_ref,
    down_ref, up_ref, send_ref, edge_ref, u1_ref, v1_ref, q1_ref, k_ref, t0_ref, kr_ref,
    u1p, v1p, s1p, u2p, v2p, hh, s2p, b_ref, w0q, w1_ref, rr, *, arrive, leave,
):
    total = u1_ref.shape[0]
    tiles = total // ROWS
    lane, sub = masks(ROWS * STEP)
    clear_ends(s0p, u1p, v1p, s1p, u2p, v2p)
    arrive(0, 1, 2)
    gauge_table(tile_ref, cell_ref, value_ref, send_ref)
    arrive(3, 4, 5, 6, 7, 8)
    blocks = range(0, tiles, STEP)

    def cut(c, lead=0):
        return slice(lead + ROWS * c, lead + ROWS * (c + STEP))

    for c in blocks:
        at = cut(c)
        depth, rough, east, north = h_ref[at, :], rough_ref[at, :], u0_ref[at, :], v0_ref[at, :]
        wet = wet_ref[at, :].astype(jnp.float32)
        kr = 4.0 * rough * jnp.exp((-4.0 / 3.0) * jnp.log(depth))
        k = 0.5 * kr * rough
        speed = jnp.sqrt(east * east + north * north + 1.0)
        inverse = 1.0 / (1.0 + k * speed)
        y = wet * inverse
        b = 0.2 * depth * y
        u1 = y * east - b * across(s0p, c, STEP, lane)
        v1 = y * north - b * along(s0p, None, c, STEP, sub)
        u1p[cut(c, ROWS), :] = u1
        v1p[cut(c, ROWS), :] = v1
        u1_ref[at, :] = u1
        v1_ref[at, :] = v1
        b_ref[at, :] = b
        k_ref[at, :] = k
        kr_ref[at, :] = kr
        t0_ref[at, :] = kr * speed * inverse
        w0q[at, :] = 0.25 * wet
    leave(4, 5, 7, 8, 9)
    for c in blocks:
        at = cut(c)
        quarter = w0q[at, :]
        q1 = s0p[cut(c, ROWS), :] - quarter * across(u1p, c, STEP, lane)
        q1_ref[at, :] = q1
        s1p[cut(c, ROWS), :] = q1 - quarter * along(v1p, None, c, STEP, sub)
    leave(6)
    for c in blocks:
        at = cut(c)
        wet = wet_ref[cut(c, total), :].astype(jnp.float32)
        east, north = u1_ref[at, :], v1_ref[at, :]
        depth = 0.2 * h_ref[at, :]
        y = wet / (1.0 + k_ref[at, :] * jnp.sqrt(east * east + north * north + 1.0))
        h = depth * y
        hh[at, :] = h
        rr[at, :] = depth * wet
        w1_ref[at, :] = wet
        u2p[cut(c, ROWS), :] = y * east - h * across(s1p, c, STEP, lane)
        v2p[cut(c, ROWS), :] = y * north - h * along(s1p, None, c, STEP, sub)
    for c in blocks:
        at = cut(c)
        change = across(u2p, c, STEP, lane) + along(v2p, None, c, STEP, sub)
        s2p[at, :] = s1p[cut(c, ROWS), :] - 0.25 * w1_ref[at, :] * change
    held = {
        (1, "s0"): (s0p, ROWS), (1, "v1"): (v1_ref, 0), (1, "b"): (b_ref, 0), (1, "s1"): (s1p, ROWS),
        (1, "r"): (rr, 0), (1, "u1"): (u1_ref, 0), (1, "k"): (k_ref, 0), (1, "sv"): (sv_ref, 0),
        (2, "s1"): (s1p, ROWS), (2, "w0"): (w0q, 0), (2, "v2"): (v2p, ROWS), (2, "h"): (hh, 0),
        (2, "u2"): (u2p, ROWS), (2, "sv"): (sv_ref, 0),
        (3, "v2"): (v2p, ROWS), (3, "h"): (hh, 0), (3, "s2"): (s2p, 0), (3, "sv"): (sv_ref, 0),
    }
    arrive(9)
    for i, key in enumerate(EDGES):
        ref, lead = held[key]
        for j, row in enumerate((0, ROWS - 1)):
            first = (j * len(EDGES) + i) * tiles
            edge_ref[first : first + tiles, :] = row_of(ref, row, tiles, lead)
    leave(3)
    for key, place in SLOT.items():
        ref, lead = held[key]
        down_ref[place * tiles : (place + 1) * tiles, :] = row_of(ref, ROWS - key[0], tiles, lead)
        up_ref[place * tiles : (place + 1) * tiles, :] = row_of(ref, key[0] - 1, tiles, lead)


def forward_kernel(
    edge_ref, top_ref, bot_ref, v1i_ref, q1_ref, wet_ref, u1_ref, k_ref, h_ref, kr_ref,
    v1_ref, s2_ref, u2_ref, v2_ref, y_ref, yh_ref, t2_ref, kk_ref, pass_ref,
    v1p, s1p, u2p, v2p, v1r, s1r, v2r, da, db, dc, dd, de, df, *, arrive, leave,
):
    total = u1_ref.shape[0]
    tiles = total // ROWS
    lane, sub = masks(ROWS * STEP)
    dlane = lax.broadcasted_iota(jnp.int32, (tiles, LANES), 1)
    clear_ends(v1p, s1p, u2p, v2p, da, db, dc, dd, de, df)
    blocks = range(0, tiles, STEP)

    def cut(c, lead=0):
        return slice(lead + ROWS * c, lead + ROWS * (c + STEP))

    sides = ((top_ref, -1.0, 0, (da, db, dc)), (bot_ref, 1.0, ROWS - 1, (dd, de, df)))

    def got(ref, n, name):
        place = SLOT[(n, name)]
        return ref[place * tiles : (place + 1) * tiles, :]

    def own(edge, i):
        first = (len(EDGES) * (edge > 0) + i) * tiles
        return edge_ref[first : first + tiles, :]

    arrive(0, 3)
    v1p[ROWS : ROWS + total, :] = v1i_ref[...]
    kept = []
    for ref, sigma, edge, scr in sides:
        b = got(ref, 1, "b")
        delta = b * own(edge, 0)
        v1_1 = got(ref, 1, "v1") + sigma * delta
        v1_e = own(edge, 1) - sigma * own(edge, 2) * got(ref, 1, "s0")
        v1p[pl.ds(ROWS + edge, tiles, stride=ROWS), :] = v1_e
        v1r[pl.ds(edge, tiles, stride=ROWS), :] = v1_1
        bump = got(ref, 2, "w0") * delta
        s1_2 = got(ref, 2, "s1") + bump
        w0_1 = jnp.where(b > 0.0, 1.0, 0.0)
        s1_1 = got(ref, 1, "s1") + (0.25 * sigma) * w0_1 * v1_e
        s1r[pl.ds(edge, tiles, stride=ROWS), :] = s1_1
        r, u1_1, h2, h3 = got(ref, 1, "r"), got(ref, 1, "u1"), got(ref, 2, "h"), got(ref, 3, "h")
        w1_1 = jnp.where(r > 0.0, 1.0, 0.0)
        inverse = 1.0 / (1.0 + got(ref, 1, "k") * jnp.sqrt(u1_1 * u1_1 + v1_1 * v1_1 + 1.0))
        v2i_2 = got(ref, 2, "v2")
        v2_2 = v2i_2 + 0.25 * w0_1 * h2 * v1_e
        v2_3 = got(ref, 3, "v2") + sigma * h3 * bump
        u2_2 = got(ref, 2, "u2") - h2 * across_dense(bump, scr[0], dlane)
        s2_3 = got(ref, 3, "s2") + (0.25 * sigma) * jnp.where(h3 > 0.0, 1.0, 0.0) * (v2_2 - v2i_2)
        u2_1 = (w1_1 * u1_1 - r * across_dense(s1_1, scr[1], dlane)) * inverse
        kept.append((v1_1, s1_1, s1_2, w0_1, w1_1, r, inverse, h2, v2_2, v2_3, u2_1, u2_2, s2_3))
    arrive(4, 5)
    for c in blocks:
        at = cut(c)
        quarter = 0.25 * wet_ref[at, :].astype(jnp.float32)
        v1_ref[at, :] = v1p[cut(c, ROWS), :]
        s1p[cut(c, ROWS), :] = q1_ref[at, :] - quarter * along(v1p, v1r, c, STEP, sub)
    leave(0)
    arrive(6, 7, 8, 9)
    late = []
    for (ref, sigma, edge, scr), values in zip(sides, kept):
        v1_1, s1_1, s1_2, w0_1, w1_1, r, inverse, h2, v2_2, v2_3, u2_1, u2_2, s2_3 = values
        s1_e = row_of(s1p, edge, tiles, ROWS)
        v2_1 = (w1_1 * v1_1 - sigma * r * (s1_2 - s1_e)) * inverse
        v2r[pl.ds(edge, tiles, stride=ROWS), :] = v2_1
        w1_2 = jnp.where(h2 > 0.0, 0.25, 0.0)
        s2_2 = s1_2 - w1_2 * (across_dense(u2_2, scr[2], dlane) + sigma * (v2_3 - v2_1))
        late.append((s2_2, across_dense(u2_1, scr[0], dlane)))
    for c in blocks:
        at = cut(c)
        east, north = u1_ref[at, :], v1_ref[at, :]
        speed2 = east * east + north * north + 1.0
        slow = lax.rsqrt(speed2)
        speed = speed2 * slow
        k = k_ref[at, :]
        inverse = 1.0 / (1.0 + k * speed)
        y = wet_ref[cut(c, total), :].astype(jnp.float32) * inverse
        yh = 0.2 * h_ref[at, :] * y
        u2 = y * east - yh * across(s1p, c, STEP, lane)
        v2 = y * north - yh * along(s1p, s1r, c, STEP, sub)
        u2p[cut(c, ROWS), :] = u2
        v2p[cut(c, ROWS), :] = v2
        u2_ref[at, :] = u2
        v2_ref[at, :] = v2
        y_ref[at, :] = y
        yh_ref[at, :] = yh
        t2_ref[at, :] = kr_ref[at, :] * speed * inverse
        kk_ref[at, :] = k * inverse * slow
    leave(2, 3, 4, 5, 6, 7)
    for c in blocks:
        at = cut(c)
        wet = wet_ref[cut(c, total), :].astype(jnp.float32)
        change = across(u2p, c, STEP, lane) + along(v2p, v2r, c, STEP, sub)
        s2_ref[at, :] = s1p[cut(c, ROWS), :] - 0.25 * wet * change
    leave(1)
    for d, ((ref, sigma, edge, scr), values, more) in enumerate(zip(sides, kept, late)):
        v1_1, s1_1, s1_2, w0_1, w1_1, r, inverse, h2, v2_2, v2_3, u2_1, u2_2, s2_3 = values
        s2_2, du2_1 = more
        v2_e = row_of(v2p, edge, tiles, ROWS)
        s2_1 = s1_1 - 0.25 * w1_1 * (du2_1 + sigma * (v2_2 - v2_e))
        surveyed = [got(ref, n, "sv") for n in (1, 2, 3)]
        for i, value in enumerate((s2_1, s2_2, s2_3, r * inverse, w0_1, h2, got(ref, 3, "h"), *surveyed)):
            first = (d * len(PASS) + i) * tiles
            pass_ref[first : first + tiles, :] = value
    leave(8)


def gauge_fields(places, lanes, values, rows):
    grid = lax.broadcasted_iota(jnp.int32, (rows, LANES), 0)
    lane = lax.broadcasted_iota(jnp.int32, (LANES, LANES), 0)
    left, right = [], []
    for place, at, value in zip(places, lanes, values):
        left.append(jnp.where(grid == place, 1.0, 0.0).astype(jnp.bfloat16))
        hit = lane == at
        high = value.astype(jnp.bfloat16).astype(jnp.float32)
        rest = value - high
        middle = rest.astype(jnp.bfloat16).astype(jnp.float32)
        low = rest - middle
        parts = [jnp.where(hit, part, 0.0).astype(jnp.bfloat16) for part in (high, middle, low)]
        parts.append(jnp.where(hit, 1.0, 0.0).astype(jnp.bfloat16))
        right.append(jnp.concatenate(parts, axis=0))
    out = lax.dot_general(
        jnp.concatenate(left, axis=1), jnp.concatenate(right, axis=1), (((1,), (1,)), ((), ())),
        preferred_element_type=jnp.float32,
    )
    summed = out[:, :LANES] + out[:, LANES : 2 * LANES] + out[:, 2 * LANES : 3 * LANES]
    return summed, out[:, 3 * LANES :]


def backward_kernel(
    gauge_ref, s2_ref, sv_ref, wet_ref, pass_ref, u2_ref, v2_ref, kk_ref, y_ref, yh_ref, u1_ref, v1_ref, t2_ref, t0_ref,
    grad_ref,
    x2p, x2r, pup, pvp, pvr, x1p, x1r, b2s, au1, av1, vs, ms, vt, mt, da, db, dc, dd, *, arrive, leave,
):
    total = s2_ref.shape[0]
    tiles = total // ROWS
    lane, sub = masks(ROWS * STEP)
    dlane = lax.broadcasted_iota(jnp.int32, (tiles, LANES), 1)
    clear_ends(x2p, pup, pvp, x1p, da, db, dc, dd)
    blocks = range(0, tiles, STEP)

    def cut(c, lead=0):
        return slice(lead + ROWS * c, lead + ROWS * (c + STEP))

    x = gauge_ref[...]
    turned = jnp.concatenate([x, pltpu.roll(x, LANES - 4, 1)], axis=0)
    if turned.shape[0] < LANES:
        fill = jnp.full((LANES - turned.shape[0], LANES), -1.0, jnp.float32)
        turned = jnp.concatenate([turned, fill], axis=0)
    turned = jnp.transpose(turned)
    for group in range(3):
        places, lanes, values = [], [], []
        for k in range(4):
            cell = turned[8 * group + k : 8 * group + k + 1, :].astype(jnp.int32)
            value = turned[64 + 8 * group + k : 65 + 8 * group + k, :]
            row, col = cell >> 13, cell & 8191
            tile = col >> 7
            if group == 0:
                place = jnp.where(cell < 0, -1, tile * ROWS + row)
            elif group == 1:
                place = jnp.where((cell < 0) | (row < 5), -1, (7 - row) * tiles + tile)
            else:
                place = jnp.where((cell < 0) | (row > 2), -1, row * tiles + tile)
            places.append(place)
            lanes.append(col & 127)
            values.append(value)
        if group == 0:
            vs[...], ms[...] = gauge_fields(places, lanes, values, total)
        else:
            first = (group - 1) * 3 * tiles
            sums, counts = gauge_fields(places, lanes, values, 3 * tiles)
            vt[first : first + 3 * tiles, :] = sums
            mt[first : first + 3 * tiles, :] = counts
    arrive(1, 2, 3, 4)
    sides = ((-1.0, 0, (da, db)), (1.0, ROWS - 1, (dc, dd)))
    kept = []
    for d, (sigma, edge, scr) in enumerate(sides):
        got = {}
        for i, name in enumerate(PASS):
            first = (d * len(PASS) + i) * tiles
            got[name] = pass_ref[first : first + tiles, :]
        senses = []
        for n in (1, 2, 3):
            first = (d * 3 + n - 1) * tiles
            count, summed = mt[first : first + tiles, :], vt[first : first + tiles, :]
            senses.append((1.0 + count) * got[f"s2_{n}"] - got[f"sv{n}"] - summed)
        y1, h2 = got["y1"], got["h2"]
        x2_1 = jnp.where(y1 > 0.0, senses[0], 0.0)
        x2_2 = jnp.where(h2 > 0.0, senses[1], 0.0)
        x2_3 = jnp.where(got["h3"] > 0.0, senses[2], 0.0)
        x2r[pl.ds(edge, tiles, stride=ROWS), :] = x2_1
        pu_1 = 0.25 * y1 * across_dense(x2_1, scr[0], dlane)
        pv_2 = (0.25 * sigma) * h2 * (x2_3 - x2_1)
        kept.append((senses[0] + across_dense(pu_1, scr[1], dlane) + sigma * pv_2, x2_2, y1, got["w0"]))
    for c in blocks:
        at = cut(c)
        b2 = (1.0 + ms[at, :]) * s2_ref[at, :] - sv_ref[at, :] - vs[at, :]
        b2s[at, :] = b2
        x2p[cut(c, ROWS), :] = wet_ref[cut(c, total), :].astype(jnp.float32) * b2
    arrive(5, 6, 7, 8, 9, 10, 11, 12)
    for (sigma, edge, scr), (part, x2_2, y1, w0_1) in zip(sides, kept):
        pvr[pl.ds(edge, tiles, stride=ROWS), :] = (0.25 * sigma) * y1 * (x2_2 - row_of(x2p, edge, tiles, ROWS))
    for c in blocks:
        at = cut(c)
        a_u2 = 0.25 * across(x2p, c, STEP, lane)
        a_v2 = 0.25 * along(x2p, x2r, c, STEP, sub)
        energy = a_u2 * u2_ref[at, :] + a_v2 * v2_ref[at, :]
        y, yh, pull = y_ref[at, :], yh_ref[at, :], energy * kk_ref[at, :]
        pup[cut(c, ROWS), :] = yh * a_u2
        pvp[cut(c, ROWS), :] = yh * a_v2
        au1[at, :] = y * a_u2 - pull * u1_ref[at, :]
        av1[at, :] = y * a_v2 - pull * v1_ref[at, :]
        vs[at, :] = energy * t2_ref[at, :]
    for (sigma, edge, scr), (part, x2_2, y1, w0_1) in zip(sides, kept):
        x1r[pl.ds(edge, tiles, stride=ROWS), :] = w0_1 * (part - sigma * row_of(pvp, edge, tiles, ROWS))
    for c in blocks:
        at = cut(c)
        a_s1 = b2s[at, :] + across(pup, c, STEP, lane) + along(pvp, pvr, c, STEP, sub)
        x1p[cut(c, ROWS), :] = wet_ref[at, :].astype(jnp.float32) * a_s1
    arrive(13)
    for c in blocks:
        at = cut(c)
        a_u1 = au1[at, :] + 0.25 * across(x1p, c, STEP, lane)
        a_v1 = av1[at, :] + 0.25 * along(x1p, x1r, c, STEP, sub)
        energy = a_u1 * u1_ref[at, :] + a_v1 * v1_ref[at, :]
        grad_ref[at, :] = -(energy * t0_ref[at, :] + vs[at, :])


def gauge_table(tile_ref, cell_ref, value_ref, out_ref):
    strips = out_ref.shape[0]
    listed = tile_ref.shape[1]
    hit = lax.broadcasted_iota(jnp.int32, (strips, listed), 0) == tile_ref[...]
    earlier = lax.broadcasted_iota(jnp.int32, (listed, listed), 0) < lax.broadcasted_iota(jnp.int32, (listed, listed), 1)
    rank = jnp.dot(
        jnp.where(hit, 1.0, 0.0).astype(jnp.bfloat16), jnp.where(earlier, 1.0, 0.0).astype(jnp.bfloat16),
        preferred_element_type=jnp.float32,
    )
    rank = jnp.where(hit, rank, -1.0)
    cell = cell_ref[...].astype(jnp.float32) + 1.0
    value = value_ref[...]
    lane = lax.broadcasted_iota(jnp.int32, (strips, LANES), 1)
    line = lax.broadcasted_iota(jnp.int32, (strips, LANES), 0)
    own = jnp.full((strips, LANES), -1.0, jnp.float32)
    for k in range(8):
        taken = rank == float(k)
        cells = jnp.sum(jnp.where(taken, cell, 0.0), axis=1, keepdims=True) - 1.0
        values = jnp.sum(jnp.where(taken, value, 0.0), axis=1, keepdims=True)
        own = jnp.where(lane == k, cells, jnp.where(lane == 64 + k, values, own))
    above = jnp.where(line == 0, -1.0, pltpu.roll(own, 1, 0))
    below = jnp.where(line == strips - 1, -1.0, pltpu.roll(own, strips - 1, 0))
    part = lane & 63
    out_ref[...] = jnp.where(part < 8, own, jnp.where(part < 16, pltpu.roll(above, 8, 1), pltpu.roll(below, 16, 1)))


def sum_kernel(x_ref, out_ref):
    count, lines = x_ref.shape[0], x_ref.shape[1]
    for k in range(lines // ROWS):
        acc = x_ref[0, ROWS * k : ROWS * (k + 1), :]
        for e in range(1, count):
            acc = acc + x_ref[e, ROWS * k : ROWS * (k + 1), :]
        out_ref[:, LANES * k : LANES * (k + 1)] = acc


def call(body, ins, outs, scratch, name):
    count, given = len(ins), len(outs)
    moved = [i for i, (_, lead) in enumerate(ins) if lead is not HERE]
    copied = [i for i, (shape, kept) in enumerate(outs) if not kept]

    def kernel(*refs):
        sources, results, rest = refs[:count], refs[count : count + given], refs[count + given :]
        landed, left, own = rest[: len(moved)], rest[len(moved) : len(moved) + len(copied)], rest[len(moved) + len(copied) : -2]
        into, out_of = rest[-2:]
        operands, arrivals = list(sources), {}
        for j, i in enumerate(moved):
            lead, target = ins[i][1], landed[j]
            operands[i] = target
            if lead:
                target = target.at[pl.ds(lead, sources[i].shape[0])]
            arrivals[i] = pltpu.make_async_copy(sources[i], target, into.at[j])
            arrivals[i].start()
        places, departures = list(results), {}
        for j, i in enumerate(copied):
            departures[i] = pltpu.make_async_copy(left[j], results[i], out_of.at[j])
            places[i] = left[j]

        def arrive(*which):
            for i in which:
                arrivals[i].wait()

        def leave(*which):
            for i in which:
                departures[i].start()

        body(*operands, *places, *own, arrive=arrive, leave=leave)
        for departure in departures.values():
            departure.wait()

    return pl.pallas_call(
        kernel,
        out_shape=[(jax.ShapeDtypeStruct if kept else pltpu.HBM)(shape, jnp.float32) for shape, kept in outs],
        in_specs=[pl.BlockSpec(memory_space=pltpu.VMEM if lead is HERE else pltpu.HBM) for _, lead in ins],
        out_specs=[pl.BlockSpec(memory_space=pltpu.VMEM if kept else pltpu.HBM) for _, kept in outs],
        scratch_shapes=[
            pltpu.VMEM((ins[i][0].shape[0] + 2 * ins[i][1], ins[i][0].shape[1]), ins[i][0].dtype) for i in moved
        ]
        + [pltpu.VMEM(outs[i][0], jnp.float32) for i in copied]
        + [pltpu.VMEM(shape, jnp.float32) for shape in scratch]
        + [pltpu.SemaphoreType.DMA((len(moved),)), pltpu.SemaphoreType.DMA((max(1, len(copied)),))],
        name=name,
        compiler_params=pltpu.CompilerParams(vmem_limit_bytes=GRANT),
    )(*(x if lead is HERE else pltpu.with_memory_space_constraint(x, pltpu.HBM) for x, lead in ins))


def tiled(field):
    rows, cols = field.shape[-2:]
    lead = field.shape[:-2]
    parts = field.reshape(-1, rows, cols // LANES, LANES)
    return jnp.transpose(parts, (0, 2, 1, 3)).reshape(-1, LANES)


def shifted(value, axis, steps):
    count = lax.axis_size(axis)
    initial, last = max(0, -steps), min(count, count - steps)
    return lax.ppermute(value, axis, [(i, i + steps) for i in range(initial, last)])


def per_device(s0, u0, v0, depth, rough, wet, gauge_tiles, gauge_cells, gauge_values, survey):
    row_count, col_count = depth.shape
    assert row_count == ROWS and col_count == 8192
    total = row_count * col_count // LANES
    tiles = col_count // LANES
    strips = lax.axis_size("tile")
    events = lax.axis_size("event")
    s0, u0, v0, depth, rough, wet, survey = (tiled(f) for f in (s0[0], u0[0], v0[0], depth, rough, wet[0], survey[0]))
    field, padded, dense = (total, LANES), (total + 2 * ROWS, LANES), (tiles + 2 * ROWS, LANES)
    packet = (len(SENT) * tiles, LANES)
    listed = (1, gauge_cells.shape[1])
    lists = [(x.reshape(listed), 0) for x in (gauge_tiles, gauge_cells, gauge_values)]
    down, up, send, edges, u1, v1i, q1, k, t0, kr = call(
        prepare_kernel,
        lists + [(s0, ROWS)] + [(x, 0) for x in (depth, rough, u0, v0, wet, survey)],
        [(packet, True), (packet, True), ((strips, LANES), True), ((2 * len(EDGES) * tiles, LANES), False)]
        + [(field, False)] * 6,
        [padded] * 5 + [field] * 6,
        "prepare",
    )
    from_above = shifted(down, "tile", 1)
    from_below = shifted(up, "tile", -1)
    gauges = lax.all_to_all(send, "tile", 0, 0, tiled=True)
    v1, s2, u2, v2, y, yh, t2, kk, passed = call(
        forward_kernel,
        [(edges, 0), (from_above, HERE), (from_below, HERE)] + [(x, 0) for x in (v1i, q1, wet, u1, k, depth, kr)],
        [(field, False)] * 8 + [((2 * len(PASS) * tiles, LANES), False)],
        [padded] * 4 + [field] * 3 + [dense] * 6,
        "forward",
    )
    (grad,) = call(
        backward_kernel,
        [(gauges, HERE)] + [(x, 0) for x in (s2, survey, wet, passed, u2, v2, kk, y, yh, u1, v1, t2, t0)],
        [(field, True)],
        [padded, field, padded, padded, field, padded, field, field, field, field, field, field]
        + [(6 * tiles, LANES)] * 2 + [dense] * 4,
        "backward",
    )
    parts = lax.all_to_all(grad.reshape(events, total // events, LANES), "event", 0, 0, tiled=True)
    return pl.pallas_call(
        sum_kernel, out_shape=jax.ShapeDtypeStruct((ROWS, col_count // events), jnp.float32), name="total",
        compiler_params=pltpu.CompilerParams(vmem_limit_bytes=GRANT),
    )(parts)


def solution(mesh):
    placed = (
        P("event", "tile", None),
        P("event", "tile", None),
        P("event", "tile", None),
        P("tile", None),
        P("tile", None),
        P("event", None, "tile", None),
        P("event", "tile", None),
        P("event", "tile"),
        P("event", "tile"),
        P("event", "tile", None),
    )
    return jax.shard_map(
        per_device, mesh=mesh, in_specs=placed, out_specs=P("tile", "event"), check_vma=False
    )
```

```python
import functools
import jax
import jax.numpy as jnp
from jax import lax
from jax.experimental import pallas as pl
from jax.experimental.pallas import tpu as pltpu
from jax.sharding import PartitionSpec as P

LANES = 128
ROWS = 8
STEP = 4
GRANT = 16 * 1024 * 1024
HERE = None
STRIP_LEAD = 42
EVENT_LEAD = 4
RIM1 = ("s0", "v1", "b", "s1", "r", "u1", "k", "sv")
RIM2 = ("s1", "w0", "v2", "h", "u2", "sv")
RIM3 = ("v2", "h", "s2", "sv")
SENT = tuple((1, x) for x in RIM1) + tuple((2, x) for x in RIM2) + tuple((3, x) for x in RIM3)
SLOT = {key: i for i, key in enumerate(SENT)}
PASS = ("s2_1", "s2_2", "s2_3", "y1", "w0", "h2", "h3", "sv1", "sv2", "sv3")
EDGES = ((1, "s0"), (1, "v1"), (1, "b"))


def masks(rows):
    lane = lax.broadcasted_iota(jnp.int32, (rows, LANES), 1)
    sub = lax.broadcasted_iota(jnp.int32, (rows, LANES), 0) & (ROWS - 1)
    return lane, sub


def across(ref, c, n, lane, lead=ROWS):
    x = ref[lead + ROWS * c : lead + ROWS * (c + n), :]
    left = ref[ROWS * c : ROWS * (c + n), :]
    right = ref[2 * lead + ROWS * c : 2 * lead + ROWS * (c + n), :]
    ahead = pltpu.roll(jnp.where(lane == 0, right, x), LANES - 1, 1)
    behind = pltpu.roll(jnp.where(lane == LANES - 1, left, x), 1, 1)
    return ahead - behind


def along(ref, rim, c, n, sub):
    down = ref[ROWS + 1 + ROWS * c : ROWS + 1 + ROWS * (c + n), :]
    up = ref[ROWS - 1 + ROWS * c : ROWS - 1 + ROWS * (c + n), :]
    edge = 0.0 if rim is None else rim[ROWS * c : ROWS * (c + n), :]
    return jnp.where(sub == ROWS - 1, edge, down) - jnp.where(sub == 0, edge, up)


def across_dense(x, scr, lane):
    tiles = x.shape[0]
    scr[ROWS : ROWS + tiles, :] = x
    right = scr[ROWS + 1 : ROWS + 1 + tiles, :]
    left = scr[ROWS - 1 : ROWS - 1 + tiles, :]
    ahead = pltpu.roll(jnp.where(lane == 0, right, x), LANES - 1, 1)
    behind = pltpu.roll(jnp.where(lane == LANES - 1, left, x), 1, 1)
    return ahead - behind


def clear_ends(*refs):
    zero = jnp.zeros((ROWS, LANES), jnp.float32)
    for ref in refs:
        ref[0:ROWS, :] = zero
        ref[ref.shape[0] - ROWS :, :] = zero


def row_of(ref, row, tiles, lead=0):
    return ref[pl.ds(lead + row, tiles, stride=ROWS), :]


def prepare_kernel(
    tile_ref, cell_ref, value_ref, s0p, h_ref, rough_ref, u0_ref, v0_ref, wet_ref, sv_ref,
    down_ref, up_ref, send_ref, edge_ref, u1_ref, v1_ref, q1_ref, k_ref, t0_ref, kr_ref,
    u1p, v1p, s1p, u2p, v2p, hh, s2p, b_ref, w0q, w1_ref, rr, *, arrive, leave,
):
    total = u1_ref.shape[0]
    tiles = total // ROWS
    lane, sub = masks(ROWS * STEP)
    clear_ends(s0p, u1p, v1p, s1p, u2p, v2p)
    arrive(0, 1, 2)
    gauge_table(tile_ref, cell_ref, value_ref, send_ref)
    arrive(3, 4, 5, 6, 7, 8)
    blocks = range(0, tiles, STEP)

    def cut(c, lead=0):
        return slice(lead + ROWS * c, lead + ROWS * (c + STEP))

    for c in blocks:
        at = cut(c)
        depth, rough, east, north = h_ref[at, :], rough_ref[at, :], u0_ref[at, :], v0_ref[at, :]
        wet = wet_ref[at, :].astype(jnp.float32)
        kr = 4.0 * rough * jnp.exp((-4.0 / 3.0) * jnp.log(depth))
        k = 0.5 * kr * rough
        speed = jnp.sqrt(east * east + north * north + 1.0)
        inverse = 1.0 / (1.0 + k * speed)
        y = wet * inverse
        b = 0.2 * depth * y
        u1 = y * east - b * across(s0p, c, STEP, lane)
        v1 = y * north - b * along(s0p, None, c, STEP, sub)
        u1p[cut(c, ROWS), :] = u1
        v1p[cut(c, ROWS), :] = v1
        u1_ref[at, :] = u1
        v1_ref[at, :] = v1
        b_ref[at, :] = b
        k_ref[at, :] = k
        kr_ref[at, :] = kr
        t0_ref[at, :] = kr * speed * inverse
        w0q[at, :] = 0.25 * wet
    leave(4, 5, 7, 8, 9)
    for c in blocks:
        at = cut(c)
        quarter = w0q[at, :]
        q1 = s0p[cut(c, ROWS), :] - quarter * across(u1p, c, STEP, lane)
        q1_ref[at, :] = q1
        s1p[cut(c, ROWS), :] = q1 - quarter * along(v1p, None, c, STEP, sub)
    leave(6)
    for c in blocks:
        at = cut(c)
        wet = wet_ref[cut(c, total), :].astype(jnp.float32)
        east, north = u1_ref[at, :], v1_ref[at, :]
        depth = 0.2 * h_ref[at, :]
        y = wet / (1.0 + k_ref[at, :] * jnp.sqrt(east * east + north * north + 1.0))
        h = depth * y
        hh[at, :] = h
        rr[at, :] = depth * wet
        w1_ref[at, :] = wet
        u2p[cut(c, ROWS), :] = y * east - h * across(s1p, c, STEP, lane)
        v2p[cut(c, ROWS), :] = y * north - h * along(s1p, None, c, STEP, sub)
    for c in blocks:
        at = cut(c)
        change = across(u2p, c, STEP, lane) + along(v2p, None, c, STEP, sub)
        s2p[at, :] = s1p[cut(c, ROWS), :] - 0.25 * w1_ref[at, :] * change
    held = {
        (1, "s0"): (s0p, ROWS), (1, "v1"): (v1_ref, 0), (1, "b"): (b_ref, 0), (1, "s1"): (s1p, ROWS),
        (1, "r"): (rr, 0), (1, "u1"): (u1_ref, 0), (1, "k"): (k_ref, 0), (1, "sv"): (sv_ref, 0),
        (2, "s1"): (s1p, ROWS), (2, "w0"): (w0q, 0), (2, "v2"): (v2p, ROWS), (2, "h"): (hh, 0),
        (2, "u2"): (u2p, ROWS), (2, "sv"): (sv_ref, 0),
        (3, "v2"): (v2p, ROWS), (3, "h"): (hh, 0), (3, "s2"): (s2p, 0), (3, "sv"): (sv_ref, 0),
    }
    arrive(9)
    for i, key in enumerate(EDGES):
        ref, lead = held[key]
        for j, row in enumerate((0, ROWS - 1)):
            first = (j * len(EDGES) + i) * tiles
            edge_ref[first : first + tiles, :] = row_of(ref, row, tiles, lead)
    leave(3)
    for key, place in SLOT.items():
        ref, lead = held[key]
        down_ref[place * tiles : (place + 1) * tiles, :] = row_of(ref, ROWS - key[0], tiles, lead)
        up_ref[place * tiles : (place + 1) * tiles, :] = row_of(ref, key[0] - 1, tiles, lead)


def forward_kernel(
    edge_ref, top_ref, bot_ref, v1i_ref, q1_ref, wet_ref, u1_ref, k_ref, h_ref, kr_ref,
    v1_ref, s2_ref, u2_ref, v2_ref, y_ref, yh_ref, t2_ref, kk_ref, pass_ref,
    v1p, s1p, u2p, v2p, v1r, s1r, v2r, da, db, dc, dd, de, df, *, arrive, leave,
):
    total = u1_ref.shape[0]
    tiles = total // ROWS
    lane, sub = masks(ROWS * STEP)
    dlane = lax.broadcasted_iota(jnp.int32, (tiles, LANES), 1)
    clear_ends(v1p, s1p, u2p, v2p, da, db, dc, dd, de, df)
    blocks = range(0, tiles, STEP)

    def cut(c, lead=0):
        return slice(lead + ROWS * c, lead + ROWS * (c + STEP))

    sides = ((top_ref, -1.0, 0, (da, db, dc)), (bot_ref, 1.0, ROWS - 1, (dd, de, df)))

    def got(ref, n, name):
        place = SLOT[(n, name)]
        return ref[place * tiles : (place + 1) * tiles, :]

    def own(edge, i):
        first = (len(EDGES) * (edge > 0) + i) * tiles
        return edge_ref[first : first + tiles, :]

    arrive(0, 3)
    v1p[ROWS : ROWS + total, :] = v1i_ref[...]
    kept = []
    for ref, sigma, edge, scr in sides:
        b = got(ref, 1, "b")
        delta = b * own(edge, 0)
        v1_1 = got(ref, 1, "v1") + sigma * delta
        v1_e = own(edge, 1) - sigma * own(edge, 2) * got(ref, 1, "s0")
        v1p[pl.ds(ROWS + edge, tiles, stride=ROWS), :] = v1_e
        v1r[pl.ds(edge, tiles, stride=ROWS), :] = v1_1
        bump = got(ref, 2, "w0") * delta
        s1_2 = got(ref, 2, "s1") + bump
        w0_1 = jnp.where(b > 0.0, 1.0, 0.0)
        s1_1 = got(ref, 1, "s1") + (0.25 * sigma) * w0_1 * v1_e
        s1r[pl.ds(edge, tiles, stride=ROWS), :] = s1_1
        r, u1_1, h2, h3 = got(ref, 1, "r"), got(ref, 1, "u1"), got(ref, 2, "h"), got(ref, 3, "h")
        w1_1 = jnp.where(r > 0.0, 1.0, 0.0)
        inverse = 1.0 / (1.0 + got(ref, 1, "k") * jnp.sqrt(u1_1 * u1_1 + v1_1 * v1_1 + 1.0))
        v2i_2 = got(ref, 2, "v2")
        v2_2 = v2i_2 + 0.25 * w0_1 * h2 * v1_e
        v2_3 = got(ref, 3, "v2") + sigma * h3 * bump
        u2_2 = got(ref, 2, "u2") - h2 * across_dense(bump, scr[0], dlane)
        s2_3 = got(ref, 3, "s2") + (0.25 * sigma) * jnp.where(h3 > 0.0, 1.0, 0.0) * (v2_2 - v2i_2)
        u2_1 = (w1_1 * u1_1 - r * across_dense(s1_1, scr[1], dlane)) * inverse
        kept.append((v1_1, s1_1, s1_2, w0_1, w1_1, r, inverse, h2, v2_2, v2_3, u2_1, u2_2, s2_3))
    arrive(4, 5)
    for c in blocks:
        at = cut(c)
        quarter = 0.25 * wet_ref[at, :].astype(jnp.float32)
        v1_ref[at, :] = v1p[cut(c, ROWS), :]
        s1p[cut(c, ROWS), :] = q1_ref[at, :] - quarter * along(v1p, v1r, c, STEP, sub)
    leave(0)
    arrive(6, 7, 8, 9)
    late = []
    for (ref, sigma, edge, scr), values in zip(sides, kept):
        v1_1, s1_1, s1_2, w0_1, w1_1, r, inverse, h2, v2_2, v2_3, u2_1, u2_2, s2_3 = values
        s1_e = row_of(s1p, edge, tiles, ROWS)
        v2_1 = (w1_1 * v1_1 - sigma * r * (s1_2 - s1_e)) * inverse
        v2r[pl.ds(edge, tiles, stride=ROWS), :] = v2_1
        w1_2 = jnp.where(h2 > 0.0, 0.25, 0.0)
        s2_2 = s1_2 - w1_2 * (across_dense(u2_2, scr[2], dlane) + sigma * (v2_3 - v2_1))
        late.append((s2_2, across_dense(u2_1, scr[0], dlane)))
    for c in blocks:
        at = cut(c)
        east, north = u1_ref[at, :], v1_ref[at, :]
        speed2 = east * east + north * north + 1.0
        slow = lax.rsqrt(speed2)
        speed = speed2 * slow
        k = k_ref[at, :]
        inverse = 1.0 / (1.0 + k * speed)
        y = wet_ref[cut(c, total), :].astype(jnp.float32) * inverse
        yh = 0.2 * h_ref[at, :] * y
        u2 = y * east - yh * across(s1p, c, STEP, lane)
        v2 = y * north - yh * along(s1p, s1r, c, STEP, sub)
        u2p[cut(c, ROWS), :] = u2
        v2p[cut(c, ROWS), :] = v2
        u2_ref[at, :] = u2
        v2_ref[at, :] = v2
        y_ref[at, :] = y
        yh_ref[at, :] = yh
        t2_ref[at, :] = kr_ref[at, :] * speed * inverse
        kk_ref[at, :] = k * inverse * slow
    leave(2, 3, 4, 5, 6, 7)
    for c in blocks:
        at = cut(c)
        wet = wet_ref[cut(c, total), :].astype(jnp.float32)
        change = across(u2p, c, STEP, lane) + along(v2p, v2r, c, STEP, sub)
        s2_ref[at, :] = s1p[cut(c, ROWS), :] - 0.25 * wet * change
    leave(1)
    for d, ((ref, sigma, edge, scr), values, more) in enumerate(zip(sides, kept, late)):
        v1_1, s1_1, s1_2, w0_1, w1_1, r, inverse, h2, v2_2, v2_3, u2_1, u2_2, s2_3 = values
        s2_2, du2_1 = more
        v2_e = row_of(v2p, edge, tiles, ROWS)
        s2_1 = s1_1 - 0.25 * w1_1 * (du2_1 + sigma * (v2_2 - v2_e))
        surveyed = [got(ref, n, "sv") for n in (1, 2, 3)]
        for i, value in enumerate((s2_1, s2_2, s2_3, r * inverse, w0_1, h2, got(ref, 3, "h"), *surveyed)):
            first = (d * len(PASS) + i) * tiles
            pass_ref[first : first + tiles, :] = value
    leave(8)


def gauge_fields(places, lanes, values, rows):
    grid = lax.broadcasted_iota(jnp.int32, (rows, LANES), 0)
    lane = lax.broadcasted_iota(jnp.int32, (LANES, LANES), 0)
    left, right = [], []
    for place, at, value in zip(places, lanes, values):
        left.append(jnp.where(grid == place, 1.0, 0.0).astype(jnp.bfloat16))
        hit = lane == at
        high = value.astype(jnp.bfloat16).astype(jnp.float32)
        rest = value - high
        middle = rest.astype(jnp.bfloat16).astype(jnp.float32)
        low = rest - middle
        parts = [jnp.where(hit, part, 0.0).astype(jnp.bfloat16) for part in (high, middle, low)]
        parts.append(jnp.where(hit, 1.0, 0.0).astype(jnp.bfloat16))
        right.append(jnp.concatenate(parts, axis=0))
    out = lax.dot_general(
        jnp.concatenate(left, axis=1), jnp.concatenate(right, axis=1), (((1,), (1,)), ((), ())),
        preferred_element_type=jnp.float32,
    )
    summed = out[:, :LANES] + out[:, LANES : 2 * LANES] + out[:, 2 * LANES : 3 * LANES]
    return summed, out[:, 3 * LANES :]


def backward_kernel(
    gauge_ref, s2_ref, sv_ref, wet_ref, pass_ref, u2_ref, v2_ref, kk_ref, y_ref, yh_ref, u1_ref, v1_ref, t2_ref, t0_ref,
    grad_ref,
    x2p, x2r, pup, pvp, pvr, x1p, x1r, b2s, au1, av1, vs, ms, vt, mt, da, db, dc, dd, *, arrive, leave, shift,
):
    total = s2_ref.shape[0]
    tiles = total // ROWS
    lane, sub = masks(ROWS * STEP)
    dlane = lax.broadcasted_iota(jnp.int32, (tiles, LANES), 1)
    clear_ends(x2p, pup, pvp, x1p, da, db, dc, dd)
    blocks = range(0, tiles, STEP)

    def cut(c, lead=0):
        return slice(lead + ROWS * c, lead + ROWS * (c + STEP))

    x = gauge_ref[...]
    turned = jnp.concatenate([x, pltpu.roll(x, LANES - 4, 1)], axis=0)
    if turned.shape[0] < LANES:
        fill = jnp.full((LANES - turned.shape[0], LANES), -1.0, jnp.float32)
        turned = jnp.concatenate([turned, fill], axis=0)
    turned = jnp.transpose(turned)
    for group in range(3):
        places, lanes, values = [], [], []
        for k in range(4):
            cell = turned[8 * group + k : 8 * group + k + 1, :].astype(jnp.int32)
            value = turned[64 + 8 * group + k : 65 + 8 * group + k, :]
            row, col = cell >> 13, cell & 8191
            tile = col >> 7
            if group == 0:
                place = jnp.where(cell < 0, -1, tile * ROWS + row)
            elif group == 1:
                place = jnp.where((cell < 0) | (row < 5), -1, (7 - row) * tiles + tile)
            else:
                place = jnp.where((cell < 0) | (row > 2), -1, row * tiles + tile)
            places.append(place)
            lanes.append(col & 127)
            values.append(value)
        if group == 0:
            vs[...], ms[...] = gauge_fields(places, lanes, values, total)
        else:
            first = (group - 1) * 3 * tiles
            sums, counts = gauge_fields(places, lanes, values, 3 * tiles)
            vt[first : first + 3 * tiles, :] = sums
            mt[first : first + 3 * tiles, :] = counts
    arrive(1, 2, 3, 4)
    sides = ((-1.0, 0, (da, db)), (1.0, ROWS - 1, (dc, dd)))
    kept = []
    for d, (sigma, edge, scr) in enumerate(sides):
        got = {}
        for i, name in enumerate(PASS):
            first = (d * len(PASS) + i) * tiles
            got[name] = pass_ref[first : first + tiles, :]
        senses = []
        for n in (1, 2, 3):
            first = (d * 3 + n - 1) * tiles
            count, summed = mt[first : first + tiles, :], vt[first : first + tiles, :]
            senses.append((1.0 + count) * got[f"s2_{n}"] - got[f"sv{n}"] - summed)
        y1, h2 = got["y1"], got["h2"]
        x2_1 = jnp.where(y1 > 0.0, senses[0], 0.0)
        x2_2 = jnp.where(h2 > 0.0, senses[1], 0.0)
        x2_3 = jnp.where(got["h3"] > 0.0, senses[2], 0.0)
        x2r[pl.ds(edge, tiles, stride=ROWS), :] = x2_1
        pu_1 = 0.25 * y1 * across_dense(x2_1, scr[0], dlane)
        pv_2 = (0.25 * sigma) * h2 * (x2_3 - x2_1)
        kept.append((senses[0] + across_dense(pu_1, scr[1], dlane) + sigma * pv_2, x2_2, y1, got["w0"]))
    for c in blocks:
        at = cut(c)
        b2 = (1.0 + ms[at, :]) * s2_ref[at, :] - sv_ref[at, :] - vs[at, :]
        b2s[at, :] = b2
        x2p[cut(c, ROWS), :] = wet_ref[cut(c, total), :].astype(jnp.float32) * b2
    arrive(5, 6, 7, 8, 9, 10, 11, 12)
    for (sigma, edge, scr), (part, x2_2, y1, w0_1) in zip(sides, kept):
        pvr[pl.ds(edge, tiles, stride=ROWS), :] = (0.25 * sigma) * y1 * (x2_2 - row_of(x2p, edge, tiles, ROWS))
    for c in blocks:
        at = cut(c)
        a_u2 = 0.25 * across(x2p, c, STEP, lane)
        a_v2 = 0.25 * along(x2p, x2r, c, STEP, sub)
        energy = a_u2 * u2_ref[at, :] + a_v2 * v2_ref[at, :]
        y, yh, pull = y_ref[at, :], yh_ref[at, :], energy * kk_ref[at, :]
        pup[cut(c, ROWS), :] = yh * a_u2
        pvp[cut(c, ROWS), :] = yh * a_v2
        au1[at, :] = y * a_u2 - pull * u1_ref[at, :]
        av1[at, :] = y * a_v2 - pull * v1_ref[at, :]
        vs[at, :] = energy * t2_ref[at, :]
    for (sigma, edge, scr), (part, x2_2, y1, w0_1) in zip(sides, kept):
        x1r[pl.ds(edge, tiles, stride=ROWS), :] = w0_1 * (part - sigma * row_of(pvp, edge, tiles, ROWS))
    for c in blocks:
        at = cut(c)
        a_s1 = b2s[at, :] + across(pup, c, STEP, lane) + along(pvp, pvr, c, STEP, sub)
        x1p[cut(c, ROWS), :] = wet_ref[at, :].astype(jnp.float32) * a_s1
    arrive(13)
    for c in blocks:
        at = cut(c)
        a_u1 = au1[at, :] + 0.25 * across(x1p, c, STEP, lane)
        a_v1 = av1[at, :] + 0.25 * along(x1p, x1r, c, STEP, sub)
        energy = a_u1 * u1_ref[at, :] + a_v1 * v1_ref[at, :]
        grad_ref[cut((c - shift) % tiles), :] = -(energy * t0_ref[at, :] + vs[at, :])


def turned_order(count, first):
    return [(i + first) % count for i in range(count)]


def gauge_table(tile_ref, cell_ref, value_ref, out_ref):
    strips = out_ref.shape[0]
    listed = tile_ref.shape[1]
    first = STRIP_LEAD * strips // 64
    hit = (lax.broadcasted_iota(jnp.int32, (strips, listed), 0) + first) % strips == tile_ref[...]
    earlier = lax.broadcasted_iota(jnp.int32, (listed, listed), 0) < lax.broadcasted_iota(jnp.int32, (listed, listed), 1)
    rank = jnp.dot(
        jnp.where(hit, 1.0, 0.0).astype(jnp.bfloat16), jnp.where(earlier, 1.0, 0.0).astype(jnp.bfloat16),
        preferred_element_type=jnp.float32,
    )
    rank = jnp.where(hit, rank, -1.0)
    cell = cell_ref[...].astype(jnp.float32) + 1.0
    value = value_ref[...]
    lane = lax.broadcasted_iota(jnp.int32, (strips, LANES), 1)
    line = (lax.broadcasted_iota(jnp.int32, (strips, LANES), 0) + first) % strips
    own = jnp.full((strips, LANES), -1.0, jnp.float32)
    for k in range(8):
        taken = rank == float(k)
        cells = jnp.sum(jnp.where(taken, cell, 0.0), axis=1, keepdims=True) - 1.0
        values = jnp.sum(jnp.where(taken, value, 0.0), axis=1, keepdims=True)
        own = jnp.where(lane == k, cells, jnp.where(lane == 64 + k, values, own))
    above = jnp.where(line == 0, -1.0, pltpu.roll(own, 1, 0))
    below = jnp.where(line == strips - 1, -1.0, pltpu.roll(own, strips - 1, 0))
    part = lane & 63
    out_ref[...] = jnp.where(part < 8, own, jnp.where(part < 16, pltpu.roll(above, 8, 1), pltpu.roll(below, 16, 1)))


def sum_kernel(x_ref, out_ref):
    count, lines = x_ref.shape[0], x_ref.shape[1]
    for k in range(lines // ROWS):
        acc = x_ref[0, ROWS * k : ROWS * (k + 1), :]
        for e in range(1, count):
            acc = acc + x_ref[e, ROWS * k : ROWS * (k + 1), :]
        out_ref[:, LANES * k : LANES * (k + 1)] = acc


def call(body, ins, outs, scratch, name):
    count, given = len(ins), len(outs)
    moved = [i for i, (_, lead) in enumerate(ins) if lead is not HERE]
    copied = [i for i, (shape, kept) in enumerate(outs) if not kept]

    def kernel(*refs):
        sources, results, rest = refs[:count], refs[count : count + given], refs[count + given :]
        landed, left, own = rest[: len(moved)], rest[len(moved) : len(moved) + len(copied)], rest[len(moved) + len(copied) : -2]
        into, out_of = rest[-2:]
        operands, arrivals = list(sources), {}
        for j, i in enumerate(moved):
            lead, target = ins[i][1], landed[j]
            operands[i] = target
            if lead:
                target = target.at[pl.ds(lead, sources[i].shape[0])]
            arrivals[i] = pltpu.make_async_copy(sources[i], target, into.at[j])
            arrivals[i].start()
        places, departures = list(results), {}
        for j, i in enumerate(copied):
            departures[i] = pltpu.make_async_copy(left[j], results[i], out_of.at[j])
            places[i] = left[j]

        def arrive(*which):
            for i in which:
                arrivals[i].wait()

        def leave(*which):
            for i in which:
                departures[i].start()

        body(*operands, *places, *own, arrive=arrive, leave=leave)
        for departure in departures.values():
            departure.wait()

    return pl.pallas_call(
        kernel,
        out_shape=[(jax.ShapeDtypeStruct if kept else pltpu.HBM)(shape, jnp.float32) for shape, kept in outs],
        in_specs=[pl.BlockSpec(memory_space=pltpu.VMEM if lead is HERE else pltpu.HBM) for _, lead in ins],
        out_specs=[pl.BlockSpec(memory_space=pltpu.VMEM if kept else pltpu.HBM) for _, kept in outs],
        scratch_shapes=[
            pltpu.VMEM((ins[i][0].shape[0] + 2 * ins[i][1], ins[i][0].shape[1]), ins[i][0].dtype) for i in moved
        ]
        + [pltpu.VMEM(outs[i][0], jnp.float32) for i in copied]
        + [pltpu.VMEM(shape, jnp.float32) for shape in scratch]
        + [pltpu.SemaphoreType.DMA((len(moved),)), pltpu.SemaphoreType.DMA((max(1, len(copied)),))],
        name=name,
        compiler_params=pltpu.CompilerParams(vmem_limit_bytes=GRANT),
    )(*(x if lead is HERE else pltpu.with_memory_space_constraint(x, pltpu.HBM) for x, lead in ins))


def tiled(field):
    rows, cols = field.shape[-2:]
    lead = field.shape[:-2]
    parts = field.reshape(-1, rows, cols // LANES, LANES)
    return jnp.transpose(parts, (0, 2, 1, 3)).reshape(-1, LANES)


def shifted(value, axis, steps):
    count = lax.axis_size(axis)
    initial, last = max(0, -steps), min(count, count - steps)
    return lax.ppermute(value, axis, [(i, i + steps) for i in range(initial, last)])


def per_device(s0, u0, v0, depth, rough, wet, gauge_tiles, gauge_cells, gauge_values, survey):
    row_count, col_count = depth.shape
    assert row_count == ROWS and col_count == 8192
    total = row_count * col_count // LANES
    tiles = col_count // LANES
    strips = lax.axis_size("tile")
    events = lax.axis_size("event")
    s0, u0, v0, depth, rough, wet, survey = (tiled(f) for f in (s0[0], u0[0], v0[0], depth, rough, wet[0], survey[0]))
    field, padded, dense = (total, LANES), (total + 2 * ROWS, LANES), (tiles + 2 * ROWS, LANES)
    packet = (len(SENT) * tiles, LANES)
    listed = (1, gauge_cells.shape[1])
    lists = [(x.reshape(listed), 0) for x in (gauge_tiles, gauge_cells, gauge_values)]
    down, up, send, edges, u1, v1i, q1, k, t0, kr = call(
        prepare_kernel,
        lists + [(s0, ROWS)] + [(x, 0) for x in (depth, rough, u0, v0, wet, survey)],
        [(packet, True), (packet, True), ((strips, LANES), True), ((2 * len(EDGES) * tiles, LANES), False)]
        + [(field, False)] * 6,
        [padded] * 5 + [field] * 6,
        "prepare",
    )
    from_above = shifted(down, "tile", 1)
    from_below = shifted(up, "tile", -1)
    gauges = lax.all_to_all(send, "tile", 0, 0, axis_index_groups=[turned_order(strips, STRIP_LEAD * strips // 64)], tiled=True)
    v1, s2, u2, v2, y, yh, t2, kk, passed = call(
        forward_kernel,
        [(edges, 0), (from_above, HERE), (from_below, HERE)] + [(x, 0) for x in (v1i, q1, wet, u1, k, depth, kr)],
        [(field, False)] * 8 + [((2 * len(PASS) * tiles, LANES), False)],
        [padded] * 4 + [field] * 3 + [dense] * 6,
        "forward",
    )
    order = turned_order(events, EVENT_LEAD * events // 8)
    (grad,) = call(
        functools.partial(backward_kernel, shift=order[0] * (tiles // events)),
        [(gauges, HERE)] + [(x, 0) for x in (s2, survey, wet, passed, u2, v2, kk, y, yh, u1, v1, t2, t0)],
        [(field, True)],
        [padded, field, padded, padded, field, padded, field, field, field, field, field, field]
        + [(6 * tiles, LANES)] * 2 + [dense] * 4,
        "backward",
    )
    parts = lax.all_to_all(grad.reshape(events, total // events, LANES), "event", 0, 0, axis_index_groups=[order], tiled=True)
    return pl.pallas_call(
        sum_kernel, out_shape=jax.ShapeDtypeStruct((ROWS, col_count // events), jnp.float32), name="total",
        compiler_params=pltpu.CompilerParams(vmem_limit_bytes=GRANT),
    )(parts)


def solution(mesh):
    placed = (
        P("event", "tile", None),
        P("event", "tile", None),
        P("event", "tile", None),
        P("tile", None),
        P("tile", None),
        P("event", None, "tile", None),
        P("event", "tile", None),
        P("event", "tile"),
        P("event", "tile"),
        P("event", "tile", None),
    )
    return jax.shard_map(
        per_device, mesh=mesh, in_specs=placed, out_specs=P("tile", "event"), check_vma=False
    )
```

```python
import functools
import jax
import jax.numpy as jnp
from jax import lax
from jax.experimental import pallas as pl
from jax.experimental.pallas import tpu as pltpu
from jax.sharding import PartitionSpec as P

LANES = 128
ROWS = 8
STEP = 4
GRANT = 16 * 1024 * 1024
HERE = None
STRIP_LEAD = 42
STRIP_STRIDE = 1
EVENT_LEAD = 4
RIM1 = ("s0", "v1", "b", "s1", "r", "u1", "k", "sv")
RIM2 = ("s1", "w0", "v2", "h", "s2", "sv")
RIM3 = ("h", "s2", "sv")
SENT = tuple((1, x) for x in RIM1) + tuple((2, x) for x in RIM2) + tuple((3, x) for x in RIM3)
SLOT = {key: i for i, key in enumerate(SENT)}
PASS = ("s2_1", "s2_2", "s2_3", "y1", "w0", "h2", "h3", "sv1", "sv2", "sv3")
EDGES = 3


def masks(rows):
    lane = lax.broadcasted_iota(jnp.int32, (rows, LANES), 1)
    sub = lax.broadcasted_iota(jnp.int32, (rows, LANES), 0) & (ROWS - 1)
    return lane, sub


def across(ref, c, n, lane, lead=ROWS):
    x = ref[lead + ROWS * c : lead + ROWS * (c + n), :]
    left = ref[ROWS * c : ROWS * (c + n), :]
    right = ref[2 * lead + ROWS * c : 2 * lead + ROWS * (c + n), :]
    ahead = pltpu.roll(jnp.where(lane == 0, right, x), LANES - 1, 1)
    behind = pltpu.roll(jnp.where(lane == LANES - 1, left, x), 1, 1)
    return ahead - behind


def along(ref, rim, c, n, sub):
    down = ref[ROWS + 1 + ROWS * c : ROWS + 1 + ROWS * (c + n), :]
    up = ref[ROWS - 1 + ROWS * c : ROWS - 1 + ROWS * (c + n), :]
    edge = 0.0 if rim is None else rim[ROWS * c : ROWS * (c + n), :]
    return jnp.where(sub == ROWS - 1, edge, down) - jnp.where(sub == 0, edge, up)


def across_dense(x, scr, lane):
    tiles = x.shape[0]
    scr[ROWS : ROWS + tiles, :] = x
    right = scr[ROWS + 1 : ROWS + 1 + tiles, :]
    left = scr[ROWS - 1 : ROWS - 1 + tiles, :]
    ahead = pltpu.roll(jnp.where(lane == 0, right, x), LANES - 1, 1)
    behind = pltpu.roll(jnp.where(lane == LANES - 1, left, x), 1, 1)
    return ahead - behind


def clear_ends(*refs):
    zero = jnp.zeros((ROWS, LANES), jnp.float32)
    for ref in refs:
        ref[0:ROWS, :] = zero
        ref[ref.shape[0] - ROWS :, :] = zero


def row_of(ref, row, tiles, lead=0):
    return ref[pl.ds(lead + row, tiles, stride=ROWS), :]


def prepare_kernel(
    tile_ref, cell_ref, value_ref, s0p, h_ref, rough_ref, u0_ref, v0_ref, wet_ref, sv_ref,
    down_ref, up_ref, send_ref, edge_ref, u1_ref, v1_ref, q1_ref, k_ref, t0_ref, kr_ref,
    u1p, v1p, s1p, u2p, v2p, hh, s2p, b_ref, w0q, w1_ref, rr, *, arrive, leave,
):
    total = u1_ref.shape[0]
    tiles = total // ROWS
    lane, sub = masks(ROWS * STEP)
    clear_ends(s0p, u1p, v1p, s1p, u2p, v2p)
    arrive(0, 1, 2)
    gauge_table(tile_ref, cell_ref, value_ref, send_ref)
    leave(2)
    arrive(3, 4, 5, 6, 7, 8)
    blocks = range(0, tiles, STEP)

    def cut(c, lead=0):
        return slice(lead + ROWS * c, lead + ROWS * (c + STEP))

    for c in blocks:
        at = cut(c)
        depth, rough, east, north = h_ref[at, :], rough_ref[at, :], u0_ref[at, :], v0_ref[at, :]
        wet = wet_ref[at, :].astype(jnp.float32)
        kr = 4.0 * rough * jnp.exp((-4.0 / 3.0) * jnp.log(depth))
        k = 0.5 * kr * rough
        square = east * east + north * north + 1.0
        speed = square * lax.rsqrt(square)
        inverse = 1.0 / (1.0 + k * speed)
        y = wet * inverse
        b = 0.2 * depth * y
        u1 = y * east - b * across(s0p, c, STEP, lane)
        v1 = y * north - b * along(s0p, None, c, STEP, sub)
        u1p[cut(c, ROWS), :] = u1
        v1p[cut(c, ROWS), :] = v1
        u1_ref[at, :] = u1
        v1_ref[at, :] = v1
        b_ref[at, :] = b
        k_ref[at, :] = k
        kr_ref[at, :] = kr
        t0_ref[at, :] = kr * speed * inverse
        w0q[at, :] = 0.25 * wet
    for i, (ref, lead) in enumerate(((s0p, ROWS), (v1_ref, 0), (b_ref, 0))):
        for j, row in enumerate((0, ROWS - 1)):
            first = (j * EDGES + i) * tiles
            edge_ref[first : first + tiles, :] = row_of(ref, row, tiles, lead)
    leave(3, 4, 5, 7, 8, 9)
    for c in blocks:
        at = cut(c)
        quarter = w0q[at, :]
        q1 = s0p[cut(c, ROWS), :] - quarter * across(u1p, c, STEP, lane)
        q1_ref[at, :] = q1
        s1p[cut(c, ROWS), :] = q1 - quarter * along(v1p, None, c, STEP, sub)
    leave(6)
    for c in blocks:
        at = cut(c)
        wet = wet_ref[cut(c, total), :].astype(jnp.float32)
        east, north = u1_ref[at, :], v1_ref[at, :]
        depth = 0.2 * h_ref[at, :]
        square = east * east + north * north + 1.0
        y = wet / (1.0 + k_ref[at, :] * (square * lax.rsqrt(square)))
        h = depth * y
        hh[at, :] = h
        rr[at, :] = depth * wet
        w1_ref[at, :] = wet
        u2p[cut(c, ROWS), :] = y * east - h * across(s1p, c, STEP, lane)
        v2 = y * north - h * along(s1p, None, c, STEP, sub)
        v2p[cut(c, ROWS), :] = jnp.where((sub == 0) | (sub == ROWS - 1), 0.0, v2)
    for c in blocks:
        at = cut(c)
        change = across(u2p, c, STEP, lane) + along(v2p, None, c, STEP, sub)
        s2p[at, :] = s1p[cut(c, ROWS), :] - 0.25 * w1_ref[at, :] * change
    held = {
        (1, "s0"): (s0p, ROWS), (1, "v1"): (v1_ref, 0), (1, "b"): (b_ref, 0), (1, "s1"): (s1p, ROWS),
        (1, "r"): (rr, 0), (1, "u1"): (u1_ref, 0), (1, "k"): (k_ref, 0), (1, "sv"): (sv_ref, 0),
        (2, "s1"): (s1p, ROWS), (2, "w0"): (w0q, 0), (2, "v2"): (v2p, ROWS), (2, "h"): (hh, 0),
        (2, "s2"): (s2p, 0), (2, "sv"): (sv_ref, 0), (3, "h"): (hh, 0), (3, "s2"): (s2p, 0), (3, "sv"): (sv_ref, 0),
    }
    arrive(9)
    for key, place in SLOT.items():
        ref, lead = held[key]
        down_ref[place * tiles : (place + 1) * tiles, :] = row_of(ref, ROWS - key[0], tiles, lead)
        up_ref[place * tiles : (place + 1) * tiles, :] = row_of(ref, key[0] - 1, tiles, lead)


def forward_kernel(
    edge_ref, top_ref, bot_ref, v1i_ref, q1_ref, wet_ref, u1_ref, k_ref, h_ref, kr_ref,
    v1_ref, s2_ref, u2_ref, v2_ref, y_ref, yh_ref, t2_ref, kk_ref, pass_ref,
    v1p, s1p, u2p, v2p, v1r, s1r, v2r, da, db, dc, dd, de, df, *, arrive, leave,
):
    total = u1_ref.shape[0]
    tiles = total // ROWS
    lane, sub = masks(ROWS * STEP)
    dlane = lax.broadcasted_iota(jnp.int32, (tiles, LANES), 1)
    clear_ends(v1p, s1p, u2p, v2p, da, db, dc, dd, de, df)
    blocks = range(0, tiles, STEP)

    def cut(c, lead=0):
        return slice(lead + ROWS * c, lead + ROWS * (c + STEP))

    sides = ((top_ref, -1.0, 0, (da, db, dc)), (bot_ref, 1.0, ROWS - 1, (dd, de, df)))

    def got(ref, n, name):
        place = SLOT[(n, name)]
        return ref[place * tiles : (place + 1) * tiles, :]

    def own(edge, i):
        first = (EDGES * (edge > 0) + i) * tiles
        return edge_ref[first : first + tiles, :]

    arrive(0, 3)
    v1p[ROWS : ROWS + total, :] = v1i_ref[...]
    kept = []
    for ref, sigma, edge, scr in sides:
        b = got(ref, 1, "b")
        delta = b * own(edge, 0)
        v1_1 = got(ref, 1, "v1") + sigma * delta
        v1_e = own(edge, 1) - sigma * own(edge, 2) * got(ref, 1, "s0")
        v1p[pl.ds(ROWS + edge, tiles, stride=ROWS), :] = v1_e
        v1r[pl.ds(edge, tiles, stride=ROWS), :] = v1_1
        bump = got(ref, 2, "w0") * delta
        s1_2 = got(ref, 2, "s1") + bump
        w0_1 = jnp.where(b > 0.0, 1.0, 0.0)
        s1_1 = got(ref, 1, "s1") + (0.25 * sigma) * w0_1 * v1_e
        s1r[pl.ds(edge, tiles, stride=ROWS), :] = s1_1
        r, u1_1, h2, h3 = got(ref, 1, "r"), got(ref, 1, "u1"), got(ref, 2, "h"), got(ref, 3, "h")
        w1_1 = jnp.where(r > 0.0, 1.0, 0.0)
        inverse = 1.0 / (1.0 + got(ref, 1, "k") * jnp.sqrt(u1_1 * u1_1 + v1_1 * v1_1 + 1.0))
        v2i_2 = got(ref, 2, "v2")
        v2_2 = v2i_2 + 0.25 * w0_1 * h2 * v1_e
        v2_3 = sigma * h3 * bump
        u2_2 = -h2 * across_dense(bump, scr[0], dlane)
        s2_3 = got(ref, 3, "s2") + (0.25 * sigma) * jnp.where(h3 > 0.0, 1.0, 0.0) * (v2_2 - v2i_2)
        u2_1 = (w1_1 * u1_1 - r * across_dense(s1_1, scr[1], dlane)) * inverse
        kept.append((v1_1, s1_1, s1_2, w0_1, w1_1, r, inverse, h2, v2_2, v2_3, u2_1, u2_2, s2_3, bump))
    arrive(4, 5)
    for c in blocks:
        at = cut(c)
        quarter = 0.25 * wet_ref[at, :].astype(jnp.float32)
        v1_ref[at, :] = v1p[cut(c, ROWS), :]
        s1p[cut(c, ROWS), :] = q1_ref[at, :] - quarter * along(v1p, v1r, c, STEP, sub)
    leave(0)
    arrive(6, 7, 8, 9)
    late = []
    for (ref, sigma, edge, scr), values in zip(sides, kept):
        v1_1, s1_1, s1_2, w0_1, w1_1, r, inverse, h2, v2_2, v2_3, u2_1, u2_2, s2_3, bump = values
        s1_e = row_of(s1p, edge, tiles, ROWS)
        v2_1 = (w1_1 * v1_1 - sigma * r * (s1_2 - s1_e)) * inverse
        v2r[pl.ds(edge, tiles, stride=ROWS), :] = v2_1
        w1_2 = jnp.where(h2 > 0.0, 0.25, 0.0)
        s2_2 = got(ref, 2, "s2") + bump - w1_2 * (across_dense(u2_2, scr[2], dlane) + sigma * (v2_3 - v2_1))
        late.append((s2_2, across_dense(u2_1, scr[0], dlane)))
    for c in blocks:
        at = cut(c)
        east, north = u1_ref[at, :], v1_ref[at, :]
        speed2 = east * east + north * north + 1.0
        slow = lax.rsqrt(speed2)
        speed = speed2 * slow
        k = k_ref[at, :]
        inverse = 1.0 / (1.0 + k * speed)
        y = wet_ref[cut(c, total), :].astype(jnp.float32) * inverse
        yh = 0.2 * h_ref[at, :] * y
        u2 = y * east - yh * across(s1p, c, STEP, lane)
        v2 = y * north - yh * along(s1p, s1r, c, STEP, sub)
        u2p[cut(c, ROWS), :] = u2
        v2p[cut(c, ROWS), :] = v2
        u2_ref[at, :] = u2
        v2_ref[at, :] = v2
        y_ref[at, :] = y
        yh_ref[at, :] = yh
        t2_ref[at, :] = kr_ref[at, :] * speed * inverse
        kk_ref[at, :] = k * inverse * slow
    leave(2, 3, 4, 5, 6, 7)
    for c in blocks:
        at = cut(c)
        wet = wet_ref[cut(c, total), :].astype(jnp.float32)
        change = across(u2p, c, STEP, lane) + along(v2p, v2r, c, STEP, sub)
        s2_ref[at, :] = s1p[cut(c, ROWS), :] - 0.25 * wet * change
    leave(1)
    for d, ((ref, sigma, edge, scr), values, more) in enumerate(zip(sides, kept, late)):
        v1_1, s1_1, s1_2, w0_1, w1_1, r, inverse, h2, v2_2, v2_3, u2_1, u2_2, s2_3, bump = values
        s2_2, du2_1 = more
        v2_e = row_of(v2p, edge, tiles, ROWS)
        s2_1 = s1_1 - 0.25 * w1_1 * (du2_1 + sigma * (v2_2 - v2_e))
        surveyed = [got(ref, n, "sv") for n in (1, 2, 3)]
        for i, value in enumerate((s2_1, s2_2, s2_3, r * inverse, w0_1, h2, got(ref, 3, "h"), *surveyed)):
            first = (d * len(PASS) + i) * tiles
            pass_ref[first : first + tiles, :] = value
    leave(8)


def gauge_fields(places, lanes, values, rows):
    grid = lax.broadcasted_iota(jnp.int32, (rows, LANES), 0)
    lane = lax.broadcasted_iota(jnp.int32, (LANES, LANES), 0)
    left, right = [], []
    for place, at, value in zip(places, lanes, values):
        left.append(jnp.where(grid == place, 1.0, 0.0).astype(jnp.bfloat16))
        hit = lane == at
        high = value.astype(jnp.bfloat16).astype(jnp.float32)
        rest = value - high
        middle = rest.astype(jnp.bfloat16).astype(jnp.float32)
        low = rest - middle
        parts = [jnp.where(hit, part, 0.0).astype(jnp.bfloat16) for part in (high, middle, low)]
        parts.append(jnp.where(hit, 1.0, 0.0).astype(jnp.bfloat16))
        right.append(jnp.concatenate(parts, axis=0))
    out = lax.dot_general(
        jnp.concatenate(left, axis=1), jnp.concatenate(right, axis=1), (((1,), (1,)), ((), ())),
        preferred_element_type=jnp.float32,
    )
    summed = out[:, :LANES] + out[:, LANES : 2 * LANES] + out[:, 2 * LANES : 3 * LANES]
    return summed, out[:, 3 * LANES :]


def backward_kernel(
    gauge_ref, s2_ref, sv_ref, y_ref, pass_ref, u2_ref, v2_ref, kk_ref, wet_ref, yh_ref, u1_ref, v1_ref, t2_ref, t0_ref,
    grad_ref,
    x2p, x2r, pup, pvp, pvr, x1p, x1r, b2s, au1, av1, vs, ms, vt, mt, da, db, dc, dd, *, arrive, leave, shift,
):
    total = s2_ref.shape[0]
    tiles = total // ROWS
    lane, sub = masks(ROWS * STEP)
    dlane = lax.broadcasted_iota(jnp.int32, (tiles, LANES), 1)
    clear_ends(x2p, pup, pvp, x1p, da, db, dc, dd)
    blocks = range(0, tiles, STEP)

    def cut(c, lead=0):
        return slice(lead + ROWS * c, lead + ROWS * (c + STEP))

    x = gauge_ref[...]
    turned = jnp.concatenate([x, pltpu.roll(x, LANES - 4, 1)], axis=0)
    if turned.shape[0] < LANES:
        fill = jnp.full((LANES - turned.shape[0], LANES), -1.0, jnp.float32)
        turned = jnp.concatenate([turned, fill], axis=0)
    turned = jnp.transpose(turned)
    for group in range(3):
        places, lanes, values = [], [], []
        for k in range(4):
            cell = turned[8 * group + k : 8 * group + k + 1, :].astype(jnp.int32)
            value = turned[64 + 8 * group + k : 65 + 8 * group + k, :]
            row, col = cell >> 13, cell & 8191
            tile = col >> 7
            if group == 0:
                place = jnp.where(cell < 0, -1, tile * ROWS + row)
            elif group == 1:
                place = jnp.where((cell < 0) | (row < 5), -1, (7 - row) * tiles + tile)
            else:
                place = jnp.where((cell < 0) | (row > 2), -1, row * tiles + tile)
            places.append(place)
            lanes.append(col & 127)
            values.append(value)
        if group == 0:
            vs[...], ms[...] = gauge_fields(places, lanes, values, total)
        else:
            first = (group - 1) * 3 * tiles
            sums, counts = gauge_fields(places, lanes, values, 3 * tiles)
            vt[first : first + 3 * tiles, :] = sums
            mt[first : first + 3 * tiles, :] = counts
    arrive(1, 2, 3, 4)
    sides = ((-1.0, 0, (da, db)), (1.0, ROWS - 1, (dc, dd)))
    kept = []
    for d, (sigma, edge, scr) in enumerate(sides):
        got = {}
        for i, name in enumerate(PASS):
            first = (d * len(PASS) + i) * tiles
            got[name] = pass_ref[first : first + tiles, :]
        senses = []
        for n in (1, 2, 3):
            first = (d * 3 + n - 1) * tiles
            count, summed = mt[first : first + tiles, :], vt[first : first + tiles, :]
            senses.append((1.0 + count) * got[f"s2_{n}"] - got[f"sv{n}"] - summed)
        y1, h2 = got["y1"], got["h2"]
        x2_1 = jnp.where(y1 > 0.0, senses[0], 0.0)
        x2_2 = jnp.where(h2 > 0.0, senses[1], 0.0)
        x2_3 = jnp.where(got["h3"] > 0.0, senses[2], 0.0)
        x2r[pl.ds(edge, tiles, stride=ROWS), :] = x2_1
        pu_1 = 0.25 * y1 * across_dense(x2_1, scr[0], dlane)
        pv_2 = (0.25 * sigma) * h2 * (x2_3 - x2_1)
        kept.append((senses[0] + across_dense(pu_1, scr[1], dlane) + sigma * pv_2, x2_2, y1, got["w0"]))
    for c in blocks:
        at = cut(c)
        b2 = (1.0 + ms[at, :]) * s2_ref[at, :] - sv_ref[at, :] - vs[at, :]
        b2s[at, :] = b2
        x2p[cut(c, ROWS), :] = jnp.where(y_ref[at, :] > 0.0, b2, 0.0)
    arrive(5, 6, 7, 8, 9, 10, 11, 12)
    for (sigma, edge, scr), (part, x2_2, y1, w0_1) in zip(sides, kept):
        pvr[pl.ds(edge, tiles, stride=ROWS), :] = (0.25 * sigma) * y1 * (x2_2 - row_of(x2p, edge, tiles, ROWS))
    for c in blocks:
        at = cut(c)
        a_u2 = 0.25 * across(x2p, c, STEP, lane)
        a_v2 = 0.25 * along(x2p, x2r, c, STEP, sub)
        energy = a_u2 * u2_ref[at, :] + a_v2 * v2_ref[at, :]
        y, yh, pull = y_ref[at, :], yh_ref[at, :], energy * kk_ref[at, :]
        pup[cut(c, ROWS), :] = yh * a_u2
        pvp[cut(c, ROWS), :] = yh * a_v2
        au1[at, :] = y * a_u2 - pull * u1_ref[at, :]
        av1[at, :] = y * a_v2 - pull * v1_ref[at, :]
        vs[at, :] = energy * t2_ref[at, :]
    for (sigma, edge, scr), (part, x2_2, y1, w0_1) in zip(sides, kept):
        x1r[pl.ds(edge, tiles, stride=ROWS), :] = w0_1 * (part - sigma * row_of(pvp, edge, tiles, ROWS))
    for c in blocks:
        at = cut(c)
        a_s1 = b2s[at, :] + across(pup, c, STEP, lane) + along(pvp, pvr, c, STEP, sub)
        x1p[cut(c, ROWS), :] = wet_ref[at, :].astype(jnp.float32) * a_s1
    arrive(13)
    for c in blocks:
        at = cut(c)
        a_u1 = au1[at, :] + 0.25 * across(x1p, c, STEP, lane)
        a_v1 = av1[at, :] + 0.25 * along(x1p, x1r, c, STEP, sub)
        energy = a_u1 * u1_ref[at, :] + a_v1 * v1_ref[at, :]
        grad_ref[cut((c - shift) % tiles), :] = -(energy * t0_ref[at, :] + vs[at, :])


def turned_order(count, first, stride=1):
    return [(i * stride + first) % count for i in range(count)]


def gauge_table(tile_ref, cell_ref, value_ref, out_ref):
    strips = out_ref.shape[0]
    listed = tile_ref.shape[1]
    strip = (lax.broadcasted_iota(jnp.int32, (strips, listed), 0) * STRIP_STRIDE + STRIP_LEAD) % strips
    tile = tile_ref[...]
    hits = [jnp.where(strip + side == tile, 1.0, 0.0) for side in (0, -1, 1)]
    earlier = lax.broadcasted_iota(jnp.int32, (listed, listed), 0) < lax.broadcasted_iota(jnp.int32, (listed, listed), 1)
    ranks = jnp.dot(
        hits[0].astype(jnp.bfloat16), jnp.where(earlier, 1.0, 0.0).astype(jnp.bfloat16), preferred_element_type=jnp.float32
    )
    rank = jnp.sum(hits[0] * ranks, axis=0, keepdims=True).astype(jnp.int32)
    line = lax.broadcasted_iota(jnp.int32, (LANES, listed), 0)
    rest = jnp.where(line < 64, cell_ref[...].astype(jnp.float32) + 1.0, value_ref[...])
    rest = jnp.where((line & 63) == rank, rest, 0.0)
    hits = jnp.concatenate(hits, axis=0).astype(jnp.bfloat16)
    table = jnp.zeros((3 * strips, LANES), jnp.float32)
    for _ in range(3):
        part = rest.astype(jnp.bfloat16)
        table = table + lax.dot_general(hits, part, (((1,), (1,)), ((), ())), preferred_element_type=jnp.float32)
        rest = rest - part.astype(jnp.float32)
    lane = lax.broadcasted_iota(jnp.int32, (strips, LANES), 1)
    table = [table[i * strips : (i + 1) * strips, :] - jnp.where(lane < 64, 1.0, 0.0) for i in range(3)]
    part = lane & 63
    out_ref[...] = jnp.where(
        part < 8, table[0], jnp.where(part < 16, pltpu.roll(table[1], 8, 1), pltpu.roll(table[2], 16, 1))
    )


def sum_kernel(x_ref, out_ref):
    count, lines = x_ref.shape[0], x_ref.shape[1]
    for k in range(lines // ROWS):
        acc = x_ref[0, ROWS * k : ROWS * (k + 1), :]
        for e in range(1, count):
            acc = acc + x_ref[e, ROWS * k : ROWS * (k + 1), :]
        out_ref[:, LANES * k : LANES * (k + 1)] = acc


def call(body, ins, outs, scratch, name):
    count, given = len(ins), len(outs)
    taken = [pair[2] if len(pair) > 2 else pair[0].shape[0] for pair in ins]
    ins = [pair[:2] for pair in ins]
    moved = [i for i, (_, lead) in enumerate(ins) if lead is not HERE]
    copied = [i for i, (shape, kept) in enumerate(outs) if not kept]

    def kernel(*refs):
        sources, results, rest = refs[:count], refs[count : count + given], refs[count + given :]
        landed, left, own = rest[: len(moved)], rest[len(moved) : len(moved) + len(copied)], rest[len(moved) + len(copied) : -2]
        into, out_of = rest[-2:]
        operands, arrivals = list(sources), {}
        for j, i in enumerate(moved):
            lead, target, source = ins[i][1], landed[j], sources[i]
            operands[i] = target
            if lead:
                target = target.at[pl.ds(lead, taken[i])]
            if taken[i] < source.shape[0]:
                source = source.at[pl.ds(0, taken[i])]
            arrivals[i] = pltpu.make_async_copy(source, target, into.at[j])
            arrivals[i].start()
        places, departures = list(results), {}
        for j, i in enumerate(copied):
            departures[i] = pltpu.make_async_copy(left[j], results[i], out_of.at[j])
            places[i] = left[j]

        def arrive(*which):
            for i in which:
                if i in arrivals:
                    arrivals[i].wait()

        def leave(*which):
            for i in which:
                if i in departures:
                    departures[i].start()

        body(*operands, *places, *own, arrive=arrive, leave=leave)
        for departure in departures.values():
            departure.wait()

    return pl.pallas_call(
        kernel,
        out_shape=[(jax.ShapeDtypeStruct if kept else pltpu.HBM)(shape, jnp.float32) for shape, kept in outs],
        in_specs=[pl.BlockSpec(memory_space=pltpu.VMEM if lead is HERE else pltpu.HBM) for _, lead in ins],
        out_specs=[pl.BlockSpec(memory_space=pltpu.VMEM if kept else pltpu.HBM) for _, kept in outs],
        scratch_shapes=[
            pltpu.VMEM((taken[i] + 2 * ins[i][1], ins[i][0].shape[1]), ins[i][0].dtype) for i in moved
        ]
        + [pltpu.VMEM(outs[i][0], jnp.float32) for i in copied]
        + [pltpu.VMEM(shape, jnp.float32) for shape in scratch]
        + [pltpu.SemaphoreType.DMA((len(moved),)), pltpu.SemaphoreType.DMA((max(1, len(copied)),))],
        name=name,
        compiler_params=pltpu.CompilerParams(vmem_limit_bytes=GRANT),
    )(*(x if lead is HERE else pltpu.with_memory_space_constraint(x, pltpu.HBM) for x, lead in ins))


def tiled(field):
    rows, cols = field.shape[-2:]
    lead = field.shape[:-2]
    parts = field.reshape(-1, rows, cols // LANES, LANES)
    return jnp.transpose(parts, (0, 2, 1, 3)).reshape(-1, LANES)


def shifted(value, axis, steps):
    count = lax.axis_size(axis)
    initial, last = max(0, -steps), min(count, count - steps)
    return lax.ppermute(value, axis, [(i, i + steps) for i in range(initial, last)])


def per_device(s0, u0, v0, depth, rough, wet, gauge_tiles, gauge_cells, gauge_values, survey):
    row_count, col_count = depth.shape
    assert row_count == ROWS and col_count == 8192
    total = row_count * col_count // LANES
    tiles = col_count // LANES
    strips = lax.axis_size("tile")
    events = lax.axis_size("event")
    s0, u0, v0, depth, rough, wet, survey = (tiled(f) for f in (s0[0], u0[0], v0[0], depth, rough, wet[0], survey[0]))
    field, padded, dense = (total, LANES), (total + 2 * ROWS, LANES), (tiles + 2 * ROWS, LANES)
    packet = (len(SENT) * tiles, LANES)
    listed = (1, gauge_cells.shape[1])
    lists = [(x.reshape(listed), 0) for x in (gauge_tiles, gauge_cells, gauge_values)]
    down, up, send, edges, u1, v1i, q1, k, t0, kr = call(
        prepare_kernel,
        lists + [(s0, ROWS)] + [(x, 0) for x in (depth, rough, u0, v0, wet, survey)],
        [(packet, True), (packet, True), ((strips, LANES), False), ((2 * EDGES * tiles, LANES), False)]
        + [(field, False)] * 6,
        [padded] * 5 + [field] * 6,
        "prepare",
    )
    from_above = shifted(down, "tile", 1)
    from_below = shifted(up, "tile", -1)
    gauges = lax.all_to_all(send, "tile", 0, 0, axis_index_groups=[turned_order(strips, STRIP_LEAD, STRIP_STRIDE)], tiled=True)
    v1, s2, u2, v2, y, yh, t2, kk, passed = call(
        forward_kernel,
        [(edges, 0), (from_above, HERE), (from_below, HERE)] + [(x, 0) for x in (v1i, q1, wet, u1, k, depth, kr)],
        [(field, True)] * 6 + [(field, False)] * 2 + [((2 * len(PASS) * tiles, LANES), True)],
        [padded] * 4 + [field] * 3 + [dense] * 6,
        "forward",
    )
    order = turned_order(events, EVENT_LEAD * events // 8)
    (grad,) = call(
        functools.partial(backward_kernel, shift=order[0] * (tiles // events)),
        [(gauges, HERE), (s2, HERE), (survey, 0), (y, HERE), (passed, HERE), (u2, HERE), (v2, HERE), (kk, 0)]
        + [(wet, 0, total), (yh, HERE), (u1, 0), (v1, HERE), (t2, 0), (t0, 0)],
        [(field, True)],
        [padded, field, padded, padded, field, padded, field, field, field, field, field, field]
        + [(6 * tiles, LANES)] * 2 + [dense] * 4,
        "backward",
    )
    parts = lax.all_to_all(grad.reshape(events, total // events, LANES), "event", 0, 0, axis_index_groups=[order], tiled=True)
    return pl.pallas_call(
        sum_kernel, out_shape=jax.ShapeDtypeStruct((ROWS, col_count // events), jnp.float32), name="total",
        compiler_params=pltpu.CompilerParams(vmem_limit_bytes=GRANT),
    )(parts)


def solution(mesh):
    placed = (
        P("event", "tile", None),
        P("event", "tile", None),
        P("event", "tile", None),
        P("tile", None),
        P("tile", None),
        P("event", None, "tile", None),
        P("event", "tile", None),
        P("event", "tile"),
        P("event", "tile"),
        P("event", "tile", None),
    )
    return jax.shard_map(
        per_device, mesh=mesh, in_specs=placed, out_specs=P("tile", "event"), check_vma=False
    )
```

```python
import functools
import jax
import jax.numpy as jnp
from jax import lax
from jax.experimental import pallas as pl
from jax.experimental.pallas import tpu as pltpu
from jax.sharding import PartitionSpec as P

LANES = 128
ROWS = 8
STEP = 4
GRANT = 16 * 1024 * 1024
HERE = None
STRIP_LEAD = 42
STRIP_STRIDE = 1
EVENT_LEAD = 4
RIM1 = ("s0", "v1", "b", "s1", "r", "u1", "k", "sv")
RIM2 = ("s1", "w0", "v2", "h", "s2", "sv")
RIM3 = ("h", "s2", "sv")
SENT = tuple((1, x) for x in RIM1) + tuple((2, x) for x in RIM2) + tuple((3, x) for x in RIM3)
SLOT = {key: i for i, key in enumerate(SENT)}
PASS = ("s2_1", "s2_2", "s2_3", "y1", "w0", "h2", "h3", "sv1", "sv2", "sv3")
EDGES = 3


def masks(rows):
    lane = lax.broadcasted_iota(jnp.int32, (rows, LANES), 1)
    sub = lax.broadcasted_iota(jnp.int32, (rows, LANES), 0) & (ROWS - 1)
    return lane, sub


def across(ref, c, n, lane, lead=ROWS):
    x = ref[lead + ROWS * c : lead + ROWS * (c + n), :]
    left = ref[ROWS * c : ROWS * (c + n), :]
    right = ref[2 * lead + ROWS * c : 2 * lead + ROWS * (c + n), :]
    ahead = pltpu.roll(jnp.where(lane == 0, right, x), LANES - 1, 1)
    behind = pltpu.roll(jnp.where(lane == LANES - 1, left, x), 1, 1)
    return ahead - behind


def along(ref, rim, c, n, sub):
    down = ref[ROWS + 1 + ROWS * c : ROWS + 1 + ROWS * (c + n), :]
    up = ref[ROWS - 1 + ROWS * c : ROWS - 1 + ROWS * (c + n), :]
    edge = 0.0 if rim is None else rim[ROWS * c : ROWS * (c + n), :]
    return jnp.where(sub == ROWS - 1, edge, down) - jnp.where(sub == 0, edge, up)


def across_dense(x, scr, lane):
    tiles = x.shape[0]
    scr[ROWS : ROWS + tiles, :] = x
    right = scr[ROWS + 1 : ROWS + 1 + tiles, :]
    left = scr[ROWS - 1 : ROWS - 1 + tiles, :]
    ahead = pltpu.roll(jnp.where(lane == 0, right, x), LANES - 1, 1)
    behind = pltpu.roll(jnp.where(lane == LANES - 1, left, x), 1, 1)
    return ahead - behind


def clear_ends(*refs):
    zero = jnp.zeros((ROWS, LANES), jnp.float32)
    for ref in refs:
        ref[0:ROWS, :] = zero
        ref[ref.shape[0] - ROWS :, :] = zero


def row_of(ref, row, tiles, lead=0):
    return ref[pl.ds(lead + row, tiles, stride=ROWS), :]


def prepare_kernel(
    tile_ref, cell_ref, value_ref, s0p, h_ref, rough_ref, u0_ref, v0_ref, wet_ref, sv_ref,
    down_ref, up_ref, send_ref, edge_ref, u1_ref, v1_ref, q1_ref, k_ref, t0_ref, kr_ref,
    u1p, v1p, s1p, u2p, v2p, hh, s2p, b_ref, w0q, w1_ref, rr, *, arrive, leave,
):
    total = u1_ref.shape[0]
    tiles = total // ROWS
    lane, sub = masks(ROWS * STEP)
    clear_ends(s0p, u1p, v1p, s1p, u2p, v2p)
    arrive(0, 1, 2)
    gauge_table(tile_ref, cell_ref, value_ref, send_ref)
    leave(2)
    blocks = range(0, tiles, STEP)

    def cut(c, lead=0):
        return slice(lead + ROWS * c, lead + ROWS * (c + STEP))

    arrive(3)
    for c in blocks:
        if c * 2 % tiles == 0:
            arrive(*((2 * c // tiles, i) for i in (4, 5, 6, 7, 8)))
        at = cut(c)
        depth, rough, east, north = h_ref[at, :], rough_ref[at, :], u0_ref[at, :], v0_ref[at, :]
        wet = wet_ref[at, :].astype(jnp.float32)
        kr = 4.0 * rough * jnp.exp((-4.0 / 3.0) * jnp.log(depth))
        k = 0.5 * kr * rough
        square = east * east + north * north + 1.0
        speed = square * lax.rsqrt(square)
        inverse = 1.0 / (1.0 + k * speed)
        y = wet * inverse
        b = 0.2 * depth * y
        u1 = y * east - b * across(s0p, c, STEP, lane)
        v1 = y * north - b * along(s0p, None, c, STEP, sub)
        u1p[cut(c, ROWS), :] = u1
        v1p[cut(c, ROWS), :] = v1
        u1_ref[at, :] = u1
        v1_ref[at, :] = v1
        b_ref[at, :] = b
        k_ref[at, :] = k
        kr_ref[at, :] = kr
        t0_ref[at, :] = kr * speed * inverse
        w0q[at, :] = 0.25 * wet
    for i, (ref, lead) in enumerate(((s0p, ROWS), (v1_ref, 0), (b_ref, 0))):
        for j, row in enumerate((0, ROWS - 1)):
            first = (j * EDGES + i) * tiles
            edge_ref[first : first + tiles, :] = row_of(ref, row, tiles, lead)
    leave(3, 4, 5, 7, 8, 9)
    for c in blocks:
        at = cut(c)
        quarter = w0q[at, :]
        q1 = s0p[cut(c, ROWS), :] - quarter * across(u1p, c, STEP, lane)
        q1_ref[at, :] = q1
        s1p[cut(c, ROWS), :] = q1 - quarter * along(v1p, None, c, STEP, sub)
    leave(6)
    arrive((2, 8), (3, 8))
    for c in blocks:
        at = cut(c)
        wet = wet_ref[cut(c, total), :].astype(jnp.float32)
        east, north = u1_ref[at, :], v1_ref[at, :]
        depth = 0.2 * h_ref[at, :]
        square = east * east + north * north + 1.0
        y = wet / (1.0 + k_ref[at, :] * (square * lax.rsqrt(square)))
        h = depth * y
        hh[at, :] = h
        rr[at, :] = depth * wet
        w1_ref[at, :] = wet
        u2p[cut(c, ROWS), :] = y * east - h * across(s1p, c, STEP, lane)
        v2 = y * north - h * along(s1p, None, c, STEP, sub)
        v2p[cut(c, ROWS), :] = jnp.where((sub == 0) | (sub == ROWS - 1), 0.0, v2)
    for c in blocks:
        at = cut(c)
        change = across(u2p, c, STEP, lane) + along(v2p, None, c, STEP, sub)
        s2p[at, :] = s1p[cut(c, ROWS), :] - 0.25 * w1_ref[at, :] * change
    held = {
        (1, "s0"): (s0p, ROWS), (1, "v1"): (v1_ref, 0), (1, "b"): (b_ref, 0), (1, "s1"): (s1p, ROWS),
        (1, "r"): (rr, 0), (1, "u1"): (u1_ref, 0), (1, "k"): (k_ref, 0), (1, "sv"): (sv_ref, 0),
        (2, "s1"): (s1p, ROWS), (2, "w0"): (w0q, 0), (2, "v2"): (v2p, ROWS), (2, "h"): (hh, 0),
        (2, "s2"): (s2p, 0), (2, "sv"): (sv_ref, 0), (3, "h"): (hh, 0), (3, "s2"): (s2p, 0), (3, "sv"): (sv_ref, 0),
    }
    arrive(9)
    for key, place in SLOT.items():
        ref, lead = held[key]
        down_ref[place * tiles : (place + 1) * tiles, :] = row_of(ref, ROWS - key[0], tiles, lead)
        up_ref[place * tiles : (place + 1) * tiles, :] = row_of(ref, key[0] - 1, tiles, lead)


def forward_kernel(
    edge_ref, top_ref, bot_ref, v1i_ref, q1_ref, wet_ref, u1_ref, k_ref, h_ref, kr_ref,
    v1_ref, s2_ref, u2_ref, v2_ref, y_ref, yh_ref, t2_ref, kk_ref, pass_ref,
    v1p, s1p, u2p, v2p, v1r, s1r, v2r, da, db, dc, dd, de, df, *, arrive, leave,
):
    total = u1_ref.shape[0]
    tiles = total // ROWS
    lane, sub = masks(ROWS * STEP)
    dlane = lax.broadcasted_iota(jnp.int32, (tiles, LANES), 1)
    clear_ends(v1p, s1p, u2p, v2p, da, db, dc, dd, de, df)
    blocks = range(0, tiles, STEP)

    def cut(c, lead=0):
        return slice(lead + ROWS * c, lead + ROWS * (c + STEP))

    sides = ((top_ref, -1.0, 0, (da, db, dc)), (bot_ref, 1.0, ROWS - 1, (dd, de, df)))

    def got(ref, n, name):
        place = SLOT[(n, name)]
        return ref[place * tiles : (place + 1) * tiles, :]

    def own(edge, i):
        first = (EDGES * (edge > 0) + i) * tiles
        return edge_ref[first : first + tiles, :]

    arrive(0, 3)
    v1p[ROWS : ROWS + total, :] = v1i_ref[...]
    kept = []
    for ref, sigma, edge, scr in sides:
        b = got(ref, 1, "b")
        delta = b * own(edge, 0)
        v1_1 = got(ref, 1, "v1") + sigma * delta
        v1_e = own(edge, 1) - sigma * own(edge, 2) * got(ref, 1, "s0")
        v1p[pl.ds(ROWS + edge, tiles, stride=ROWS), :] = v1_e
        v1r[pl.ds(edge, tiles, stride=ROWS), :] = v1_1
        bump = got(ref, 2, "w0") * delta
        s1_2 = got(ref, 2, "s1") + bump
        w0_1 = jnp.where(b > 0.0, 1.0, 0.0)
        s1_1 = got(ref, 1, "s1") + (0.25 * sigma) * w0_1 * v1_e
        s1r[pl.ds(edge, tiles, stride=ROWS), :] = s1_1
        r, u1_1, h2, h3 = got(ref, 1, "r"), got(ref, 1, "u1"), got(ref, 2, "h"), got(ref, 3, "h")
        w1_1 = jnp.where(r > 0.0, 1.0, 0.0)
        inverse = 1.0 / (1.0 + got(ref, 1, "k") * jnp.sqrt(u1_1 * u1_1 + v1_1 * v1_1 + 1.0))
        v2i_2 = got(ref, 2, "v2")
        v2_2 = v2i_2 + 0.25 * w0_1 * h2 * v1_e
        v2_3 = sigma * h3 * bump
        u2_2 = -h2 * across_dense(bump, scr[0], dlane)
        s2_3 = got(ref, 3, "s2") + (0.25 * sigma) * jnp.where(h3 > 0.0, 1.0, 0.0) * (v2_2 - v2i_2)
        u2_1 = (w1_1 * u1_1 - r * across_dense(s1_1, scr[1], dlane)) * inverse
        kept.append((v1_1, s1_1, s1_2, w0_1, w1_1, r, inverse, h2, v2_2, v2_3, u2_1, u2_2, s2_3, bump))
    arrive(4, 5)
    for c in blocks:
        at = cut(c)
        quarter = 0.25 * wet_ref[at, :].astype(jnp.float32)
        v1_ref[at, :] = v1p[cut(c, ROWS), :]
        s1p[cut(c, ROWS), :] = q1_ref[at, :] - quarter * along(v1p, v1r, c, STEP, sub)
    leave(0)
    arrive(6, 7, 8, 9)
    late = []
    for (ref, sigma, edge, scr), values in zip(sides, kept):
        v1_1, s1_1, s1_2, w0_1, w1_1, r, inverse, h2, v2_2, v2_3, u2_1, u2_2, s2_3, bump = values
        s1_e = row_of(s1p, edge, tiles, ROWS)
        v2_1 = (w1_1 * v1_1 - sigma * r * (s1_2 - s1_e)) * inverse
        v2r[pl.ds(edge, tiles, stride=ROWS), :] = v2_1
        w1_2 = jnp.where(h2 > 0.0, 0.25, 0.0)
        s2_2 = got(ref, 2, "s2") + bump - w1_2 * (across_dense(u2_2, scr[2], dlane) + sigma * (v2_3 - v2_1))
        late.append((s2_2, across_dense(u2_1, scr[0], dlane)))
    for c in blocks:
        at = cut(c)
        east, north = u1_ref[at, :], v1_ref[at, :]
        speed2 = east * east + north * north + 1.0
        slow = lax.rsqrt(speed2)
        speed = speed2 * slow
        k = k_ref[at, :]
        inverse = 1.0 / (1.0 + k * speed)
        y = wet_ref[cut(c, total), :].astype(jnp.float32) * inverse
        yh = 0.2 * h_ref[at, :] * y
        u2 = y * east - yh * across(s1p, c, STEP, lane)
        v2 = y * north - yh * along(s1p, s1r, c, STEP, sub)
        u2p[cut(c, ROWS), :] = u2
        v2p[cut(c, ROWS), :] = v2
        u2_ref[at, :] = u2
        v2_ref[at, :] = v2
        y_ref[at, :] = y
        yh_ref[at, :] = yh
        t2_ref[at, :] = kr_ref[at, :] * speed * inverse
        kk_ref[at, :] = k * inverse * slow
    leave(2, 3, 4, 5, 6, 7)
    for c in blocks:
        at = cut(c)
        wet = wet_ref[cut(c, total), :].astype(jnp.float32)
        change = across(u2p, c, STEP, lane) + along(v2p, v2r, c, STEP, sub)
        s2_ref[at, :] = s1p[cut(c, ROWS), :] - 0.25 * wet * change
    leave(1)
    for d, ((ref, sigma, edge, scr), values, more) in enumerate(zip(sides, kept, late)):
        v1_1, s1_1, s1_2, w0_1, w1_1, r, inverse, h2, v2_2, v2_3, u2_1, u2_2, s2_3, bump = values
        s2_2, du2_1 = more
        v2_e = row_of(v2p, edge, tiles, ROWS)
        s2_1 = s1_1 - 0.25 * w1_1 * (du2_1 + sigma * (v2_2 - v2_e))
        surveyed = [got(ref, n, "sv") for n in (1, 2, 3)]
        for i, value in enumerate((s2_1, s2_2, s2_3, r * inverse, w0_1, h2, got(ref, 3, "h"), *surveyed)):
            first = (d * len(PASS) + i) * tiles
            pass_ref[first : first + tiles, :] = value
    leave(8)


def gauge_fields(places, lanes, values, rows):
    grid = lax.broadcasted_iota(jnp.int32, (rows, LANES), 0)
    lane = lax.broadcasted_iota(jnp.int32, (LANES, LANES), 0)
    left, right = [], []
    for place, at, value in zip(places, lanes, values):
        left.append(jnp.where(grid == place, 1.0, 0.0).astype(jnp.bfloat16))
        hit = lane == at
        high = value.astype(jnp.bfloat16).astype(jnp.float32)
        rest = value - high
        middle = rest.astype(jnp.bfloat16).astype(jnp.float32)
        low = rest - middle
        parts = [jnp.where(hit, part, 0.0).astype(jnp.bfloat16) for part in (high, middle, low)]
        parts.append(jnp.where(hit, 1.0, 0.0).astype(jnp.bfloat16))
        right.append(jnp.concatenate(parts, axis=0))
    out = lax.dot_general(
        jnp.concatenate(left, axis=1), jnp.concatenate(right, axis=1), (((1,), (1,)), ((), ())),
        preferred_element_type=jnp.float32,
    )
    summed = out[:, :LANES] + out[:, LANES : 2 * LANES] + out[:, 2 * LANES : 3 * LANES]
    return summed, out[:, 3 * LANES :]


def backward_kernel(
    gauge_ref, s2_ref, sv_ref, y_ref, pass_ref, u2_ref, v2_ref, kk_ref, wet_ref, yh_ref, u1_ref, v1_ref, t2_ref, t0_ref,
    grad_ref,
    x2p, x2r, pup, pvp, pvr, x1p, x1r, b2s, au1, av1, vs, ms, vt, mt, da, db, dc, dd, *, arrive, leave, shift,
):
    total = s2_ref.shape[0]
    tiles = total // ROWS
    lane, sub = masks(ROWS * STEP)
    dlane = lax.broadcasted_iota(jnp.int32, (tiles, LANES), 1)
    clear_ends(x2p, pup, pvp, x1p, da, db, dc, dd)
    blocks = range(0, tiles, STEP)

    def cut(c, lead=0):
        return slice(lead + ROWS * c, lead + ROWS * (c + STEP))

    x = gauge_ref[...]
    turned = jnp.concatenate([x, pltpu.roll(x, LANES - 4, 1)], axis=0)
    if turned.shape[0] < LANES:
        fill = jnp.full((LANES - turned.shape[0], LANES), -1.0, jnp.float32)
        turned = jnp.concatenate([turned, fill], axis=0)
    turned = jnp.transpose(turned)
    for group in range(3):
        places, lanes, values = [], [], []
        for k in range(4):
            cell = turned[8 * group + k : 8 * group + k + 1, :].astype(jnp.int32)
            value = turned[64 + 8 * group + k : 65 + 8 * group + k, :]
            row, col = cell >> 13, cell & 8191
            tile = col >> 7
            if group == 0:
                place = jnp.where(cell < 0, -1, tile * ROWS + row)
            elif group == 1:
                place = jnp.where((cell < 0) | (row < 5), -1, (7 - row) * tiles + tile)
            else:
                place = jnp.where((cell < 0) | (row > 2), -1, row * tiles + tile)
            places.append(place)
            lanes.append(col & 127)
            values.append(value)
        if group == 0:
            vs[...], ms[...] = gauge_fields(places, lanes, values, total)
        else:
            first = (group - 1) * 3 * tiles
            sums, counts = gauge_fields(places, lanes, values, 3 * tiles)
            vt[first : first + 3 * tiles, :] = sums
            mt[first : first + 3 * tiles, :] = counts
    arrive(1, 2, 3, 4)
    sides = ((-1.0, 0, (da, db)), (1.0, ROWS - 1, (dc, dd)))
    kept = []
    for d, (sigma, edge, scr) in enumerate(sides):
        got = {}
        for i, name in enumerate(PASS):
            first = (d * len(PASS) + i) * tiles
            got[name] = pass_ref[first : first + tiles, :]
        senses = []
        for n in (1, 2, 3):
            first = (d * 3 + n - 1) * tiles
            count, summed = mt[first : first + tiles, :], vt[first : first + tiles, :]
            senses.append((1.0 + count) * got[f"s2_{n}"] - got[f"sv{n}"] - summed)
        y1, h2 = got["y1"], got["h2"]
        x2_1 = jnp.where(y1 > 0.0, senses[0], 0.0)
        x2_2 = jnp.where(h2 > 0.0, senses[1], 0.0)
        x2_3 = jnp.where(got["h3"] > 0.0, senses[2], 0.0)
        x2r[pl.ds(edge, tiles, stride=ROWS), :] = x2_1
        pu_1 = 0.25 * y1 * across_dense(x2_1, scr[0], dlane)
        pv_2 = (0.25 * sigma) * h2 * (x2_3 - x2_1)
        kept.append((senses[0] + across_dense(pu_1, scr[1], dlane) + sigma * pv_2, x2_2, y1, got["w0"]))
    for c in blocks:
        at = cut(c)
        b2 = (1.0 + ms[at, :]) * s2_ref[at, :] - sv_ref[at, :] - vs[at, :]
        b2s[at, :] = b2
        x2p[cut(c, ROWS), :] = jnp.where(y_ref[at, :] > 0.0, b2, 0.0)
    arrive(5, 6, 7, 8, 9, 10, 11, 12)
    for (sigma, edge, scr), (part, x2_2, y1, w0_1) in zip(sides, kept):
        pvr[pl.ds(edge, tiles, stride=ROWS), :] = (0.25 * sigma) * y1 * (x2_2 - row_of(x2p, edge, tiles, ROWS))
    for c in blocks:
        at = cut(c)
        a_u2 = 0.25 * across(x2p, c, STEP, lane)
        a_v2 = 0.25 * along(x2p, x2r, c, STEP, sub)
        energy = a_u2 * u2_ref[at, :] + a_v2 * v2_ref[at, :]
        y, yh, pull = y_ref[at, :], yh_ref[at, :], energy * kk_ref[at, :]
        pup[cut(c, ROWS), :] = yh * a_u2
        pvp[cut(c, ROWS), :] = yh * a_v2
        au1[at, :] = y * a_u2 - pull * u1_ref[at, :]
        av1[at, :] = y * a_v2 - pull * v1_ref[at, :]
        vs[at, :] = energy * t2_ref[at, :]
    for (sigma, edge, scr), (part, x2_2, y1, w0_1) in zip(sides, kept):
        x1r[pl.ds(edge, tiles, stride=ROWS), :] = w0_1 * (part - sigma * row_of(pvp, edge, tiles, ROWS))
    for c in blocks:
        at = cut(c)
        a_s1 = b2s[at, :] + across(pup, c, STEP, lane) + along(pvp, pvr, c, STEP, sub)
        x1p[cut(c, ROWS), :] = wet_ref[at, :].astype(jnp.float32) * a_s1
    arrive(13)
    for c in blocks:
        at = cut(c)
        a_u1 = au1[at, :] + 0.25 * across(x1p, c, STEP, lane)
        a_v1 = av1[at, :] + 0.25 * along(x1p, x1r, c, STEP, sub)
        energy = a_u1 * u1_ref[at, :] + a_v1 * v1_ref[at, :]
        grad_ref[cut((c - shift) % tiles), :] = -(energy * t0_ref[at, :] + vs[at, :])


def turned_order(count, first, stride=1):
    return [(i * stride + first) % count for i in range(count)]


def gauge_table(tile_ref, cell_ref, value_ref, out_ref):
    strips = out_ref.shape[0]
    listed = tile_ref.shape[1]
    strip = (lax.broadcasted_iota(jnp.int32, (strips, listed), 0) * STRIP_STRIDE + STRIP_LEAD) % strips
    tile = tile_ref[...]
    hits = [jnp.where(strip + side == tile, 1.0, 0.0) for side in (0, -1, 1)]
    earlier = lax.broadcasted_iota(jnp.int32, (listed, listed), 0) < lax.broadcasted_iota(jnp.int32, (listed, listed), 1)
    ranks = jnp.dot(
        hits[0].astype(jnp.bfloat16), jnp.where(earlier, 1.0, 0.0).astype(jnp.bfloat16), preferred_element_type=jnp.float32
    )
    rank = jnp.sum(hits[0] * ranks, axis=0, keepdims=True).astype(jnp.int32)
    line = lax.broadcasted_iota(jnp.int32, (LANES, listed), 0)
    rest = jnp.where(line < 64, cell_ref[...].astype(jnp.float32) + 1.0, value_ref[...])
    rest = jnp.where((line & 63) == rank, rest, 0.0)
    hits = jnp.concatenate(hits, axis=0).astype(jnp.bfloat16)
    table = jnp.zeros((3 * strips, LANES), jnp.float32)
    for _ in range(3):
        part = rest.astype(jnp.bfloat16)
        table = table + lax.dot_general(hits, part, (((1,), (1,)), ((), ())), preferred_element_type=jnp.float32)
        rest = rest - part.astype(jnp.float32)
    lane = lax.broadcasted_iota(jnp.int32, (strips, LANES), 1)
    table = [table[i * strips : (i + 1) * strips, :] - jnp.where(lane < 64, 1.0, 0.0) for i in range(3)]
    part = lane & 63
    out_ref[...] = jnp.where(
        part < 8, table[0], jnp.where(part < 16, pltpu.roll(table[1], 8, 1), pltpu.roll(table[2], 16, 1))
    )


def sum_kernel(x_ref, out_ref):
    count, lines = x_ref.shape[0], x_ref.shape[1]
    for k in range(lines // ROWS):
        acc = x_ref[0, ROWS * k : ROWS * (k + 1), :]
        for e in range(1, count):
            acc = acc + x_ref[e, ROWS * k : ROWS * (k + 1), :]
        out_ref[:, LANES * k : LANES * (k + 1)] = acc


def call(body, ins, outs, scratch, name):
    count, given = len(ins), len(outs)
    taken = [pair[2] if len(pair) > 2 else pair[0].shape[0] for pair in ins]
    pieces = [pair[3] if len(pair) > 3 else 1 for pair in ins]
    ins = [pair[:2] for pair in ins]
    moved = [i for i, (_, lead) in enumerate(ins) if lead is not HERE]
    copied = [i for i, (shape, kept) in enumerate(outs) if not kept]

    def kernel(*refs):
        sources, results, rest = refs[:count], refs[count : count + given], refs[count + given :]
        landed, left, own = rest[: len(moved)], rest[len(moved) : len(moved) + len(copied)], rest[len(moved) + len(copied) : -2]
        into, out_of = rest[-2:]
        operands, arrivals = list(sources), {}
        for j, i in enumerate(moved):
            operands[i] = landed[j]
            size = taken[i] // pieces[i]
            for part in range(pieces[i]):
                place = ins[i][1] + part * size
                target, source = landed[j], sources[i]
                if size < target.shape[0]:
                    target = target.at[pl.ds(place, size)]
                if size < source.shape[0]:
                    source = source.at[pl.ds(part * size, size)]
                arrivals[part, i] = pltpu.make_async_copy(source, target, into.at[len(arrivals)])
        for key in sorted(arrivals):
            arrivals[key].start()
        places, departures = list(results), {}
        for j, i in enumerate(copied):
            departures[i] = pltpu.make_async_copy(left[j], results[i], out_of.at[j])
            places[i] = left[j]

        def arrive(*which):
            for i in which:
                for part in range(pieces[i]) if isinstance(i, int) else ():
                    if (part, i) in arrivals:
                        arrivals[part, i].wait()
                if not isinstance(i, int):
                    arrivals[i].wait()

        def leave(*which):
            for i in which:
                if i in departures:
                    departures[i].start()

        body(*operands, *places, *own, arrive=arrive, leave=leave)
        for departure in departures.values():
            departure.wait()

    return pl.pallas_call(
        kernel,
        out_shape=[(jax.ShapeDtypeStruct if kept else pltpu.HBM)(shape, jnp.float32) for shape, kept in outs],
        in_specs=[pl.BlockSpec(memory_space=pltpu.VMEM if lead is HERE else pltpu.HBM) for _, lead in ins],
        out_specs=[pl.BlockSpec(memory_space=pltpu.VMEM if kept else pltpu.HBM) for _, kept in outs],
        scratch_shapes=[
            pltpu.VMEM((taken[i] + 2 * ins[i][1], ins[i][0].shape[1]), ins[i][0].dtype) for i in moved
        ]
        + [pltpu.VMEM(outs[i][0], jnp.float32) for i in copied]
        + [pltpu.VMEM(shape, jnp.float32) for shape in scratch]
        + [pltpu.SemaphoreType.DMA((sum(pieces[i] for i in moved),)), pltpu.SemaphoreType.DMA((max(1, len(copied)),))],
        name=name,
        compiler_params=pltpu.CompilerParams(vmem_limit_bytes=GRANT),
    )(*(x if lead is HERE else pltpu.with_memory_space_constraint(x, pltpu.HBM) for x, lead in ins))


def tiled(field):
    rows, cols = field.shape[-2:]
    lead = field.shape[:-2]
    parts = field.reshape(-1, rows, cols // LANES, LANES)
    return jnp.transpose(parts, (0, 2, 1, 3)).reshape(-1, LANES)


def shifted(value, axis, steps):
    count = lax.axis_size(axis)
    initial, last = max(0, -steps), min(count, count - steps)
    return lax.ppermute(value, axis, [(i, i + steps) for i in range(initial, last)])


def per_device(s0, u0, v0, depth, rough, wet, gauge_tiles, gauge_cells, gauge_values, survey):
    row_count, col_count = depth.shape
    assert row_count == ROWS and col_count == 8192
    total = row_count * col_count // LANES
    tiles = col_count // LANES
    strips = lax.axis_size("tile")
    events = lax.axis_size("event")
    s0, u0, v0, depth, rough, wet, survey = (tiled(f) for f in (s0[0], u0[0], v0[0], depth, rough, wet[0], survey[0]))
    field, padded, dense = (total, LANES), (total + 2 * ROWS, LANES), (tiles + 2 * ROWS, LANES)
    packet = (len(SENT) * tiles, LANES)
    listed = (1, gauge_cells.shape[1])
    lists = [(x.reshape(listed), 0) for x in (gauge_tiles, gauge_cells, gauge_values)]
    down, up, send, edges, u1, v1i, q1, k, t0, kr = call(
        prepare_kernel,
        lists + [(s0, ROWS)] + [(x, 0, total, 2) for x in (depth, rough, u0, v0)] + [(wet, 0, 2 * total, 4), (survey, 0)],
        [(packet, True), (packet, True), ((strips, LANES), False), ((2 * EDGES * tiles, LANES), False)]
        + [(field, False)] * 6,
        [padded] * 5 + [field] * 6,
        "prepare",
    )
    from_above = shifted(down, "tile", 1)
    from_below = shifted(up, "tile", -1)
    gauges = lax.all_to_all(send, "tile", 0, 0, axis_index_groups=[turned_order(strips, STRIP_LEAD, STRIP_STRIDE)], tiled=True)
    v1, s2, u2, v2, y, yh, t2, kk, passed = call(
        forward_kernel,
        [(edges, 0), (from_above, HERE), (from_below, HERE)] + [(x, 0) for x in (v1i, q1, wet, u1, k, depth, kr)],
        [(field, True)] * 6 + [(field, False)] * 2 + [((2 * len(PASS) * tiles, LANES), True)],
        [padded] * 4 + [field] * 3 + [dense] * 6,
        "forward",
    )
    order = turned_order(events, EVENT_LEAD * events // 8)
    (grad,) = call(
        functools.partial(backward_kernel, shift=order[0] * (tiles // events)),
        [(gauges, HERE), (s2, HERE), (survey, 0), (y, HERE), (passed, HERE), (u2, HERE), (v2, HERE), (kk, 0)]
        + [(wet, 0, total), (yh, HERE), (u1, 0), (v1, HERE), (t2, 0), (t0, 0)],
        [(field, True)],
        [padded, field, padded, padded, field, padded, field, field, field, field, field, field]
        + [(6 * tiles, LANES)] * 2 + [dense] * 4,
        "backward",
    )
    parts = lax.all_to_all(grad.reshape(events, total // events, LANES), "event", 0, 0, axis_index_groups=[order], tiled=True)
    return pl.pallas_call(
        sum_kernel, out_shape=jax.ShapeDtypeStruct((ROWS, col_count // events), jnp.float32), name="total",
        compiler_params=pltpu.CompilerParams(vmem_limit_bytes=GRANT),
    )(parts)


def solution(mesh):
    placed = (
        P("event", "tile", None),
        P("event", "tile", None),
        P("event", "tile", None),
        P("tile", None),
        P("tile", None),
        P("event", None, "tile", None),
        P("event", "tile", None),
        P("event", "tile"),
        P("event", "tile"),
        P("event", "tile", None),
    )
    return jax.shard_map(
        per_device, mesh=mesh, in_specs=placed, out_specs=P("tile", "event"), check_vma=False
    )
```

```python
import functools
import jax
import jax.numpy as jnp
from jax import lax
from jax.experimental import pallas as pl
from jax.experimental.pallas import tpu as pltpu
from jax.sharding import PartitionSpec as P

LANES = 128
ROWS = 8
STEP = 4
GRANT = 16 * 1024 * 1024
HERE = None
STRIP_LEAD = 42
STRIP_STRIDE = 1
EVENT_LEAD = 4
RIM1 = ("s0", "v1", "b", "s1", "r", "u1", "k", "sv")
RIM2 = ("s1", "w0", "v2", "h", "s2", "sv")
RIM3 = ("h", "s2", "sv")
SENT = tuple((1, x) for x in RIM1) + tuple((2, x) for x in RIM2) + tuple((3, x) for x in RIM3)
SLOT = {key: i for i, key in enumerate(SENT)}
PASS = ("s2_1", "s2_2", "s2_3", "y1", "w0", "h2", "h3", "sv1", "sv2", "sv3")
EDGES = 3


def masks(rows):
    lane = lax.broadcasted_iota(jnp.int32, (rows, LANES), 1)
    sub = lax.broadcasted_iota(jnp.int32, (rows, LANES), 0) & (ROWS - 1)
    return lane, sub


def across(ref, c, n, lane, lead=ROWS):
    x = ref[lead + ROWS * c : lead + ROWS * (c + n), :]
    left = ref[ROWS * c : ROWS * (c + n), :]
    right = ref[2 * lead + ROWS * c : 2 * lead + ROWS * (c + n), :]
    ahead = pltpu.roll(jnp.where(lane == 0, right, x), LANES - 1, 1)
    behind = pltpu.roll(jnp.where(lane == LANES - 1, left, x), 1, 1)
    return ahead - behind


def along(ref, rim, c, n, sub):
    down = ref[ROWS + 1 + ROWS * c : ROWS + 1 + ROWS * (c + n), :]
    up = ref[ROWS - 1 + ROWS * c : ROWS - 1 + ROWS * (c + n), :]
    edge = 0.0 if rim is None else rim[ROWS * c : ROWS * (c + n), :]
    return jnp.where(sub == ROWS - 1, edge, down) - jnp.where(sub == 0, edge, up)


def across_dense(x, scr, lane):
    tiles = x.shape[0]
    scr[ROWS : ROWS + tiles, :] = x
    right = scr[ROWS + 1 : ROWS + 1 + tiles, :]
    left = scr[ROWS - 1 : ROWS - 1 + tiles, :]
    ahead = pltpu.roll(jnp.where(lane == 0, right, x), LANES - 1, 1)
    behind = pltpu.roll(jnp.where(lane == LANES - 1, left, x), 1, 1)
    return ahead - behind


def clear_ends(*refs):
    zero = jnp.zeros((ROWS, LANES), jnp.float32)
    for ref in refs:
        ref[0:ROWS, :] = zero
        ref[ref.shape[0] - ROWS :, :] = zero


def row_of(ref, row, tiles, lead=0):
    return ref[pl.ds(lead + row, tiles, stride=ROWS), :]


def prepare_kernel(
    tile_ref, cell_ref, value_ref, s0p, h_ref, rough_ref, u0_ref, v0_ref, wet_ref, sv_ref,
    down_ref, up_ref, send_ref, edge_ref, u1_ref, v1_ref, t0_ref,
    k_ref, u1p, v1p, s1p, u2p, v2p, hh, s2p, b_ref, w0q, w1_ref, rr, *, arrive, leave,
):
    total = u1_ref.shape[0]
    tiles = total // ROWS
    lane, sub = masks(ROWS * STEP)
    clear_ends(s0p, u1p, v1p, s1p, u2p, v2p)
    arrive(0, 1, 2)
    gauge_table(tile_ref, cell_ref, value_ref, send_ref)
    leave(2)
    blocks = range(0, tiles, STEP)

    def cut(c, lead=0):
        return slice(lead + ROWS * c, lead + ROWS * (c + STEP))

    arrive(3)
    for c in blocks:
        if c * 2 == tiles:
            leave((0, 4), (0, 5), (0, 6))
        if c * 2 % tiles == 0:
            arrive(*((2 * c // tiles, i) for i in (4, 5, 6, 7, 8)))
        at = cut(c)
        depth, rough, east, north = h_ref[at, :], rough_ref[at, :], u0_ref[at, :], v0_ref[at, :]
        wet = wet_ref[at, :].astype(jnp.float32)
        kr = 4.0 * rough * jnp.exp((-4.0 / 3.0) * jnp.log(depth))
        k = 0.5 * kr * rough
        square = east * east + north * north + 1.0
        speed = square * lax.rsqrt(square)
        inverse = 1.0 / (1.0 + k * speed)
        y = wet * inverse
        b = 0.2 * depth * y
        u1 = y * east - b * across(s0p, c, STEP, lane)
        v1 = y * north - b * along(s0p, None, c, STEP, sub)
        u1p[cut(c, ROWS), :] = u1
        v1p[cut(c, ROWS), :] = v1
        u1_ref[at, :] = u1
        v1_ref[at, :] = v1
        b_ref[at, :] = b
        k_ref[at, :] = k
        t0_ref[at, :] = kr * speed * inverse
        w0q[at, :] = 0.25 * wet
    for i, (ref, lead) in enumerate(((s0p, ROWS), (v1_ref, 0), (b_ref, 0))):
        for j, row in enumerate((0, ROWS - 1)):
            first = (j * EDGES + i) * tiles
            edge_ref[first : first + tiles, :] = row_of(ref, row, tiles, lead)
    leave((1, 4), (1, 5), (1, 6), 3)
    for c in blocks:
        at = cut(c)
        quarter = w0q[at, :]
        q1 = s0p[cut(c, ROWS), :] - quarter * across(u1p, c, STEP, lane)
        s1p[cut(c, ROWS), :] = q1 - quarter * along(v1p, None, c, STEP, sub)
    arrive((2, 8), (3, 8))
    for c in blocks:
        at = cut(c)
        wet = wet_ref[cut(c, total), :].astype(jnp.float32)
        east, north = u1_ref[at, :], v1_ref[at, :]
        depth = 0.2 * h_ref[at, :]
        square = east * east + north * north + 1.0
        y = wet / (1.0 + k_ref[at, :] * (square * lax.rsqrt(square)))
        h = depth * y
        hh[at, :] = h
        rr[at, :] = depth * wet
        w1_ref[at, :] = wet
        u2p[cut(c, ROWS), :] = y * east - h * across(s1p, c, STEP, lane)
        v2 = y * north - h * along(s1p, None, c, STEP, sub)
        v2p[cut(c, ROWS), :] = jnp.where((sub == 0) | (sub == ROWS - 1), 0.0, v2)
    for c in blocks:
        at = cut(c)
        change = across(u2p, c, STEP, lane) + along(v2p, None, c, STEP, sub)
        s2p[at, :] = s1p[cut(c, ROWS), :] - 0.25 * w1_ref[at, :] * change
    held = {
        (1, "s0"): (s0p, ROWS), (1, "v1"): (v1_ref, 0), (1, "b"): (b_ref, 0), (1, "s1"): (s1p, ROWS),
        (1, "r"): (rr, 0), (1, "u1"): (u1_ref, 0), (1, "k"): (k_ref, 0), (1, "sv"): (sv_ref, 0),
        (2, "s1"): (s1p, ROWS), (2, "w0"): (w0q, 0), (2, "v2"): (v2p, ROWS), (2, "h"): (hh, 0),
        (2, "s2"): (s2p, 0), (2, "sv"): (sv_ref, 0), (3, "h"): (hh, 0), (3, "s2"): (s2p, 0), (3, "sv"): (sv_ref, 0),
    }
    arrive(9)
    for key, place in SLOT.items():
        ref, lead = held[key]
        down_ref[place * tiles : (place + 1) * tiles, :] = row_of(ref, ROWS - key[0], tiles, lead)
        up_ref[place * tiles : (place + 1) * tiles, :] = row_of(ref, key[0] - 1, tiles, lead)


def forward_kernel(
    edge_ref, top_ref, bot_ref, v1i_ref, s0_ref, wet_ref, u1p, h_ref, rough_ref,
    v1_ref, s2_ref, u2_ref, v2_ref, y_ref, yh_ref, t2_ref, kk_ref, pass_ref,
    v1p, s1p, u2p, v2p, v1r, s1r, v2r, da, db, dc, dd, de, df, *, arrive, leave,
):
    total = v1i_ref.shape[0]
    tiles = total // ROWS
    lane, sub = masks(ROWS * STEP)
    dlane = lax.broadcasted_iota(jnp.int32, (tiles, LANES), 1)
    clear_ends(u1p, v1p, s1p, u2p, v2p, da, db, dc, dd, de, df)
    blocks = range(0, tiles, STEP)

    def cut(c, lead=0):
        return slice(lead + ROWS * c, lead + ROWS * (c + STEP))

    sides = ((top_ref, -1.0, 0, (da, db, dc)), (bot_ref, 1.0, ROWS - 1, (dd, de, df)))

    def got(ref, n, name):
        place = SLOT[(n, name)]
        return ref[place * tiles : (place + 1) * tiles, :]

    def own(edge, i):
        first = (EDGES * (edge > 0) + i) * tiles
        return edge_ref[first : first + tiles, :]

    arrive(0, 3)
    v1p[ROWS : ROWS + total, :] = v1i_ref[...]
    kept = []
    for ref, sigma, edge, scr in sides:
        b = got(ref, 1, "b")
        delta = b * own(edge, 0)
        v1_1 = got(ref, 1, "v1") + sigma * delta
        v1_e = own(edge, 1) - sigma * own(edge, 2) * got(ref, 1, "s0")
        v1p[pl.ds(ROWS + edge, tiles, stride=ROWS), :] = v1_e
        v1r[pl.ds(edge, tiles, stride=ROWS), :] = v1_1
        bump = got(ref, 2, "w0") * delta
        s1_2 = got(ref, 2, "s1") + bump
        w0_1 = jnp.where(b > 0.0, 1.0, 0.0)
        s1_1 = got(ref, 1, "s1") + (0.25 * sigma) * w0_1 * v1_e
        s1r[pl.ds(edge, tiles, stride=ROWS), :] = s1_1
        r, u1_1, h2, h3 = got(ref, 1, "r"), got(ref, 1, "u1"), got(ref, 2, "h"), got(ref, 3, "h")
        w1_1 = jnp.where(r > 0.0, 1.0, 0.0)
        inverse = 1.0 / (1.0 + got(ref, 1, "k") * jnp.sqrt(u1_1 * u1_1 + v1_1 * v1_1 + 1.0))
        v2i_2 = got(ref, 2, "v2")
        v2_2 = v2i_2 + 0.25 * w0_1 * h2 * v1_e
        v2_3 = sigma * h3 * bump
        u2_2 = -h2 * across_dense(bump, scr[0], dlane)
        s2_3 = got(ref, 3, "s2") + (0.25 * sigma) * jnp.where(h3 > 0.0, 1.0, 0.0) * (v2_2 - v2i_2)
        u2_1 = (w1_1 * u1_1 - r * across_dense(s1_1, scr[1], dlane)) * inverse
        kept.append((v1_1, s1_1, s1_2, w0_1, w1_1, r, inverse, h2, v2_2, v2_3, u2_1, u2_2, s2_3, bump))
    arrive(4, 5, 6)
    for c in blocks:
        at = cut(c)
        quarter = 0.25 * wet_ref[at, :].astype(jnp.float32)
        v1_ref[at, :] = v1p[cut(c, ROWS), :]
        change = across(u1p, c, STEP, lane) + along(v1p, v1r, c, STEP, sub)
        s1p[cut(c, ROWS), :] = s0_ref[at, :] - quarter * change
    leave(0)
    arrive(7, 8)
    late = []
    for (ref, sigma, edge, scr), values in zip(sides, kept):
        v1_1, s1_1, s1_2, w0_1, w1_1, r, inverse, h2, v2_2, v2_3, u2_1, u2_2, s2_3, bump = values
        s1_e = row_of(s1p, edge, tiles, ROWS)
        v2_1 = (w1_1 * v1_1 - sigma * r * (s1_2 - s1_e)) * inverse
        v2r[pl.ds(edge, tiles, stride=ROWS), :] = v2_1
        w1_2 = jnp.where(h2 > 0.0, 0.25, 0.0)
        s2_2 = got(ref, 2, "s2") + bump - w1_2 * (across_dense(u2_2, scr[2], dlane) + sigma * (v2_3 - v2_1))
        late.append((s2_2, across_dense(u2_1, scr[0], dlane)))
    for c in blocks:
        at = cut(c)
        east, north = u1p[cut(c, ROWS), :], v1_ref[at, :]
        speed2 = east * east + north * north + 1.0
        slow = lax.rsqrt(speed2)
        speed = speed2 * slow
        depth, rough = h_ref[at, :], rough_ref[at, :]
        kr = 4.0 * rough * jnp.exp((-4.0 / 3.0) * jnp.log(depth))
        k = 0.5 * kr * rough
        inverse = 1.0 / (1.0 + k * speed)
        y = wet_ref[cut(c, total), :].astype(jnp.float32) * inverse
        yh = 0.2 * depth * y
        u2 = y * east - yh * across(s1p, c, STEP, lane)
        v2 = y * north - yh * along(s1p, s1r, c, STEP, sub)
        u2p[cut(c, ROWS), :] = u2
        v2p[cut(c, ROWS), :] = v2
        u2_ref[at, :] = u2
        v2_ref[at, :] = v2
        y_ref[at, :] = y
        yh_ref[at, :] = yh
        t2_ref[at, :] = kr * speed * inverse
        kk_ref[at, :] = k * inverse * slow
    leave(2, 3, 4, 5, 6, 7)
    for c in blocks:
        at = cut(c)
        wet = wet_ref[cut(c, total), :].astype(jnp.float32)
        change = across(u2p, c, STEP, lane) + along(v2p, v2r, c, STEP, sub)
        s2_ref[at, :] = s1p[cut(c, ROWS), :] - 0.25 * wet * change
    leave(1)
    for d, ((ref, sigma, edge, scr), values, more) in enumerate(zip(sides, kept, late)):
        v1_1, s1_1, s1_2, w0_1, w1_1, r, inverse, h2, v2_2, v2_3, u2_1, u2_2, s2_3, bump = values
        s2_2, du2_1 = more
        v2_e = row_of(v2p, edge, tiles, ROWS)
        s2_1 = s1_1 - 0.25 * w1_1 * (du2_1 + sigma * (v2_2 - v2_e))
        surveyed = [got(ref, n, "sv") for n in (1, 2, 3)]
        for i, value in enumerate((s2_1, s2_2, s2_3, r * inverse, w0_1, h2, got(ref, 3, "h"), *surveyed)):
            first = (d * len(PASS) + i) * tiles
            pass_ref[first : first + tiles, :] = value
    leave(8)


def gauge_fields(places, lanes, values, rows):
    grid = lax.broadcasted_iota(jnp.int32, (rows, LANES), 0)
    lane = lax.broadcasted_iota(jnp.int32, (LANES, LANES), 0)
    left, right = [], []
    for place, at, value in zip(places, lanes, values):
        left.append(jnp.where(grid == place, 1.0, 0.0).astype(jnp.bfloat16))
        hit = lane == at
        high = value.astype(jnp.bfloat16).astype(jnp.float32)
        rest = value - high
        middle = rest.astype(jnp.bfloat16).astype(jnp.float32)
        low = rest - middle
        parts = [jnp.where(hit, part, 0.0).astype(jnp.bfloat16) for part in (high, middle, low)]
        parts.append(jnp.where(hit, 1.0, 0.0).astype(jnp.bfloat16))
        right.append(jnp.concatenate(parts, axis=0))
    out = lax.dot_general(
        jnp.concatenate(left, axis=1), jnp.concatenate(right, axis=1), (((1,), (1,)), ((), ())),
        preferred_element_type=jnp.float32,
    )
    summed = out[:, :LANES] + out[:, LANES : 2 * LANES] + out[:, 2 * LANES : 3 * LANES]
    return summed, out[:, 3 * LANES :]


def backward_kernel(
    gauge_ref, s2_ref, sv_ref, y_ref, pass_ref, u2_ref, v2_ref, kk_ref, wet_ref, yh_ref, u1_ref, v1_ref, t2_ref, t0_ref,
    grad_ref,
    x2p, x2r, pup, pvp, pvr, x1p, x1r, b2s, au1, av1, vs, ms, vt, mt, da, db, dc, dd, *, arrive, leave, shift,
):
    total = s2_ref.shape[0]
    tiles = total // ROWS
    lane, sub = masks(ROWS * STEP)
    dlane = lax.broadcasted_iota(jnp.int32, (tiles, LANES), 1)
    clear_ends(x2p, pup, pvp, x1p, da, db, dc, dd)
    blocks = range(0, tiles, STEP)

    def cut(c, lead=0):
        return slice(lead + ROWS * c, lead + ROWS * (c + STEP))

    x = gauge_ref[...]
    turned = jnp.concatenate([x, pltpu.roll(x, LANES - 4, 1)], axis=0)
    if turned.shape[0] < LANES:
        fill = jnp.full((LANES - turned.shape[0], LANES), -1.0, jnp.float32)
        turned = jnp.concatenate([turned, fill], axis=0)
    turned = jnp.transpose(turned)
    for group in range(3):
        places, lanes, values = [], [], []
        for k in range(4):
            cell = turned[8 * group + k : 8 * group + k + 1, :].astype(jnp.int32)
            value = turned[64 + 8 * group + k : 65 + 8 * group + k, :]
            row, col = cell >> 13, cell & 8191
            tile = col >> 7
            if group == 0:
                place = jnp.where(cell < 0, -1, tile * ROWS + row)
            elif group == 1:
                place = jnp.where((cell < 0) | (row < 5), -1, (7 - row) * tiles + tile)
            else:
                place = jnp.where((cell < 0) | (row > 2), -1, row * tiles + tile)
            places.append(place)
            lanes.append(col & 127)
            values.append(value)
        if group == 0:
            vs[...], ms[...] = gauge_fields(places, lanes, values, total)
        else:
            first = (group - 1) * 3 * tiles
            sums, counts = gauge_fields(places, lanes, values, 3 * tiles)
            vt[first : first + 3 * tiles, :] = sums
            mt[first : first + 3 * tiles, :] = counts
    arrive(1, 2, 3, 4)
    sides = ((-1.0, 0, (da, db)), (1.0, ROWS - 1, (dc, dd)))
    kept = []
    for d, (sigma, edge, scr) in enumerate(sides):
        got = {}
        for i, name in enumerate(PASS):
            first = (d * len(PASS) + i) * tiles
            got[name] = pass_ref[first : first + tiles, :]
        senses = []
        for n in (1, 2, 3):
            first = (d * 3 + n - 1) * tiles
            count, summed = mt[first : first + tiles, :], vt[first : first + tiles, :]
            senses.append((1.0 + count) * got[f"s2_{n}"] - got[f"sv{n}"] - summed)
        y1, h2 = got["y1"], got["h2"]
        x2_1 = jnp.where(y1 > 0.0, senses[0], 0.0)
        x2_2 = jnp.where(h2 > 0.0, senses[1], 0.0)
        x2_3 = jnp.where(got["h3"] > 0.0, senses[2], 0.0)
        x2r[pl.ds(edge, tiles, stride=ROWS), :] = x2_1
        pu_1 = 0.25 * y1 * across_dense(x2_1, scr[0], dlane)
        pv_2 = (0.25 * sigma) * h2 * (x2_3 - x2_1)
        kept.append((senses[0] + across_dense(pu_1, scr[1], dlane) + sigma * pv_2, x2_2, y1, got["w0"]))
    for c in blocks:
        at = cut(c)
        b2 = (1.0 + ms[at, :]) * s2_ref[at, :] - sv_ref[at, :] - vs[at, :]
        b2s[at, :] = b2
        x2p[cut(c, ROWS), :] = jnp.where(y_ref[at, :] > 0.0, b2, 0.0)
    arrive(5, 6, 7, 8, 9, 10, 11, 12)
    for (sigma, edge, scr), (part, x2_2, y1, w0_1) in zip(sides, kept):
        pvr[pl.ds(edge, tiles, stride=ROWS), :] = (0.25 * sigma) * y1 * (x2_2 - row_of(x2p, edge, tiles, ROWS))
    for c in blocks:
        at = cut(c)
        a_u2 = 0.25 * across(x2p, c, STEP, lane)
        a_v2 = 0.25 * along(x2p, x2r, c, STEP, sub)
        energy = a_u2 * u2_ref[at, :] + a_v2 * v2_ref[at, :]
        y, yh, pull = y_ref[at, :], yh_ref[at, :], energy * kk_ref[at, :]
        pup[cut(c, ROWS), :] = yh * a_u2
        pvp[cut(c, ROWS), :] = yh * a_v2
        au1[at, :] = y * a_u2 - pull * u1_ref[at, :]
        av1[at, :] = y * a_v2 - pull * v1_ref[at, :]
        vs[at, :] = energy * t2_ref[at, :]
    for (sigma, edge, scr), (part, x2_2, y1, w0_1) in zip(sides, kept):
        x1r[pl.ds(edge, tiles, stride=ROWS), :] = w0_1 * (part - sigma * row_of(pvp, edge, tiles, ROWS))
    for c in blocks:
        at = cut(c)
        a_s1 = b2s[at, :] + across(pup, c, STEP, lane) + along(pvp, pvr, c, STEP, sub)
        x1p[cut(c, ROWS), :] = wet_ref[at, :].astype(jnp.float32) * a_s1
    arrive(13)
    for c in blocks:
        at = cut(c)
        a_u1 = au1[at, :] + 0.25 * across(x1p, c, STEP, lane)
        a_v1 = av1[at, :] + 0.25 * along(x1p, x1r, c, STEP, sub)
        energy = a_u1 * u1_ref[at, :] + a_v1 * v1_ref[at, :]
        grad_ref[cut((c - shift) % tiles), :] = -(energy * t0_ref[at, :] + vs[at, :])


def turned_order(count, first, stride=1):
    return [(i * stride + first) % count for i in range(count)]


def gauge_table(tile_ref, cell_ref, value_ref, out_ref):
    strips = out_ref.shape[0]
    listed = tile_ref.shape[1]
    strip = (lax.broadcasted_iota(jnp.int32, (strips, listed), 0) * STRIP_STRIDE + STRIP_LEAD) % strips
    tile = tile_ref[...]
    hits = [jnp.where(strip + side == tile, 1.0, 0.0) for side in (0, -1, 1)]
    earlier = lax.broadcasted_iota(jnp.int32, (listed, listed), 0) < lax.broadcasted_iota(jnp.int32, (listed, listed), 1)
    ranks = jnp.dot(
        hits[0].astype(jnp.bfloat16), jnp.where(earlier, 1.0, 0.0).astype(jnp.bfloat16), preferred_element_type=jnp.float32
    )
    rank = jnp.sum(hits[0] * ranks, axis=0, keepdims=True).astype(jnp.int32)
    line = lax.broadcasted_iota(jnp.int32, (LANES, listed), 0)
    rest = jnp.where(line < 64, cell_ref[...].astype(jnp.float32) + 1.0, value_ref[...])
    rest = jnp.where((line & 63) == rank, rest, 0.0)
    hits = jnp.concatenate(hits, axis=0).astype(jnp.bfloat16)
    table = jnp.zeros((3 * strips, LANES), jnp.float32)
    for _ in range(3):
        part = rest.astype(jnp.bfloat16)
        table = table + lax.dot_general(hits, part, (((1,), (1,)), ((), ())), preferred_element_type=jnp.float32)
        rest = rest - part.astype(jnp.float32)
    lane = lax.broadcasted_iota(jnp.int32, (strips, LANES), 1)
    table = [table[i * strips : (i + 1) * strips, :] - jnp.where(lane < 64, 1.0, 0.0) for i in range(3)]
    part = lane & 63
    out_ref[...] = jnp.where(
        part < 8, table[0], jnp.where(part < 16, pltpu.roll(table[1], 8, 1), pltpu.roll(table[2], 16, 1))
    )


def sum_kernel(x_ref, out_ref):
    count, lines = x_ref.shape[0], x_ref.shape[1]
    for k in range(lines // ROWS):
        acc = x_ref[0, ROWS * k : ROWS * (k + 1), :]
        for e in range(1, count):
            acc = acc + x_ref[e, ROWS * k : ROWS * (k + 1), :]
        out_ref[:, LANES * k : LANES * (k + 1)] = acc


def call(body, ins, outs, scratch, name):
    count, given = len(ins), len(outs)
    taken = [pair[2] if len(pair) > 2 else pair[0].shape[0] for pair in ins]
    pieces = [pair[3] if len(pair) > 3 else 1 for pair in ins]
    ins = [pair[:2] for pair in ins]
    shares = [pair[2] if len(pair) > 2 else 1 for pair in outs]
    outs = [pair[:2] for pair in outs]
    moved = [i for i, (_, lead) in enumerate(ins) if lead is not HERE]
    copied = [i for i, (shape, kept) in enumerate(outs) if not kept]

    def kernel(*refs):
        sources, results, rest = refs[:count], refs[count : count + given], refs[count + given :]
        landed, left, own = rest[: len(moved)], rest[len(moved) : len(moved) + len(copied)], rest[len(moved) + len(copied) : -2]
        into, out_of = rest[-2:]
        operands, arrivals = list(sources), {}
        for j, i in enumerate(moved):
            operands[i] = landed[j]
            size = taken[i] // pieces[i]
            for part in range(pieces[i]):
                place = ins[i][1] + part * size
                target, source = landed[j], sources[i]
                if size < target.shape[0]:
                    target = target.at[pl.ds(place, size)]
                if size < source.shape[0]:
                    source = source.at[pl.ds(part * size, size)]
                arrivals[part, i] = pltpu.make_async_copy(source, target, into.at[len(arrivals)])
        for key in sorted(arrivals):
            arrivals[key].start()
        places, departures = list(results), {}
        for j, i in enumerate(copied):
            size = outs[i][0][0] // shares[i]
            for part in range(shares[i]):
                target, source = results[i], left[j]
                if shares[i] > 1:
                    target, source = target.at[pl.ds(part * size, size)], source.at[pl.ds(part * size, size)]
                departures[part, i] = pltpu.make_async_copy(source, target, out_of.at[len(departures)])
            places[i] = left[j]

        def arrive(*which):
            for i in which:
                for part in range(pieces[i]) if isinstance(i, int) else ():
                    if (part, i) in arrivals:
                        arrivals[part, i].wait()
                if not isinstance(i, int):
                    arrivals[i].wait()

        def leave(*which):
            for i in which:
                for key in [(0, i)] if isinstance(i, int) else [i]:
                    if key in departures:
                        departures[key].start()

        body(*operands, *places, *own, arrive=arrive, leave=leave)
        for departure in departures.values():
            departure.wait()

    return pl.pallas_call(
        kernel,
        out_shape=[(jax.ShapeDtypeStruct if kept else pltpu.HBM)(shape, jnp.float32) for shape, kept in outs],
        in_specs=[pl.BlockSpec(memory_space=pltpu.VMEM if lead is HERE else pltpu.HBM) for _, lead in ins],
        out_specs=[pl.BlockSpec(memory_space=pltpu.VMEM if kept else pltpu.HBM) for _, kept in outs],
        scratch_shapes=[
            pltpu.VMEM((taken[i] + 2 * ins[i][1], ins[i][0].shape[1]), ins[i][0].dtype) for i in moved
        ]
        + [pltpu.VMEM(outs[i][0], jnp.float32) for i in copied]
        + [pltpu.VMEM(shape, jnp.float32) for shape in scratch]
        + [pltpu.SemaphoreType.DMA((sum(pieces[i] for i in moved),)), pltpu.SemaphoreType.DMA((max(1, sum(shares[i] for i in copied)),))],
        name=name,
        compiler_params=pltpu.CompilerParams(vmem_limit_bytes=GRANT),
    )(*(x if lead is HERE else pltpu.with_memory_space_constraint(x, pltpu.HBM) for x, lead in ins))


def tiled(field):
    rows, cols = field.shape[-2:]
    lead = field.shape[:-2]
    parts = field.reshape(-1, rows, cols // LANES, LANES)
    return jnp.transpose(parts, (0, 2, 1, 3)).reshape(-1, LANES)


def shifted(value, axis, steps):
    count = lax.axis_size(axis)
    initial, last = max(0, -steps), min(count, count - steps)
    return lax.ppermute(value, axis, [(i, i + steps) for i in range(initial, last)])


def per_device(s0, u0, v0, depth, rough, wet, gauge_tiles, gauge_cells, gauge_values, survey):
    row_count, col_count = depth.shape
    assert row_count == ROWS and col_count == 8192
    total = row_count * col_count // LANES
    tiles = col_count // LANES
    strips = lax.axis_size("tile")
    events = lax.axis_size("event")
    s0, u0, v0, depth, rough, wet, survey = (tiled(f) for f in (s0[0], u0[0], v0[0], depth, rough, wet[0], survey[0]))
    field, padded, dense = (total, LANES), (total + 2 * ROWS, LANES), (tiles + 2 * ROWS, LANES)
    packet = (len(SENT) * tiles, LANES)
    listed = (1, gauge_cells.shape[1])
    lists = [(x.reshape(listed), 0) for x in (gauge_tiles, gauge_cells, gauge_values)]
    down, up, send, edges, u1, v1i, t0 = call(
        prepare_kernel,
        lists + [(s0, ROWS)] + [(x, 0, total, 2) for x in (depth, rough, u0, v0)] + [(wet, 0, 2 * total, 4), (survey, 0)],
        [(packet, True), (packet, True), ((strips, LANES), False), ((2 * EDGES * tiles, LANES), False)]
        + [(field, False, 2)] * 3,
        [field] + [padded] * 5 + [field] * 6,
        "prepare",
    )
    from_above = shifted(down, "tile", 1)
    from_below = shifted(up, "tile", -1)
    gauges = lax.all_to_all(send, "tile", 0, 0, axis_index_groups=[turned_order(strips, STRIP_LEAD, STRIP_STRIDE)], tiled=True)
    v1, s2, u2, v2, y, yh, t2, kk, passed = call(
        forward_kernel,
        [(edges, 0), (from_above, HERE), (from_below, HERE)] + [(x, 0) for x in (v1i, s0, wet)] + [(u1, ROWS), (depth, 0), (rough, 0)],
        [(field, True)] * 6 + [(field, False)] * 2 + [((2 * len(PASS) * tiles, LANES), True)],
        [padded] * 4 + [field] * 3 + [dense] * 6,
        "forward",
    )
    order = turned_order(events, EVENT_LEAD * events // 8)
    (grad,) = call(
        functools.partial(backward_kernel, shift=order[0] * (tiles // events)),
        [(gauges, HERE), (s2, HERE), (survey, 0), (y, HERE), (passed, HERE), (u2, HERE), (v2, HERE), (kk, 0)]
        + [(wet, 0, total), (yh, HERE), (u1, 0), (v1, HERE), (t2, 0), (t0, 0)],
        [(field, True)],
        [padded, field, padded, padded, field, padded, field, field, field, field, field, field]
        + [(6 * tiles, LANES)] * 2 + [dense] * 4,
        "backward",
    )
    parts = lax.all_to_all(grad.reshape(events, total // events, LANES), "event", 0, 0, axis_index_groups=[order], tiled=True)
    return pl.pallas_call(
        sum_kernel, out_shape=jax.ShapeDtypeStruct((ROWS, col_count // events), jnp.float32), name="total",
        compiler_params=pltpu.CompilerParams(vmem_limit_bytes=GRANT),
    )(parts)


def solution(mesh):
    placed = (
        P("event", "tile", None),
        P("event", "tile", None),
        P("event", "tile", None),
        P("tile", None),
        P("tile", None),
        P("event", None, "tile", None),
        P("event", "tile", None),
        P("event", "tile"),
        P("event", "tile"),
        P("event", "tile", None),
    )
    return jax.shard_map(
        per_device, mesh=mesh, in_specs=placed, out_specs=P("tile", "event"), check_vma=False
    )
```

```python
import functools
import jax
import jax.numpy as jnp
from jax import lax
from jax.experimental import pallas as pl
from jax.experimental.pallas import tpu as pltpu
from jax.sharding import PartitionSpec as P

LANES = 128
ROWS = 8
STEP = 4
GRANT = 16 * 1024 * 1024
HERE = None
STRIP_LEAD = 44
STRIP_STRIDE = 1
EVENT_LEAD = 4
RIM1 = ("s0", "v1", "b", "s1", "r", "u1", "k", "sv")
RIM2 = ("s1", "w0", "v2", "h", "s2", "sv")
RIM3 = ("h", "s2", "sv")
SENT = tuple((1, x) for x in RIM1) + tuple((2, x) for x in RIM2) + tuple((3, x) for x in RIM3)
SLOT = {key: i for i, key in enumerate(SENT)}
PASS = ("s2_1", "s2_2", "s2_3", "y1", "w0", "h2", "h3", "sv1", "sv2", "sv3")
EDGES = 3


def masks(rows):
    lane = lax.broadcasted_iota(jnp.int32, (rows, LANES), 1)
    sub = lax.broadcasted_iota(jnp.int32, (rows, LANES), 0) & (ROWS - 1)
    return lane, sub


def across(ref, c, n, lane, lead=ROWS):
    x = ref[lead + ROWS * c : lead + ROWS * (c + n), :]
    left = ref[ROWS * c : ROWS * (c + n), :]
    right = ref[2 * lead + ROWS * c : 2 * lead + ROWS * (c + n), :]
    ahead = pltpu.roll(jnp.where(lane == 0, right, x), LANES - 1, 1)
    behind = pltpu.roll(jnp.where(lane == LANES - 1, left, x), 1, 1)
    return ahead - behind


def along(ref, rim, c, n, sub):
    down = ref[ROWS + 1 + ROWS * c : ROWS + 1 + ROWS * (c + n), :]
    up = ref[ROWS - 1 + ROWS * c : ROWS - 1 + ROWS * (c + n), :]
    edge = 0.0 if rim is None else rim[ROWS * c : ROWS * (c + n), :]
    return jnp.where(sub == ROWS - 1, edge, down) - jnp.where(sub == 0, edge, up)


def across_dense(x, scr, lane):
    tiles = x.shape[0]
    scr[ROWS : ROWS + tiles, :] = x
    right = scr[ROWS + 1 : ROWS + 1 + tiles, :]
    left = scr[ROWS - 1 : ROWS - 1 + tiles, :]
    ahead = pltpu.roll(jnp.where(lane == 0, right, x), LANES - 1, 1)
    behind = pltpu.roll(jnp.where(lane == LANES - 1, left, x), 1, 1)
    return ahead - behind


def clear_ends(*refs):
    zero = jnp.zeros((ROWS, LANES), jnp.float32)
    for ref in refs:
        ref[0:ROWS, :] = zero
        ref[ref.shape[0] - ROWS :, :] = zero


def row_of(ref, row, tiles, lead=0):
    return ref[pl.ds(lead + row, tiles, stride=ROWS), :]


def prepare_kernel(
    tile_ref, cell_ref, value_ref, s0p, h_ref, rough_ref, u0_ref, v0_ref, wet_ref, sv_ref,
    down_ref, up_ref, send_ref, edge_ref, u1_ref, v1_ref, t0_ref,
    k_ref, u1p, v1p, s1p, u2p, v2p, hh, s2p, b_ref, w0q, w1_ref, rr, *, arrive, leave,
):
    total = u1_ref.shape[0]
    tiles = total // ROWS
    lane, sub = masks(ROWS * STEP)
    clear_ends(s0p, u1p, v1p, s1p, u2p, v2p)
    arrive(0, 1, 2)
    gauge_table(tile_ref, cell_ref, value_ref, send_ref)
    leave(2)
    blocks = range(0, tiles, STEP)

    def cut(c, lead=0):
        return slice(lead + ROWS * c, lead + ROWS * (c + STEP))

    arrive(3)
    for c in blocks:
        if c * 2 == tiles:
            leave((0, 4), (0, 5), (0, 6))
        if c * 2 % tiles == 0:
            arrive(*((2 * c // tiles, i) for i in (4, 5, 6, 7, 8)))
        at = cut(c)
        depth, rough, east, north = h_ref[at, :], rough_ref[at, :], u0_ref[at, :], v0_ref[at, :]
        wet = wet_ref[at, :].astype(jnp.float32)
        kr = 4.0 * rough * jnp.exp((-4.0 / 3.0) * jnp.log(depth))
        k = 0.5 * kr * rough
        square = east * east + north * north + 1.0
        speed = square * lax.rsqrt(square)
        inverse = 1.0 / (1.0 + k * speed)
        y = wet * inverse
        b = 0.2 * depth * y
        u1 = y * east - b * across(s0p, c, STEP, lane)
        v1 = y * north - b * along(s0p, None, c, STEP, sub)
        u1p[cut(c, ROWS), :] = u1
        v1p[cut(c, ROWS), :] = v1
        u1_ref[at, :] = u1
        v1_ref[at, :] = v1
        b_ref[at, :] = b
        k_ref[at, :] = k
        t0_ref[at, :] = kr * speed * inverse
        w0q[at, :] = 0.25 * wet
    for i, (ref, lead) in enumerate(((s0p, ROWS), (v1_ref, 0), (b_ref, 0))):
        for j, row in enumerate((0, ROWS - 1)):
            first = (j * EDGES + i) * tiles
            edge_ref[first : first + tiles, :] = row_of(ref, row, tiles, lead)
    leave((1, 4), (1, 5), (1, 6), 3)
    for c in blocks:
        at = cut(c)
        quarter = w0q[at, :]
        q1 = s0p[cut(c, ROWS), :] - quarter * across(u1p, c, STEP, lane)
        s1p[cut(c, ROWS), :] = q1 - quarter * along(v1p, None, c, STEP, sub)
    arrive((2, 8), (3, 8))
    for c in blocks:
        at = cut(c)
        wet = wet_ref[cut(c, total), :].astype(jnp.float32)
        east, north = u1_ref[at, :], v1_ref[at, :]
        depth = 0.2 * h_ref[at, :]
        square = east * east + north * north + 1.0
        y = wet / (1.0 + k_ref[at, :] * (square * lax.rsqrt(square)))
        h = depth * y
        hh[at, :] = h
        rr[at, :] = depth * wet
        w1_ref[at, :] = wet
        u2p[cut(c, ROWS), :] = y * east - h * across(s1p, c, STEP, lane)
        v2 = y * north - h * along(s1p, None, c, STEP, sub)
        v2p[cut(c, ROWS), :] = jnp.where((sub == 0) | (sub == ROWS - 1), 0.0, v2)
    for c in blocks:
        at = cut(c)
        change = across(u2p, c, STEP, lane) + along(v2p, None, c, STEP, sub)
        s2p[at, :] = s1p[cut(c, ROWS), :] - 0.25 * w1_ref[at, :] * change
    held = {
        (1, "s0"): (s0p, ROWS), (1, "v1"): (v1_ref, 0), (1, "b"): (b_ref, 0), (1, "s1"): (s1p, ROWS),
        (1, "r"): (rr, 0), (1, "u1"): (u1_ref, 0), (1, "k"): (k_ref, 0), (1, "sv"): (sv_ref, 0),
        (2, "s1"): (s1p, ROWS), (2, "w0"): (w0q, 0), (2, "v2"): (v2p, ROWS), (2, "h"): (hh, 0),
        (2, "s2"): (s2p, 0), (2, "sv"): (sv_ref, 0), (3, "h"): (hh, 0), (3, "s2"): (s2p, 0), (3, "sv"): (sv_ref, 0),
    }
    arrive(9)
    for key, place in SLOT.items():
        ref, lead = held[key]
        down_ref[place * tiles : (place + 1) * tiles, :] = row_of(ref, ROWS - key[0], tiles, lead)
        up_ref[place * tiles : (place + 1) * tiles, :] = row_of(ref, key[0] - 1, tiles, lead)


def forward_kernel(
    edge_ref, top_ref, bot_ref, v1i_ref, s0_ref, wet_ref, u1p, h_ref, rough_ref,
    v1_ref, s2_ref, u2_ref, v2_ref, y_ref, yh_ref, t2_ref, kk_ref, pass_ref,
    v1p, s1p, u2p, v2p, v1r, s1r, v2r, da, db, dc, dd, de, df, *, arrive, leave,
):
    total = v1i_ref.shape[0]
    tiles = total // ROWS
    lane, sub = masks(ROWS * STEP)
    dlane = lax.broadcasted_iota(jnp.int32, (tiles, LANES), 1)
    clear_ends(u1p, v1p, s1p, u2p, v2p, da, db, dc, dd, de, df)
    blocks = range(0, tiles, STEP)

    def cut(c, lead=0):
        return slice(lead + ROWS * c, lead + ROWS * (c + STEP))

    sides = ((top_ref, -1.0, 0, (da, db, dc)), (bot_ref, 1.0, ROWS - 1, (dd, de, df)))

    def got(ref, n, name):
        place = SLOT[(n, name)]
        return ref[place * tiles : (place + 1) * tiles, :]

    def own(edge, i):
        first = (EDGES * (edge > 0) + i) * tiles
        return edge_ref[first : first + tiles, :]

    arrive(0, 3)
    v1p[ROWS : ROWS + total, :] = v1i_ref[...]
    kept = []
    for ref, sigma, edge, scr in sides:
        b = got(ref, 1, "b")
        delta = b * own(edge, 0)
        v1_1 = got(ref, 1, "v1") + sigma * delta
        v1_e = own(edge, 1) - sigma * own(edge, 2) * got(ref, 1, "s0")
        v1p[pl.ds(ROWS + edge, tiles, stride=ROWS), :] = v1_e
        v1r[pl.ds(edge, tiles, stride=ROWS), :] = v1_1
        bump = got(ref, 2, "w0") * delta
        s1_2 = got(ref, 2, "s1") + bump
        w0_1 = jnp.where(b > 0.0, 1.0, 0.0)
        s1_1 = got(ref, 1, "s1") + (0.25 * sigma) * w0_1 * v1_e
        s1r[pl.ds(edge, tiles, stride=ROWS), :] = s1_1
        r, u1_1, h2, h3 = got(ref, 1, "r"), got(ref, 1, "u1"), got(ref, 2, "h"), got(ref, 3, "h")
        w1_1 = jnp.where(r > 0.0, 1.0, 0.0)
        inverse = 1.0 / (1.0 + got(ref, 1, "k") * jnp.sqrt(u1_1 * u1_1 + v1_1 * v1_1 + 1.0))
        v2i_2 = got(ref, 2, "v2")
        v2_2 = v2i_2 + 0.25 * w0_1 * h2 * v1_e
        v2_3 = sigma * h3 * bump
        u2_2 = -h2 * across_dense(bump, scr[0], dlane)
        s2_3 = got(ref, 3, "s2") + (0.25 * sigma) * jnp.where(h3 > 0.0, 1.0, 0.0) * (v2_2 - v2i_2)
        u2_1 = (w1_1 * u1_1 - r * across_dense(s1_1, scr[1], dlane)) * inverse
        kept.append((v1_1, s1_1, s1_2, w0_1, w1_1, r, inverse, h2, v2_2, v2_3, u2_1, u2_2, s2_3, bump))
    arrive(4, 5, 6)
    for c in blocks:
        at = cut(c)
        quarter = 0.25 * wet_ref[at, :].astype(jnp.float32)
        v1_ref[at, :] = v1p[cut(c, ROWS), :]
        change = across(u1p, c, STEP, lane) + along(v1p, v1r, c, STEP, sub)
        s1p[cut(c, ROWS), :] = s0_ref[at, :] - quarter * change
    leave(0)
    arrive(7, 8)
    late = []
    for (ref, sigma, edge, scr), values in zip(sides, kept):
        v1_1, s1_1, s1_2, w0_1, w1_1, r, inverse, h2, v2_2, v2_3, u2_1, u2_2, s2_3, bump = values
        s1_e = row_of(s1p, edge, tiles, ROWS)
        v2_1 = (w1_1 * v1_1 - sigma * r * (s1_2 - s1_e)) * inverse
        v2r[pl.ds(edge, tiles, stride=ROWS), :] = v2_1
        w1_2 = jnp.where(h2 > 0.0, 0.25, 0.0)
        s2_2 = got(ref, 2, "s2") + bump - w1_2 * (across_dense(u2_2, scr[2], dlane) + sigma * (v2_3 - v2_1))
        late.append((s2_2, across_dense(u2_1, scr[0], dlane)))
    for c in blocks:
        at = cut(c)
        east, north = u1p[cut(c, ROWS), :], v1_ref[at, :]
        speed2 = east * east + north * north + 1.0
        slow = lax.rsqrt(speed2)
        speed = speed2 * slow
        depth, rough = h_ref[at, :], rough_ref[at, :]
        kr = 4.0 * rough * jnp.exp((-4.0 / 3.0) * jnp.log(depth))
        k = 0.5 * kr * rough
        inverse = 1.0 / (1.0 + k * speed)
        y = wet_ref[cut(c, total), :].astype(jnp.float32) * inverse
        yh = 0.2 * depth * y
        u2 = y * east - yh * across(s1p, c, STEP, lane)
        v2 = y * north - yh * along(s1p, s1r, c, STEP, sub)
        u2p[cut(c, ROWS), :] = u2
        v2p[cut(c, ROWS), :] = v2
        u2_ref[at, :] = u2
        v2_ref[at, :] = v2
        y_ref[at, :] = y
        yh_ref[at, :] = yh
        t2_ref[at, :] = kr * speed * inverse
        kk_ref[at, :] = k * inverse * slow
    leave(2, 3, 4, 5, 6, 7)
    for c in blocks:
        at = cut(c)
        wet = wet_ref[cut(c, total), :].astype(jnp.float32)
        change = across(u2p, c, STEP, lane) + along(v2p, v2r, c, STEP, sub)
        s2_ref[at, :] = s1p[cut(c, ROWS), :] - 0.25 * wet * change
    leave(1)
    for d, ((ref, sigma, edge, scr), values, more) in enumerate(zip(sides, kept, late)):
        v1_1, s1_1, s1_2, w0_1, w1_1, r, inverse, h2, v2_2, v2_3, u2_1, u2_2, s2_3, bump = values
        s2_2, du2_1 = more
        v2_e = row_of(v2p, edge, tiles, ROWS)
        s2_1 = s1_1 - 0.25 * w1_1 * (du2_1 + sigma * (v2_2 - v2_e))
        surveyed = [got(ref, n, "sv") for n in (1, 2, 3)]
        for i, value in enumerate((s2_1, s2_2, s2_3, r * inverse, w0_1, h2, got(ref, 3, "h"), *surveyed)):
            first = (d * len(PASS) + i) * tiles
            pass_ref[first : first + tiles, :] = value
    leave(8)


def gauge_fields(places, lanes, values, rows):
    grid = lax.broadcasted_iota(jnp.int32, (rows, LANES), 0)
    lane = lax.broadcasted_iota(jnp.int32, (LANES, LANES), 0)
    left, right = [], []
    for place, at, value in zip(places, lanes, values):
        left.append(jnp.where(grid == place, 1.0, 0.0).astype(jnp.bfloat16))
        hit = lane == at
        high = value.astype(jnp.bfloat16).astype(jnp.float32)
        rest = value - high
        middle = rest.astype(jnp.bfloat16).astype(jnp.float32)
        low = rest - middle
        parts = [jnp.where(hit, part, 0.0).astype(jnp.bfloat16) for part in (high, middle, low)]
        parts.append(jnp.where(hit, 1.0, 0.0).astype(jnp.bfloat16))
        right.append(jnp.concatenate(parts, axis=0))
    out = lax.dot_general(
        jnp.concatenate(left, axis=1), jnp.concatenate(right, axis=1), (((1,), (1,)), ((), ())),
        preferred_element_type=jnp.float32,
    )
    summed = out[:, :LANES] + out[:, LANES : 2 * LANES] + out[:, 2 * LANES : 3 * LANES]
    return summed, out[:, 3 * LANES :]


def backward_kernel(
    gauge_ref, s2_ref, sv_ref, y_ref, pass_ref, u2_ref, v2_ref, kk_ref, wet_ref, yh_ref, u1_ref, v1_ref, t2_ref, t0_ref,
    grad_ref,
    x2p, x2r, pup, pvp, pvr, x1p, x1r, b2s, au1, av1, vs, ms, vt, mt, da, db, dc, dd, *, arrive, leave, shift,
):
    total = s2_ref.shape[0]
    tiles = total // ROWS
    lane, sub = masks(ROWS * STEP)
    dlane = lax.broadcasted_iota(jnp.int32, (tiles, LANES), 1)
    clear_ends(x2p, pup, pvp, x1p, da, db, dc, dd)
    blocks = range(0, tiles, STEP)

    def cut(c, lead=0):
        return slice(lead + ROWS * c, lead + ROWS * (c + STEP))

    x = gauge_ref[...]
    turned = jnp.concatenate([x, pltpu.roll(x, LANES - 4, 1)], axis=0)
    if turned.shape[0] < LANES:
        fill = jnp.full((LANES - turned.shape[0], LANES), -1.0, jnp.float32)
        turned = jnp.concatenate([turned, fill], axis=0)
    turned = jnp.transpose(turned)
    for group in range(3):
        places, lanes, values = [], [], []
        for k in range(4):
            cell = turned[8 * group + k : 8 * group + k + 1, :].astype(jnp.int32)
            value = turned[64 + 8 * group + k : 65 + 8 * group + k, :]
            row, col = cell >> 13, cell & 8191
            tile = col >> 7
            if group == 0:
                place = jnp.where(cell < 0, -1, tile * ROWS + row)
            elif group == 1:
                place = jnp.where((cell < 0) | (row < 5), -1, (7 - row) * tiles + tile)
            else:
                place = jnp.where((cell < 0) | (row > 2), -1, row * tiles + tile)
            places.append(place)
            lanes.append(col & 127)
            values.append(value)
        if group == 0:
            vs[...], ms[...] = gauge_fields(places, lanes, values, total)
        else:
            first = (group - 1) * 3 * tiles
            sums, counts = gauge_fields(places, lanes, values, 3 * tiles)
            vt[first : first + 3 * tiles, :] = sums
            mt[first : first + 3 * tiles, :] = counts
    arrive(1, 2, 3, 4)
    sides = ((-1.0, 0, (da, db)), (1.0, ROWS - 1, (dc, dd)))
    kept = []
    for d, (sigma, edge, scr) in enumerate(sides):
        got = {}
        for i, name in enumerate(PASS):
            first = (d * len(PASS) + i) * tiles
            got[name] = pass_ref[first : first + tiles, :]
        senses = []
        for n in (1, 2, 3):
            first = (d * 3 + n - 1) * tiles
            count, summed = mt[first : first + tiles, :], vt[first : first + tiles, :]
            senses.append((1.0 + count) * got[f"s2_{n}"] - got[f"sv{n}"] - summed)
        y1, h2 = got["y1"], got["h2"]
        x2_1 = jnp.where(y1 > 0.0, senses[0], 0.0)
        x2_2 = jnp.where(h2 > 0.0, senses[1], 0.0)
        x2_3 = jnp.where(got["h3"] > 0.0, senses[2], 0.0)
        x2r[pl.ds(edge, tiles, stride=ROWS), :] = x2_1
        pu_1 = 0.25 * y1 * across_dense(x2_1, scr[0], dlane)
        pv_2 = (0.25 * sigma) * h2 * (x2_3 - x2_1)
        kept.append((senses[0] + across_dense(pu_1, scr[1], dlane) + sigma * pv_2, x2_2, y1, got["w0"]))
    for c in blocks:
        at = cut(c)
        b2 = (1.0 + ms[at, :]) * s2_ref[at, :] - sv_ref[at, :] - vs[at, :]
        b2s[at, :] = b2
        x2p[cut(c, ROWS), :] = jnp.where(y_ref[at, :] > 0.0, b2, 0.0)
    arrive(5, 6, 7, 8, 9, 10, 11, 12)
    for (sigma, edge, scr), (part, x2_2, y1, w0_1) in zip(sides, kept):
        pvr[pl.ds(edge, tiles, stride=ROWS), :] = (0.25 * sigma) * y1 * (x2_2 - row_of(x2p, edge, tiles, ROWS))
    for c in blocks:
        at = cut(c)
        a_u2 = 0.25 * across(x2p, c, STEP, lane)
        a_v2 = 0.25 * along(x2p, x2r, c, STEP, sub)
        energy = a_u2 * u2_ref[at, :] + a_v2 * v2_ref[at, :]
        y, yh, pull = y_ref[at, :], yh_ref[at, :], energy * kk_ref[at, :]
        pup[cut(c, ROWS), :] = yh * a_u2
        pvp[cut(c, ROWS), :] = yh * a_v2
        au1[at, :] = y * a_u2 - pull * u1_ref[at, :]
        av1[at, :] = y * a_v2 - pull * v1_ref[at, :]
        vs[at, :] = energy * t2_ref[at, :]
    for (sigma, edge, scr), (part, x2_2, y1, w0_1) in zip(sides, kept):
        x1r[pl.ds(edge, tiles, stride=ROWS), :] = w0_1 * (part - sigma * row_of(pvp, edge, tiles, ROWS))
    for c in blocks:
        at = cut(c)
        a_s1 = b2s[at, :] + across(pup, c, STEP, lane) + along(pvp, pvr, c, STEP, sub)
        x1p[cut(c, ROWS), :] = wet_ref[at, :].astype(jnp.float32) * a_s1
    arrive(13)
    for c in blocks:
        at = cut(c)
        a_u1 = au1[at, :] + 0.25 * across(x1p, c, STEP, lane)
        a_v1 = av1[at, :] + 0.25 * along(x1p, x1r, c, STEP, sub)
        energy = a_u1 * u1_ref[at, :] + a_v1 * v1_ref[at, :]
        grad_ref[cut((c - shift) % tiles), :] = -(energy * t0_ref[at, :] + vs[at, :])


def turned_order(count, first, stride=1):
    return [(i * stride + first) % count for i in range(count)]


def gauge_table(tile_ref, cell_ref, value_ref, out_ref):
    strips = out_ref.shape[0]
    listed = tile_ref.shape[1]
    strip = (lax.broadcasted_iota(jnp.int32, (strips, listed), 0) * STRIP_STRIDE + STRIP_LEAD) % strips
    tile = tile_ref[...]
    hits = [jnp.where(strip + side == tile, 1.0, 0.0) for side in (0, -1, 1)]
    earlier = lax.broadcasted_iota(jnp.int32, (listed, listed), 0) < lax.broadcasted_iota(jnp.int32, (listed, listed), 1)
    ranks = jnp.dot(
        hits[0].astype(jnp.bfloat16), jnp.where(earlier, 1.0, 0.0).astype(jnp.bfloat16), preferred_element_type=jnp.float32
    )
    rank = jnp.sum(hits[0] * ranks, axis=0, keepdims=True).astype(jnp.int32)
    line = lax.broadcasted_iota(jnp.int32, (LANES, listed), 0)
    rest = jnp.where(line < 64, cell_ref[...].astype(jnp.float32) + 1.0, value_ref[...])
    rest = jnp.where((line & 63) == rank, rest, 0.0)
    hits = jnp.concatenate(hits, axis=0).astype(jnp.bfloat16)
    table = jnp.zeros((3 * strips, LANES), jnp.float32)
    for _ in range(3):
        part = rest.astype(jnp.bfloat16)
        table = table + lax.dot_general(hits, part, (((1,), (1,)), ((), ())), preferred_element_type=jnp.float32)
        rest = rest - part.astype(jnp.float32)
    lane = lax.broadcasted_iota(jnp.int32, (strips, LANES), 1)
    table = [table[i * strips : (i + 1) * strips, :] - jnp.where(lane < 64, 1.0, 0.0) for i in range(3)]
    part = lane & 63
    out_ref[...] = jnp.where(
        part < 8, table[0], jnp.where(part < 16, pltpu.roll(table[1], 8, 1), pltpu.roll(table[2], 16, 1))
    )


def sum_kernel(x_ref, out_ref):
    count, lines = x_ref.shape[0], x_ref.shape[1]
    for k in range(lines // ROWS):
        acc = x_ref[0, ROWS * k : ROWS * (k + 1), :]
        for e in range(1, count):
            acc = acc + x_ref[e, ROWS * k : ROWS * (k + 1), :]
        out_ref[:, LANES * k : LANES * (k + 1)] = acc


def call(body, ins, outs, scratch, name):
    count, given = len(ins), len(outs)
    taken = [pair[2] if len(pair) > 2 else pair[0].shape[0] for pair in ins]
    pieces = [pair[3] if len(pair) > 3 else 1 for pair in ins]
    ins = [pair[:2] for pair in ins]
    shares = [pair[2] if len(pair) > 2 else 1 for pair in outs]
    outs = [pair[:2] for pair in outs]
    moved = [i for i, (_, lead) in enumerate(ins) if lead is not HERE]
    copied = [i for i, (shape, kept) in enumerate(outs) if not kept]

    def kernel(*refs):
        sources, results, rest = refs[:count], refs[count : count + given], refs[count + given :]
        landed, left, own = rest[: len(moved)], rest[len(moved) : len(moved) + len(copied)], rest[len(moved) + len(copied) : -2]
        into, out_of = rest[-2:]
        operands, arrivals = list(sources), {}
        for j, i in enumerate(moved):
            operands[i] = landed[j]
            size = taken[i] // pieces[i]
            for part in range(pieces[i]):
                place = ins[i][1] + part * size
                target, source = landed[j], sources[i]
                if size < target.shape[0]:
                    target = target.at[pl.ds(place, size)]
                if size < source.shape[0]:
                    source = source.at[pl.ds(part * size, size)]
                arrivals[part, i] = pltpu.make_async_copy(source, target, into.at[len(arrivals)])
        for key in sorted(arrivals):
            arrivals[key].start()
        places, departures = list(results), {}
        for j, i in enumerate(copied):
            size = outs[i][0][0] // shares[i]
            for part in range(shares[i]):
                target, source = results[i], left[j]
                if shares[i] > 1:
                    target, source = target.at[pl.ds(part * size, size)], source.at[pl.ds(part * size, size)]
                departures[part, i] = pltpu.make_async_copy(source, target, out_of.at[len(departures)])
            places[i] = left[j]

        def arrive(*which):
            for i in which:
                for part in range(pieces[i]) if isinstance(i, int) else ():
                    if (part, i) in arrivals:
                        arrivals[part, i].wait()
                if not isinstance(i, int):
                    arrivals[i].wait()

        def leave(*which):
            for i in which:
                for key in [(0, i)] if isinstance(i, int) else [i]:
                    if key in departures:
                        departures[key].start()

        body(*operands, *places, *own, arrive=arrive, leave=leave)
        for departure in departures.values():
            departure.wait()

    return pl.pallas_call(
        kernel,
        out_shape=[(jax.ShapeDtypeStruct if kept else pltpu.HBM)(shape, jnp.float32) for shape, kept in outs],
        in_specs=[pl.BlockSpec(memory_space=pltpu.VMEM if lead is HERE else pltpu.HBM) for _, lead in ins],
        out_specs=[pl.BlockSpec(memory_space=pltpu.VMEM if kept else pltpu.HBM) for _, kept in outs],
        scratch_shapes=[
            pltpu.VMEM((taken[i] + 2 * ins[i][1], ins[i][0].shape[1]), ins[i][0].dtype) for i in moved
        ]
        + [pltpu.VMEM(outs[i][0], jnp.float32) for i in copied]
        + [pltpu.VMEM(shape, jnp.float32) for shape in scratch]
        + [pltpu.SemaphoreType.DMA((sum(pieces[i] for i in moved),)), pltpu.SemaphoreType.DMA((max(1, sum(shares[i] for i in copied)),))],
        name=name,
        compiler_params=pltpu.CompilerParams(vmem_limit_bytes=GRANT),
    )(*(x if lead is HERE else pltpu.with_memory_space_constraint(x, pltpu.HBM) for x, lead in ins))


def tiled(field):
    rows, cols = field.shape[-2:]
    lead = field.shape[:-2]
    parts = field.reshape(-1, rows, cols // LANES, LANES)
    return jnp.transpose(parts, (0, 2, 1, 3)).reshape(-1, LANES)


def shifted(value, axis, steps):
    count = lax.axis_size(axis)
    initial, last = max(0, -steps), min(count, count - steps)
    return lax.ppermute(value, axis, [(i, i + steps) for i in range(initial, last)])


def per_device(s0, u0, v0, depth, rough, wet, gauge_tiles, gauge_cells, gauge_values, survey):
    row_count, col_count = depth.shape
    assert row_count == ROWS and col_count == 8192
    total = row_count * col_count // LANES
    tiles = col_count // LANES
    strips = lax.axis_size("tile")
    events = lax.axis_size("event")
    s0, u0, v0, depth, rough, wet, survey = (tiled(f) for f in (s0[0], u0[0], v0[0], depth, rough, wet[0], survey[0]))
    field, padded, dense = (total, LANES), (total + 2 * ROWS, LANES), (tiles + 2 * ROWS, LANES)
    packet = (len(SENT) * tiles, LANES)
    listed = (1, gauge_cells.shape[1])
    lists = [(x.reshape(listed), 0) for x in (gauge_tiles, gauge_cells, gauge_values)]
    down, up, send, edges, u1, v1i, t0 = call(
        prepare_kernel,
        lists + [(s0, ROWS)] + [(x, 0, total, 2) for x in (depth, rough, u0, v0)] + [(wet, 0, 2 * total, 4), (survey, 0)],
        [(packet, True), (packet, True), ((strips, LANES), False), ((2 * EDGES * tiles, LANES), False)]
        + [(field, False, 2)] * 3,
        [field] + [padded] * 5 + [field] * 6,
        "prepare",
    )
    from_above = shifted(down, "tile", 1)
    from_below = shifted(up, "tile", -1)
    gauges = lax.all_to_all(send, "tile", 0, 0, axis_index_groups=[turned_order(strips, STRIP_LEAD, STRIP_STRIDE)], tiled=True)
    v1, s2, u2, v2, y, yh, t2, kk, passed = call(
        forward_kernel,
        [(edges, 0), (from_above, HERE), (from_below, HERE)] + [(x, 0) for x in (v1i, s0, wet)] + [(u1, ROWS), (depth, 0), (rough, 0)],
        [(field, True)] * 6 + [(field, False)] * 2 + [((2 * len(PASS) * tiles, LANES), True)],
        [padded] * 4 + [field] * 3 + [dense] * 6,
        "forward",
    )
    order = turned_order(events, EVENT_LEAD * events // 8)
    (grad,) = call(
        functools.partial(backward_kernel, shift=order[0] * (tiles // events)),
        [(gauges, HERE), (s2, HERE), (survey, 0), (y, HERE), (passed, HERE), (u2, HERE), (v2, HERE), (kk, 0)]
        + [(wet, 0, total), (yh, HERE), (u1, 0), (v1, HERE), (t2, 0), (t0, 0)],
        [(field, True)],
        [padded, field, padded, padded, field, padded, field, field, field, field, field, field]
        + [(6 * tiles, LANES)] * 2 + [dense] * 4,
        "backward",
    )
    parts = lax.all_to_all(grad.reshape(events, total // events, LANES), "event", 0, 0, axis_index_groups=[order], tiled=True)
    return pl.pallas_call(
        sum_kernel, out_shape=jax.ShapeDtypeStruct((ROWS, col_count // events), jnp.float32), name="total",
        compiler_params=pltpu.CompilerParams(vmem_limit_bytes=GRANT),
    )(parts)


def solution(mesh):
    placed = (
        P("event", "tile", None),
        P("event", "tile", None),
        P("event", "tile", None),
        P("tile", None),
        P("tile", None),
        P("event", None, "tile", None),
        P("event", "tile", None),
        P("event", "tile"),
        P("event", "tile"),
        P("event", "tile", None),
    )
    return jax.shard_map(
        per_device, mesh=mesh, in_specs=placed, out_specs=P("tile", "event"), check_vma=False
    )
```
